32 devices in a mesh: dp: 4 (over y, x), sp: 8 (over z, core).
Axes of the slice: x: 2, y: 2, z: 4, core: 2. Of those that a mesh axis runs over, the one named last changes fastest.
Arguments:
- inputs: bfloat16 [4, 2048, 1024], P('dp', 'sp'), may hold values from -6 to 6
- block_order: int32 [16], replicated, may hold values from 0 to 15, as said below
- first_gain: bfloat16 [1024], P(('dp', 'sp')), may hold values from 0.5 to 1.5
- first_shift: bfloat16 [1024], P(('dp', 'sp')), may hold values from -4 to 4
- joint_weight: bfloat16 [1024, 3072], P(('dp', 'sp')), may hold values from -0.1875 to 0.1875
- query_bias: bfloat16 [1024], P(('dp', 'sp')), may hold values from -4 to 4
- value_bias: bfloat16 [1024], P(('dp', 'sp')), may hold values from -0.625 to 0.625
- mixer_weight: bfloat16 [1024, 1024], P(('dp', 'sp')), may hold values from -1 to 1
- mixer_bias: bfloat16 [1024], P(('dp', 'sp')), may hold values from -4 to 4
- second_gain: bfloat16 [1024], P(('dp', 'sp')), may hold values from 0.5 to 1.5
- second_shift: bfloat16 [1024], P(('dp', 'sp')), may hold values from -4 to 4
- expand_weight: bfloat16 [1024, 4096], P(('dp', 'sp')), may hold values from -0.1875 to 0.1875
- expand_bias: bfloat16 [4096], P(('dp', 'sp')), may hold values from -4 to 4
- reduce_weight: bfloat16 [4096, 1024], P(('dp', 'sp')), may hold values from -0.09375 to 0.09375
- reduce_bias: bfloat16 [1024], P(('dp', 'sp')), may hold values from -4 to 4
- cotangent: bfloat16 [4, 2048, 1024], P('dp', 'sp'), may hold values from -6 to 6
Outputs:
- output: bfloat16 [4, 2048, 1024], P('dp', 'sp')
- input_gradient: bfloat16 [4, 2048, 1024], P('dp', 'sp')
- first_gain_gradient: float32 [1024], P(('dp', 'sp'))
- first_shift_gradient: float32 [1024], P(('dp', 'sp'))
- joint_weight_gradient: float32 [1024, 3072], P(('dp', 'sp'))
- query_bias_gradient: float32 [1024], P(('dp', 'sp'))
- value_bias_gradient: float32 [1024], P(('dp', 'sp'))
- mixer_weight_gradient: float32 [1024, 1024], P(('dp', 'sp'))
- mixer_bias_gradient: float32 [1024], P(('dp', 'sp'))
- second_gain_gradient: float32 [1024], P(('dp', 'sp'))
- second_shift_gradient: float32 [1024], P(('dp', 'sp'))
- expand_weight_gradient: float32 [1024, 4096], P(('dp', 'sp'))
- expand_bias_gradient: float32 [4096], P(('dp', 'sp'))
- reduce_weight_gradient: float32 [4096, 1024], P(('dp', 'sp'))
- reduce_bias_gradient: float32 [1024], P(('dp', 'sp'))
The draws below stay inside these ranges and needn't reach their ends.
Inputs may be any that keep to these rules, and one draw needn't show every extreme that they name: `block_order`: every block 0 to 15 appears once; slot 2j holds a block below 8 and slot 2j+1 holds 15 minus it.
All inputs are finite; a program needn't handle non-finite values.
Results may differ from the reference program's by a relative error of at most 0.018.
Values may be sent and summed in bfloat16 or wider, within the bound.
No kernel may reach another device: no remote copies, remote signals or barrier semaphores. Data moves between devices by JAX's collectives and lax.ppermute only.
A program may use at most 192 MiB of HBM per device.

```python
import math
import jax
import jax.numpy as jnp
from jax import lax

D = 1024
H = 16
HD = 64
FF = 4096
BLOCK = 128
LENGTH = 2048
SEQUENCES = 4
N_SP = 8


def draw_block_order(key, part):
    shuffled = jax.random.permutation(key, N_SP).astype(jnp.int32)
    mirrored = (2 * N_SP - 1 - shuffled).astype(jnp.int32)
    return jnp.stack([shuffled, mirrored], axis=1).reshape(2 * N_SP)


def levels(key, shape, shards, low, high):
    factor_of, own = 1.0, jax.random.fold_in(key, 6)
    for axis_at, parts in shards:
        heights = jnp.exp(jax.random.uniform(jax.random.fold_in(own, axis_at), (parts,), jnp.float32, low / len(shards), high / len(shards)))
        factor_of = factor_of * jnp.repeat(heights, shape[axis_at] // parts).reshape([-1 if axis == axis_at else 1 for axis in range(len(shape))])
    return factor_of


def bell_draw(own_key, shape, scale, bound, pieces=(), kind=jnp.bfloat16):
    result = jax.random.normal(own_key, shape, jnp.float32) * scale
    if len(pieces) > 0:
        result = levels(own_key, shape, pieces, -0.22, 0.18) * result
    return jnp.clip(result, min=-bound, max=bound).astype(kind)


def setup_inputs(seed: int = 0) -> dict:
    key_list = jax.random.split(jax.random.key(seed), 17)
    return {
        "inputs": bell_draw(key_list[0], (SEQUENCES, LENGTH, D), 1.0, 6.0, ((0, 4), (1, 8))),
        "block_order": draw_block_order(jax.random.fold_in(key_list[16], 71), 0),
        "first_gain": jnp.clip(1.0 + 0.1 * jax.random.normal(key_list[2], (D,), jnp.float32), 0.5, 1.5).astype(jnp.bfloat16),
        "first_shift": bell_draw(key_list[3], (D,), 0.3, 4.0, ((0, 32),)),
        "joint_weight": bell_draw(key_list[4], (D, 3 * D), D ** -0.5, 0.1875, ((0, 32),)),
        "query_bias": bell_draw(key_list[5], (D,), 0.3, 4.0, ((0, 32),)),
        "value_bias": bell_draw(key_list[6], (D,), 0.04, 0.625, ((0, 32),)),
        "mixer_weight": bell_draw(key_list[7], (D, D), (max(1, D * 64 // LENGTH)) ** -0.5, 1.0, ((0, 32),)),
        "mixer_bias": bell_draw(key_list[8], (D,), 0.3, 4.0, ((0, 32),)),
        "second_gain": jnp.clip(1.0 + 0.1 * jax.random.normal(key_list[9], (D,), jnp.float32), 0.5, 1.5).astype(jnp.bfloat16),
        "second_shift": bell_draw(key_list[10], (D,), 0.3, 4.0, ((0, 32),)),
        "expand_weight": bell_draw(key_list[11], (D, FF), D ** -0.5, 0.1875, ((0, 32),)),
        "expand_bias": bell_draw(key_list[12], (FF,), 0.3, 4.0, ((0, 32),)),
        "reduce_weight": bell_draw(key_list[13], (FF, D), FF ** -0.5, 0.09375, ((0, 32),)),
        "reduce_bias": bell_draw(key_list[14], (D,), 0.3, 4.0, ((0, 32),)),
        "cotangent": bell_draw(key_list[15], (SEQUENCES, LENGTH, D), 1.0, 6.0, ((0, 4), (1, 8))),
    }


EPS = 1e-05
HIGH = lax.Precision.HIGHEST

@jax.custom_vjp
def low(v):
    return lax.optimization_barrier(v.astype(jnp.bfloat16)).astype(jnp.float32)

@jax.custom_vjp
def low_back(v):
    return v

def low_keep(v):
    return (low(v), None)

def low_pass(kept, grad):
    return (grad,)

def back_keep(v):
    return (v, None)

def back_low(kept, grad):
    return (low(grad),)
low.defvjp(low_keep, low_pass)
low_back.defvjp(back_keep, back_low)

def product(left, right):
    return jnp.dot(left, right, precision=HIGH, preferred_element_type=jnp.float32)

def layer_norm(values, scaling, offset):
    average = lax.optimization_barrier(jnp.mean(values, axis=-1, keepdims=True))
    centred = values - average
    spread = lax.optimization_barrier(jnp.mean(centred * centred, axis=-1, keepdims=True))
    return centred * lax.rsqrt(spread + EPS) * scaling + offset

def attend_block(queries, query_places, key_rows, value_rows, key_places):
    scores = low_back(jnp.einsum('qhd,khd->hqk', queries, key_rows, precision=HIGH, preferred_element_type=jnp.float32))
    visible = key_places[None, None, :] <= query_places[None, :, None]
    powers = jnp.where(visible, jnp.exp(scores * HD ** (-0.5)), 0.0)
    totals = lax.optimization_barrier(jnp.sum(powers, axis=-1))
    unnorm = low_back(jnp.einsum('hqk,khd->qhd', low(powers), value_rows, precision=HIGH, preferred_element_type=jnp.float32))
    return unnorm / jnp.transpose(totals)[:, :, None]

def attention(queries, key_rows, value_rows, places):
    length_rows = queries.shape[0]
    block_rows = math.gcd(512, length_rows)
    grouped = queries.reshape(length_rows // block_rows, block_rows, H, HD)
    grouped_places = places.reshape(length_rows // block_rows, block_rows)
    checked = jax.checkpoint(attend_block)

    def one_block(pair_in):
        return checked(pair_in[0], pair_in[1], key_rows, value_rows, places)
    return lax.map(one_block, (grouped, grouped_places)).reshape(length_rows, H, HD)

def block_forward(sequence_rows, places, first_gain, first_shift, joint_weight, query_bias, value_bias, mixer_weight, mixer_bias, second_gain, second_shift, expand_weight, expand_bias, reduce_weight, reduce_bias):
    row_count = sequence_rows.shape[0]
    normed = low(layer_norm(sequence_rows, first_gain, first_shift))
    joint_shift = jnp.concatenate([query_bias, jnp.zeros_like(query_bias), value_bias])
    joint_rows = low(low_back(product(normed, joint_weight) + joint_shift))
    queries = joint_rows[:, :D].reshape(row_count, H, HD)
    key_rows = joint_rows[:, D:2 * D].reshape(row_count, H, HD)
    value_rows = joint_rows[:, 2 * D:].reshape(row_count, H, HD)
    mixed_rows = attention(queries, key_rows, value_rows, places).reshape(row_count, D)
    mixed_rows = low(low_back(mixed_rows))
    middle = sequence_rows + low_back(product(mixed_rows, mixer_weight) + mixer_bias)
    second = low(layer_norm(middle, second_gain, second_shift))
    before = low_back(product(second, expand_weight) + expand_bias)
    active = low(jax.nn.gelu(before, approximate=True))
    return middle + (product(active, reduce_weight) + reduce_bias)

def reference(inputs, block_order, first_gain, first_shift, joint_weight, query_bias, value_bias, mixer_weight, mixer_bias, second_gain, second_shift, expand_weight, expand_bias, reduce_weight, reduce_bias, cotangent):
    params = tuple((item.astype(jnp.float32) for item in (first_gain, first_shift, joint_weight, query_bias, value_bias, mixer_weight, mixer_bias, second_gain, second_shift, expand_weight, expand_bias, reduce_weight, reduce_bias)))
    indices = jnp.arange(LENGTH).astype(jnp.int32)
    places = (block_order[indices // BLOCK].astype(jnp.int32) * BLOCK + indices % BLOCK).astype(jnp.int32)

    def forward(rows_in, *weights):
        return block_forward(rows_in, places, *weights)

    def one_sequence(running, pair_in):
        sequence_rows, sequence_cotangent = pair_in
        output_rows, pull_back = jax.vjp(forward, sequence_rows, *params)
        pulled = pull_back(sequence_cotangent)
        updated = tuple((running_sum + new_piece for running_sum, new_piece in zip(running, pulled[1:])))
        return (updated, (output_rows.astype(jnp.bfloat16), pulled[0].astype(jnp.bfloat16)))
    start = tuple((jnp.zeros(item.shape, jnp.float32) for item in params))
    sums, (outputs, input_grads) = lax.scan(one_sequence, start, (inputs.astype(jnp.float32), cotangent.astype(jnp.float32)))
    return (outputs, input_grads, sums[0], sums[1], sums[2], sums[3], sums[4], sums[5], sums[6], sums[7], sums[8], sums[9], sums[10], sums[11], sums[12])
```

```python
import jax
import jax.numpy as jnp
from jax import lax
from jax.experimental import pallas as pl
from jax.experimental.pallas import tpu as pltpu
from jax.sharding import PartitionSpec as P

D = 1024
H = 16
HD = 64


EPS = 1e-05


def passed_along(value, axis, steps):
    count = lax.axis_size(axis)
    pairs = [(source, (source + steps) % count) for source in range(count)]
    return lax.ppermute(value, axis, pairs)


def layer_norm(values, scaling, offset):
    average = jnp.mean(values, axis=-1, keepdims=True)
    centred = values - average
    spread = jnp.mean(centred * centred, axis=-1, keepdims=True)
    return centred * lax.rsqrt(spread + EPS) * scaling + offset


def gelu_tanh(values):
    return jax.nn.gelu(values, approximate=True)


def product(left, right):
    return jnp.dot(left, right, preferred_element_type=jnp.float32)


def inner_rows(left, right):
    return lax.dot_general(
        left, right, (((0,), (0,)), ((), ())), preferred_element_type=jnp.float32
    )


def inner_cols(left, right):
    return lax.dot_general(
        left, right, (((1,), (1,)), ((), ())), preferred_element_type=jnp.float32
    )


def tile_forward(queries, key_rows, value_rows, visible, factor):
    scores = jnp.einsum("tqhd,tkhd->thqk", queries, key_rows, preferred_element_type=jnp.float32)
    powers = jnp.exp(scores * factor)
    if visible is not None:
        powers = jnp.where(visible[:, None], powers, 0.0)
    unnorm = jnp.einsum(
        "thqk,tkhd->tqhd",
        powers.astype(jnp.bfloat16),
        value_rows,
        preferred_element_type=jnp.float32,
    )
    return (unnorm, jnp.sum(powers, axis=-1))


def tile_backward(queries, grad_unnorm, grad_totals, key_rows, value_rows, visible, factor):
    scores = jnp.einsum("tqhd,tkhd->thqk", queries, key_rows, preferred_element_type=jnp.float32)
    powers = jnp.exp(scores * factor)
    if visible is not None:
        powers = jnp.where(visible[:, None], powers, 0.0)
    grad_powers = (
        jnp.einsum("tqhd,tkhd->thqk", grad_unnorm, value_rows, preferred_element_type=jnp.float32)
        + grad_totals[..., None]
    )
    grad_scores = (powers * grad_powers * factor).astype(jnp.bfloat16)
    grad_queries = jnp.einsum(
        "thqk,tkhd->tqhd", grad_scores, key_rows, preferred_element_type=jnp.float32
    )
    grad_keys = jnp.einsum(
        "thqk,tqhd->tkhd", grad_scores, queries, preferred_element_type=jnp.float32
    )
    grad_values = jnp.einsum(
        "thqk,tqhd->tkhd",
        powers.astype(jnp.bfloat16),
        grad_unnorm,
        preferred_element_type=jnp.float32,
    )
    return (grad_queries, grad_keys, grad_values)


def halves(stacked, half_rows, along):
    return (
        lax.slice_in_dim(stacked, 0, half_rows, axis=along),
        lax.slice_in_dim(stacked, half_rows, 2 * half_rows, axis=along),
    )


def query_stack(later_block, stacked, half_rows, along):
    lower_part, upper_part = halves(stacked, half_rows, along)
    return jnp.stack([upper_part, jnp.where(later_block, lower_part, upper_part)])


def key_stack(later_block, stacked, half_rows, along):
    lower_part, upper_part = halves(stacked, half_rows, along)
    return jnp.stack([lower_part, jnp.where(later_block, lower_part, upper_part)])


def query_spread(later_block, tile_pair, along):
    nothing = jnp.zeros_like(tile_pair[0])
    lower_part = jnp.where(later_block, tile_pair[1], nothing)
    upper_part = tile_pair[0] + jnp.where(later_block, nothing, tile_pair[1])
    return jnp.concatenate([lower_part, upper_part], axis=along)


def key_spread(later_block, tile_pair, along):
    nothing = jnp.zeros_like(tile_pair[0])
    lower_part = tile_pair[0] + jnp.where(later_block, tile_pair[1], nothing)
    upper_part = jnp.where(later_block, nothing, tile_pair[1])
    return jnp.concatenate([lower_part, upper_part], axis=along)


def pair_forward(later_block, queries, key_rows, value_rows, factor):
    half_rows = queries.shape[0] // 2
    unnorm, totals = tile_forward(
        query_stack(later_block, queries, half_rows, 0),
        key_stack(later_block, key_rows, half_rows, 0),
        key_stack(later_block, value_rows, half_rows, 0),
        None,
        factor,
    )
    return (query_spread(later_block, unnorm, 0), query_spread(later_block, totals, 1))


def pair_backward(later_block, queries, grad_unnorm, grad_totals, key_rows, value_rows, factor):
    half_rows = queries.shape[0] // 2
    grads = tile_backward(
        query_stack(later_block, queries, half_rows, 0),
        query_stack(later_block, grad_unnorm, half_rows, 0),
        query_stack(later_block, grad_totals, half_rows, 1),
        key_stack(later_block, key_rows, half_rows, 0),
        key_stack(later_block, value_rows, half_rows, 0),
        None,
        factor,
    )
    return (
        query_spread(later_block, grads[0], 0),
        key_spread(later_block, grads[1], 0),
        key_spread(later_block, grads[2], 0),
    )


def ring_body(
    inputs,
    block_order,
    first_gain,
    first_shift,
    joint_weight,
    query_bias,
    value_bias,
    mixer_weight,
    mixer_bias,
    second_gain,
    second_shift,
    expand_weight,
    expand_bias,
    reduce_weight,
    reduce_bias,
    cotangent,
):
    owned_shards = (
        first_gain,
        first_shift,
        joint_weight,
        query_bias,
        value_bias,
        mixer_weight,
        mixer_bias,
        second_gain,
        second_shift,
        expand_weight,
        expand_bias,
        reduce_weight,
        reduce_bias,
    )
    gathered = (
        lax.all_gather(owned_shards[0], ("dp", "sp"), axis=0, tiled=True),
        lax.all_gather(owned_shards[1], ("dp", "sp"), axis=0, tiled=True),
        lax.all_gather(owned_shards[2], ("dp", "sp"), axis=0, tiled=True),
        lax.all_gather(owned_shards[3], ("dp", "sp"), axis=0, tiled=True),
        lax.all_gather(owned_shards[4], ("dp", "sp"), axis=0, tiled=True),
        lax.all_gather(owned_shards[5], ("dp", "sp"), axis=0, tiled=True),
        lax.all_gather(owned_shards[6], ("dp", "sp"), axis=0, tiled=True),
        lax.all_gather(owned_shards[7], ("dp", "sp"), axis=0, tiled=True),
        lax.all_gather(owned_shards[8], ("dp", "sp"), axis=0, tiled=True),
        lax.all_gather(owned_shards[9], ("dp", "sp"), axis=0, tiled=True),
        lax.all_gather(owned_shards[10], ("dp", "sp"), axis=0, tiled=True),
        lax.all_gather(owned_shards[11], ("dp", "sp"), axis=0, tiled=True),
        lax.all_gather(owned_shards[12], ("dp", "sp"), axis=0, tiled=True),
    )
    (
        gain_one,
        shift_one,
        joint_full,
        query_shift,
        value_shift,
        mixer_full,
        mixer_shift,
        gain_two,
        shift_two,
        expand_full,
        expand_shift,
        reduce_full,
        reduce_shift,
    ) = gathered
    factor = HD ** (-0.5)
    members = lax.axis_size("sp")
    position = lax.axis_index("sp")
    token_rows = inputs[0].astype(jnp.float32)
    row_count = token_rows.shape[0]
    half_rows = row_count // 2
    own_low = block_order[2 * position]
    offsets = jnp.arange(half_rows, dtype=jnp.int32)
    own_places = jnp.concatenate(
        [own_low * half_rows + offsets, block_order[2 * position + 1] * half_rows + offsets]
    )
    visible = (own_places[None, :] <= own_places[:, None])[None]
    normed, first_pull = jax.vjp(
        layer_norm, token_rows, gain_one.astype(jnp.float32), shift_one.astype(jnp.float32)
    )
    normed_low = normed.astype(jnp.bfloat16)
    joint_shift = jnp.concatenate([query_shift, jnp.zeros_like(query_shift), value_shift]).astype(
        jnp.float32
    )
    joint_rows = (product(normed_low, joint_full) + joint_shift).astype(jnp.bfloat16)
    queries = joint_rows[:, :D].reshape(row_count, H, HD)
    key_rows = joint_rows[:, D : 2 * D].reshape(row_count, H, HD)
    value_rows = joint_rows[:, 2 * D :].reshape(row_count, H, HD)
    unnorm, totals = tile_forward(queries[None], key_rows[None], value_rows[None], visible, factor)

    def forward_turn(turn_index, state_in):
        moving_keys, moving_values, unnorm_sum, totals_sum = state_in
        moving_keys, moving_values = passed_along((moving_keys, moving_values), "sp", 1)
        source = (position - turn_index) % members
        later_block = own_low > block_order[2 * source]
        extra_unnorm, extra_totals = pair_forward(
            later_block, queries, moving_keys, moving_values, factor
        )
        return (moving_keys, moving_values, unnorm_sum + extra_unnorm, totals_sum + extra_totals)

    final_state = lax.fori_loop(
        1, members, forward_turn, (key_rows, value_rows, unnorm[0], totals[0])
    )
    unnorm = final_state[2]
    totals_rows = jnp.transpose(final_state[3])
    mixed = unnorm / totals_rows[:, :, None]
    mixed_rows = mixed.reshape(row_count, D).astype(jnp.bfloat16)
    middle = token_rows + (product(mixed_rows, mixer_full) + mixer_shift.astype(jnp.float32))
    second, second_pull = jax.vjp(
        layer_norm, middle, gain_two.astype(jnp.float32), shift_two.astype(jnp.float32)
    )
    second_low = second.astype(jnp.bfloat16)
    before = product(second_low, expand_full) + expand_shift.astype(jnp.float32)
    active, gelu_pull = jax.vjp(gelu_tanh, before)
    active_low = active.astype(jnp.bfloat16)
    result = middle + (product(active_low, reduce_full) + reduce_shift.astype(jnp.float32))
    joint_back, mixer_back, expand_back, reduce_back = (
        lax.all_gather(joint_weight, ("dp", "sp"), axis=0, tiled=True),
        lax.all_gather(mixer_weight, ("dp", "sp"), axis=0, tiled=True),
        lax.all_gather(expand_weight, ("dp", "sp"), axis=0, tiled=True),
        lax.all_gather(reduce_weight, ("dp", "sp"), axis=0, tiled=True),
    )
    upstream = cotangent[0]
    upstream_full = upstream.astype(jnp.float32)
    reduce_gradient = inner_rows(active_low, upstream)
    reduce_shift_gradient = jnp.sum(upstream_full, axis=0)
    grad_active = inner_cols(upstream, reduce_back)
    grad_before = gelu_pull(grad_active)[0].astype(jnp.bfloat16)
    expand_gradient = inner_rows(second_low, grad_before)
    expand_shift_gradient = jnp.sum(grad_before.astype(jnp.float32), axis=0)
    grad_second = inner_cols(grad_before, expand_back)
    grad_middle_norm, gain_two_gradient, shift_two_gradient = second_pull(grad_second)
    grad_middle = upstream_full + grad_middle_norm
    grad_branch = grad_middle.astype(jnp.bfloat16)
    mixer_gradient = inner_rows(mixed_rows, grad_branch)
    mixer_shift_gradient = jnp.sum(grad_branch.astype(jnp.float32), axis=0)
    grad_mixed = inner_cols(grad_branch, mixer_back).astype(jnp.bfloat16).reshape(row_count, H, HD)
    grad_mixed_full = grad_mixed.astype(jnp.float32)
    grad_unnorm = (grad_mixed_full / totals_rows[:, :, None]).astype(jnp.bfloat16)
    grad_totals = jnp.transpose(-jnp.sum(grad_mixed_full * mixed, axis=-1) / totals_rows)
    own_grads = tile_backward(
        queries[None],
        grad_unnorm[None],
        grad_totals[None],
        key_rows[None],
        value_rows[None],
        visible,
        factor,
    )

    def keys_turn(turn_index, state_in):
        moving_keys, moving_values, key_carry, value_carry, query_sum = state_in
        moving_keys, moving_values = passed_along((moving_keys, moving_values), "sp", 1)
        key_carry, value_carry = (
            passed_along(key_carry.astype(jnp.bfloat16), "sp", 1).astype(key_carry.dtype),
            passed_along(value_carry.astype(jnp.bfloat16), "sp", 1).astype(value_carry.dtype),
        )
        source = (position - turn_index) % members
        later_block = own_low > block_order[2 * source]
        extra_query, extra_key, extra_value = pair_backward(
            later_block, queries, grad_unnorm, grad_totals, moving_keys, moving_values, factor
        )
        return (
            moving_keys,
            moving_values,
            key_carry + extra_key,
            value_carry + extra_value,
            query_sum + extra_query,
        )

    final_back = lax.fori_loop(
        1,
        members,
        keys_turn,
        (key_rows, value_rows, own_grads[1][0], own_grads[2][0], own_grads[0][0]),
    )
    key_sum, value_sum = (
        passed_along(final_back[2].astype(jnp.bfloat16), "sp", 1).astype(jnp.float32),
        passed_along(final_back[3].astype(jnp.bfloat16), "sp", 1).astype(jnp.float32),
    )
    query_sum = final_back[4]
    grad_joint = jnp.concatenate(
        [
            query_sum.reshape(row_count, D),
            key_sum.reshape(row_count, D),
            value_sum.reshape(row_count, D),
        ],
        axis=1,
    ).astype(jnp.bfloat16)
    joint_gradient = inner_rows(normed_low, grad_joint)
    joint_sums = jnp.sum(grad_joint.astype(jnp.float32), axis=0)
    query_shift_gradient = joint_sums[:D]
    value_shift_gradient = joint_sums[2 * D :]
    grad_normed = inner_cols(grad_joint, joint_back)
    grad_rows_norm, gain_one_gradient, shift_one_gradient = first_pull(grad_normed)
    input_gradient = (grad_middle + grad_rows_norm).astype(jnp.bfloat16)
    gradient_sums = (
        lax.psum_scatter(gain_one_gradient, ("dp", "sp"), scatter_dimension=0, tiled=True),
        lax.psum_scatter(shift_one_gradient, ("dp", "sp"), scatter_dimension=0, tiled=True),
        lax.psum_scatter(joint_gradient, ("dp", "sp"), scatter_dimension=0, tiled=True),
        lax.psum_scatter(query_shift_gradient, ("dp", "sp"), scatter_dimension=0, tiled=True),
        lax.psum_scatter(value_shift_gradient, ("dp", "sp"), scatter_dimension=0, tiled=True),
        lax.psum_scatter(mixer_gradient, ("dp", "sp"), scatter_dimension=0, tiled=True),
        lax.psum_scatter(mixer_shift_gradient, ("dp", "sp"), scatter_dimension=0, tiled=True),
        lax.psum_scatter(gain_two_gradient, ("dp", "sp"), scatter_dimension=0, tiled=True),
        lax.psum_scatter(shift_two_gradient, ("dp", "sp"), scatter_dimension=0, tiled=True),
        lax.psum_scatter(expand_gradient, ("dp", "sp"), scatter_dimension=0, tiled=True),
        lax.psum_scatter(expand_shift_gradient, ("dp", "sp"), scatter_dimension=0, tiled=True),
        lax.psum_scatter(reduce_gradient, ("dp", "sp"), scatter_dimension=0, tiled=True),
        lax.psum_scatter(reduce_shift_gradient, ("dp", "sp"), scatter_dimension=0, tiled=True),
    )
    return (result.astype(jnp.bfloat16)[None], input_gradient[None]) + tuple(gradient_sums)


ALL = ("dp", "sp")
CORE_BIT = 1
Z_BITS = (0, 2, 4, 6)
X_BIT = 8
Y_BIT = 16
TILE = 512
BLOCK_ROWS = 128


def swapped(value, mask):
    count = lax.axis_size("dp") * lax.axis_size("sp")
    return lax.ppermute(value, ALL, [(source, source ^ mask) for source in range(count)])


def placed_kernel(slot_ref, *refs, col_blocks):
    pieces, out_ref, sem = refs[:16], refs[16], refs[17]
    width = pieces[0].shape[1] // col_blocks
    copies = []
    for at in range(16):
        row = slot_ref[at]
        for col in range(col_blocks):
            if col_blocks == 1:
                target = out_ref.at[row]
                source = pieces[at]
            else:
                source = pieces[at].at[:, pl.ds(col * width, width)]
                to = pl.multiple_of(slot_ref[16 + col] * width, 128)
                target = out_ref.at[row, :, pl.ds(to, width)]
            copy = pltpu.make_async_copy(source, target, sem.at[at * col_blocks + col])
            copy.start()
            copies.append(copy)
    for copy in copies:
        copy.wait()


def placed(pieces, slots, col_blocks=1):
    rows, cols = pieces[0].shape
    return pl.pallas_call(
        lambda *refs: placed_kernel(*refs, col_blocks=col_blocks),
        out_shape=jax.ShapeDtypeStruct((16, rows, cols), pieces[0].dtype),
        in_specs=[pl.BlockSpec(memory_space=pltpu.SMEM)] + [pl.BlockSpec(memory_space=pl.ANY)] * 16,
        out_specs=pl.BlockSpec(memory_space=pltpu.VMEM),
        scratch_shapes=[pltpu.SemaphoreType.DMA((16 * col_blocks,))],
        name="placed",
    )(slots, *pieces)


def spread_kernel(slot_ref, whole_ref, *refs, col_blocks):
    outs, sem = refs[:4], refs[4]
    width = whole_ref.shape[2] // col_blocks
    copies = []
    for at in range(16):
        row = slot_ref[at]
        across, along = at // 4, at % 4
        if along < 2:
            group, place = (0, across * 2 + along) if across < 2 else (1, (across - 2) * 2 + along)
        else:
            group, place = (2 + across % 2, (across // 2) * 2 + along - 2)
        for col in range(col_blocks):
            if col_blocks == 1:
                source, target = whole_ref.at[row], outs[group].at[place]
            else:
                to = pl.multiple_of(slot_ref[16 + col] * width, 128)
                source = whole_ref.at[row, :, pl.ds(to, width)]
                target = outs[group].at[place, :, pl.ds(col * width, width)]
            copy = pltpu.make_async_copy(source, target, sem.at[at * col_blocks + col])
            copy.start()
            copies.append(copy)
    for copy in copies:
        copy.wait()


def spread(whole, slots, col_blocks=1):
    rows, cols = whole.shape[1:]
    return pl.pallas_call(
        lambda *refs: spread_kernel(*refs, col_blocks=col_blocks),
        out_shape=[jax.ShapeDtypeStruct((4, rows, cols), whole.dtype)] * 4,
        in_specs=[pl.BlockSpec(memory_space=pltpu.SMEM), pl.BlockSpec(memory_space=pl.ANY)],
        out_specs=[pl.BlockSpec(memory_space=pltpu.VMEM)] * 4,
        scratch_shapes=[pltpu.SemaphoreType.DMA((16 * col_blocks,))],
        name="spread",
    )(slots, whole)


def collected(piece):
    line = [piece] + [swapped(piece, bits) for bits in Z_BITS[1:]]
    found = {}
    for along in range(4):
        first, second = (X_BIT, Y_BIT) if along < 2 else (Y_BIT, X_BIT)
        found[0, along] = line[along]
        found[first >> 3, along] = swapped(line[along], first)
        found[second >> 3, along] = swapped(line[along], second)
        found[3, along] = swapped(found[first >> 3, along], second)
    return [found[across, along] for across in range(4) for along in range(4)]


def summed(whole, slots, col_blocks=1):
    low = jnp.bfloat16
    full = jnp.float32
    keep_a, send_a, keep_b, send_b = spread(whole, slots, col_blocks)
    got_a = swapped(send_a, Y_BIT)
    got_b = swapped(send_b, X_BIT)
    onward_a = (keep_a[2:].astype(full) + got_a[2:].astype(full)).astype(low)
    onward_b = (keep_b[2:].astype(full) + got_b[2:].astype(full)).astype(low)
    here_a = keep_a[:2].astype(full) + got_a[:2].astype(full)
    here_b = keep_b[:2].astype(full) + got_b[:2].astype(full)
    here_a = here_a + swapped(onward_a, X_BIT).astype(full)
    here_b = here_b + swapped(onward_b, Y_BIT).astype(full)
    return (
        here_a[0]
        + swapped(here_a[1].astype(low), Z_BITS[1]).astype(full)
        + swapped(here_b[0].astype(low), Z_BITS[2]).astype(full)
        + swapped(here_b[1].astype(low), Z_BITS[3]).astype(full)
    )


def lanes_low(rows):
    return lax.broadcasted_iota(jnp.int32, (rows, 2 * HD), 1) < HD


def head_forward_kernel(place_ref, *refs):
    pieces, sends, (joint_ref, mixed_ref, totals_ref), (acc_ref,) = (
        refs[:4],
        refs[4:8],
        refs[8:11],
        refs[11:],
    )
    wide = 2 * HD
    for at in range(16):
        to = pl.multiple_of(place_ref[at] * BLOCK_ROWS, BLOCK_ROWS)
        joint_ref[pl.ds(to, BLOCK_ROWS), :] = pieces[at // 4][
            (at % 4) * BLOCK_ROWS : (at % 4 + 1) * BLOCK_ROWS, :
        ]
    first = lanes_low(TILE)
    sides = (first, jnp.logical_not(first))
    row_ids = lax.broadcasted_iota(jnp.int32, (TILE, TILE), 0)
    col_ids = lax.broadcasted_iota(jnp.int32, (TILE, TILE), 1)
    causal = col_ids <= row_ids

    def tile_part(queries, key_at, masked):
        key_at = pl.multiple_of(key_at, TILE)
        key_rows = joint_ref[pl.ds(key_at, TILE), wide : 2 * wide]
        value_rows = joint_ref[pl.ds(key_at, TILE), 2 * wide :]
        for side in range(2):
            powers = jnp.exp(inner_cols(queries[side], key_rows))
            if masked:
                powers = jnp.where(causal, powers, 0.0)
            extended = jnp.where(sides[side], value_rows, jnp.ones_like(value_rows))
            acc_ref[side] += product(powers.astype(jnp.bfloat16), extended)

    def query_tile(index, carry):
        query_at = pl.multiple_of(index * TILE, TILE)
        scaled = joint_ref[pl.ds(query_at, TILE), :wide] * jnp.bfloat16(HD**-0.5)
        nothing = jnp.zeros_like(scaled)
        queries = [jnp.where(side, scaled, nothing) for side in sides]
        acc_ref[...] = jnp.zeros_like(acc_ref)

        def key_tile(key_index, inner):
            tile_part(queries, key_index * TILE, False)
            return inner

        lax.fori_loop(0, index, key_tile, 0)
        tile_part(queries, query_at, True)
        low_acc, high_acc = acc_ref[0], acc_ref[1]
        unnorm = jnp.where(first, low_acc, high_acc)
        totals = pltpu.roll(jnp.where(first, high_acc, low_acc), HD, 1)
        totals_ref[pl.ds(query_at, TILE), :] = totals
        mixed_ref[pl.ds(query_at, TILE), :] = unnorm / totals
        return carry

    lax.fori_loop(0, joint_ref.shape[0] // TILE, query_tile, 0)
    for at in range(16):
        to = pl.multiple_of(place_ref[at] * BLOCK_ROWS, BLOCK_ROWS)
        sends[at // 4][(at % 4) * BLOCK_ROWS : (at % 4 + 1) * BLOCK_ROWS, :] = mixed_ref[
            pl.ds(to, BLOCK_ROWS), :
        ].astype(jnp.bfloat16)


def head_forward(pieces, places):
    rows, wide = pieces[0].shape
    total_rows = 4 * rows
    vmem = pl.BlockSpec(memory_space=pltpu.VMEM)
    return pl.pallas_call(
        head_forward_kernel,
        out_shape=[jax.ShapeDtypeStruct((rows, 2 * HD), jnp.bfloat16)] * 4
        + [
            jax.ShapeDtypeStruct((total_rows, wide), jnp.bfloat16),
            jax.ShapeDtypeStruct((total_rows, 2 * HD), jnp.float32),
            jax.ShapeDtypeStruct((total_rows, 2 * HD), jnp.float32),
        ],
        in_specs=[pl.BlockSpec(memory_space=pltpu.SMEM)] + [vmem] * 4,
        out_specs=[vmem] * 7,
        scratch_shapes=[pltpu.VMEM((2, TILE, 2 * HD), jnp.float32)],
        name="head_forward",
    )(places, *pieces)


def head_backward_kernel(place_ref, joint_ref, mixed_ref, totals_ref, *refs):
    pieces, sends, (grad_ref, side_ref, query_ref, key_ref, value_ref, joint_grad) = (
        refs[:4],
        refs[4:8],
        refs[8:],
    )
    wide = 2 * HD
    total_rows = joint_ref.shape[0]
    for at in range(16):
        to = pl.multiple_of(place_ref[at] * BLOCK_ROWS, BLOCK_ROWS)
        grad_ref[pl.ds(to, BLOCK_ROWS), :] = pieces[at // 4][
            (at % 4) * BLOCK_ROWS : (at % 4 + 1) * BLOCK_ROWS, :
        ].astype(jnp.float32)
    first = lanes_low(TILE)
    sides = (first, jnp.logical_not(first))
    lane_ids = lax.broadcasted_iota(jnp.int32, (TILE, wide), 1)
    key_ids = lax.broadcasted_iota(jnp.int32, (TILE, TILE), 0)
    query_ids = lax.broadcasted_iota(jnp.int32, (TILE, TILE), 1)
    causal = key_ids <= query_ids

    def prepare(index, carry):
        at = pl.multiple_of(index * TILE, TILE)
        grad_mixed = grad_ref[pl.ds(at, TILE), :]
        totals = totals_ref[pl.ds(at, TILE), :]
        grad_unnorm = (grad_mixed / totals).astype(jnp.bfloat16).astype(jnp.float32)
        weighed = grad_mixed * mixed_ref[pl.ds(at, TILE), :] / totals
        for side in range(2):
            grad_totals = -jnp.sum(
                jnp.where(sides[side], weighed, 0.0), axis=1, keepdims=True
            )
            coarse = grad_totals.astype(jnp.bfloat16).astype(jnp.float32)
            fine = grad_totals - coarse
            base = (1 - side) * HD
            extra = jnp.where(
                lane_ids == base, coarse, jnp.where(lane_ids == base + 1, fine, 0.0)
            )
            side_ref[side, pl.ds(at, TILE), :] = jnp.where(
                sides[side], grad_unnorm, extra
            ).astype(jnp.bfloat16)
        return carry

    lax.fori_loop(0, total_rows // TILE, prepare, 0)
    query_ref[...] = jnp.zeros_like(query_ref)

    def tile_part(query_at, key_rows, values, masked):
        query_at = pl.multiple_of(query_at, TILE)
        scaled = joint_ref[pl.ds(query_at, TILE), :wide] * jnp.bfloat16(HD**-0.5)
        nothing = jnp.zeros_like(scaled)
        for side in range(2):
            powers = jnp.exp(inner_cols(key_rows, jnp.where(sides[side], scaled, nothing)))
            if masked:
                powers = jnp.where(causal, powers, 0.0)
            upstream = side_ref[side, pl.ds(query_at, TILE), :]
            grad_scores = (powers * inner_cols(values[side], upstream)).astype(jnp.bfloat16)
            value_ref[side] += product(powers.astype(jnp.bfloat16), upstream)
            key_ref[side] += product(grad_scores, scaled)
            query_ref[side, pl.ds(query_at, TILE), :] += inner_rows(grad_scores, key_rows)

    def key_tile(index, carry):
        key_at = pl.multiple_of(index * TILE, TILE)
        key_rows = joint_ref[pl.ds(key_at, TILE), wide : 2 * wide]
        value_rows = joint_ref[pl.ds(key_at, TILE), 2 * wide :]
        values = [jnp.where(side, value_rows, jnp.ones_like(value_rows)) for side in sides]
        key_ref[...] = jnp.zeros_like(key_ref)
        value_ref[...] = jnp.zeros_like(value_ref)
        tile_part(key_at, key_rows, values, True)

        def query_tile(query_index, inner):
            tile_part(query_index * TILE, key_rows, values, False)
            return inner

        lax.fori_loop(index + 1, total_rows // TILE, query_tile, 0)
        joint_grad[pl.ds(key_at, TILE), wide : 2 * wide] = jnp.where(
            first, key_ref[0], key_ref[1]
        ).astype(jnp.bfloat16)
        joint_grad[pl.ds(key_at, TILE), 2 * wide :] = jnp.where(
            first, value_ref[0], value_ref[1]
        ).astype(jnp.bfloat16)
        return carry

    lax.fori_loop(0, total_rows // TILE, key_tile, 0)

    def finish(index, carry):
        at = pl.multiple_of(index * TILE, TILE)
        joint_grad[pl.ds(at, TILE), :wide] = (
            jnp.where(first, query_ref[0, pl.ds(at, TILE), :], query_ref[1, pl.ds(at, TILE), :])
            * HD**-0.5
        ).astype(jnp.bfloat16)
        return carry

    lax.fori_loop(0, total_rows // TILE, finish, 0)
    for at in range(16):
        to = pl.multiple_of(place_ref[at] * BLOCK_ROWS, BLOCK_ROWS)
        sends[at // 4][(at % 4) * BLOCK_ROWS : (at % 4 + 1) * BLOCK_ROWS, :] = joint_grad[
            pl.ds(to, BLOCK_ROWS), :
        ]


def head_backward(joint_sorted, mixed_sorted, totals_sorted, pieces, places):
    rows = pieces[0].shape[0]
    total_rows, wide = joint_sorted.shape
    vmem = pl.BlockSpec(memory_space=pltpu.VMEM)
    return pl.pallas_call(
        head_backward_kernel,
        out_shape=[jax.ShapeDtypeStruct((rows, wide), jnp.bfloat16)] * 4,
        in_specs=[pl.BlockSpec(memory_space=pltpu.SMEM)] + [vmem] * 7,
        out_specs=[vmem] * 4,
        scratch_shapes=[
            pltpu.VMEM((total_rows, 2 * HD), jnp.float32),
            pltpu.VMEM((2, total_rows, 2 * HD), jnp.bfloat16),
            pltpu.VMEM((2, total_rows, 2 * HD), jnp.float32),
            pltpu.VMEM((2, TILE, 2 * HD), jnp.float32),
            pltpu.VMEM((2, TILE, 2 * HD), jnp.float32),
            pltpu.VMEM((total_rows, wide), jnp.bfloat16),
        ],
        name="head_backward",
    )(places, joint_sorted, mixed_sorted, totals_sorted, *pieces)


def norm_parts(values):
    average = jnp.mean(values, axis=-1, keepdims=True)
    centred = values - average
    spread_of = jnp.mean(centred * centred, axis=-1, keepdims=True)
    inverse = lax.rsqrt(spread_of + EPS)
    return centred * inverse, inverse


def norm_pull(grad, scaled, inverse, gain):
    lifted = grad * gain
    return (
        lifted
        - jnp.mean(lifted, axis=-1, keepdims=True)
        - scaled * jnp.mean(lifted * scaled, axis=-1, keepdims=True)
    ) * inverse


def chip_body(
    inputs,
    block_order,
    first_gain,
    first_shift,
    joint_weight,
    query_bias,
    value_bias,
    mixer_weight,
    mixer_bias,
    second_gain,
    second_shift,
    expand_weight,
    expand_bias,
    reduce_weight,
    reduce_bias,
    cotangent,
):
    low, full = jnp.bfloat16, jnp.float32
    position = lax.axis_index("sp")
    group = lax.axis_index("dp")
    core = position % 2
    depth = position // 2
    even = core == 0
    own_rows = inputs.shape[1]
    share = joint_weight.shape[0]

    def own_first(value):
        return jnp.concatenate([value, swapped(value, CORE_BIT)], axis=0)

    def chip_order(mine, theirs):
        return jnp.where(
            even,
            jnp.concatenate([mine, theirs], axis=0),
            jnp.concatenate([theirs, mine], axis=0),
        )

    def cores_exchanged(parts):
        mine = jnp.where(even, parts[0], parts[1])
        theirs = jnp.where(even, parts[1], parts[0])
        return chip_order(mine, swapped(theirs, CORE_BIT))

    chip_ids = jnp.arange(16, dtype=jnp.int32)
    across, along = chip_ids // 4, chip_ids % 4
    slots = (across ^ group) * 4 + (along ^ depth)
    col_slots = jnp.arange(4, dtype=jnp.int32) ^ depth
    joint_slots = jnp.concatenate([slots, col_slots])
    mixer_slots = ((slots // 8) ^ core) * 8 + (((slots // 2) % 4) ^ depth) * 2 + slots % 2
    places = block_order[
        ((chip_ids // 4) ^ depth) * 4 + (((chip_ids // 2) % 2) ^ core) * 2 + chip_ids % 2
    ]

    small = jnp.concatenate(
        [
            first_gain,
            first_shift,
            query_bias,
            value_bias,
            mixer_bias,
            second_gain,
            second_shift,
            reduce_bias,
            expand_bias,
        ]
    ).reshape(1, -1)
    small_line = chip_order(small, swapped(small, CORE_BIT))[None]
    small_line = jnp.concatenate([small_line] + [swapped(small_line, bits) for bits in Z_BITS[1:]])
    small_all = jnp.concatenate(
        [small_line[None]] + [swapped(small_line, bits)[None] for bits in (X_BIT, Y_BIT, X_BIT + Y_BIT)]
    ).reshape(16, -1)
    pick = (slots[None, :] == chip_ids[:, None]).astype(low)
    small_all = product(pick, small_all).reshape(32, -1)
    count = share
    (
        gain_one,
        shift_one,
        query_shift,
        value_shift,
        mixer_shift,
        gain_two,
        shift_two,
        reduce_shift,
    ) = [small_all[:, at * count : (at + 1) * count].reshape(-1) for at in range(8)]
    expand_shift = small_all[:, 8 * count :].reshape(16, 2, 128)
    expand_shift = jnp.where(even, expand_shift[:, 0], expand_shift[:, 1]).reshape(-1)

    joint_parts = joint_weight.reshape(share, 3, 2, 4, 128).transpose(2, 0, 3, 1, 4).reshape(2, share, 1536)
    joint_own = cores_exchanged((joint_parts[0], joint_parts[1]))
    joint_full = placed(collected(joint_own), joint_slots, 4).reshape(D, 1536)
    mixer_own = cores_exchanged((mixer_weight[:, : D // 2], mixer_weight[:, D // 2 :]))
    mixer_cols = placed(collected(mixer_own), mixer_slots).reshape(2, D // 2, D // 2)
    mixer_mine, mixer_theirs = mixer_cols[0], swapped(mixer_cols[1], CORE_BIT)
    mixer_full = jnp.where(
        even,
        jnp.concatenate([mixer_mine, mixer_theirs], axis=1),
        jnp.concatenate([mixer_theirs, mixer_mine], axis=1),
    )
    units = expand_weight.shape[1] // 2
    expand_parts = expand_weight.reshape(share, 16, 2, 128)
    expand_own = cores_exchanged(
        (expand_parts[:, :, 0].reshape(share, units), expand_parts[:, :, 1].reshape(share, units))
    )
    expand_full = placed(collected(expand_own), slots).reshape(D, units)
    reduce_full = placed(collected(reduce_weight), slots).reshape(units, D)

    token_rows = own_first(inputs[0]).astype(full)
    upstream = own_first(cotangent[0])
    scaled_one, inverse_one = norm_parts(token_rows)
    normed = (scaled_one * gain_one + shift_one).astype(low)
    halves_of = [
        jnp.where(even, item[: D // 2], item[D // 2 :]).reshape(4, 1, 128)
        for item in (query_shift, value_shift)
    ]
    joint_shift = jnp.concatenate([halves_of[0], jnp.zeros_like(halves_of[0]), halves_of[1]], axis=1)
    joint_shift = product(
        (col_slots[:, None] == jnp.arange(4)[None, :]).astype(low), joint_shift.reshape(4, 384).astype(low)
    ).reshape(-1)
    joint_rows = (product(normed, joint_full) + joint_shift).astype(low)
    head_pieces = [joint_rows[:, at * 384 : (at + 1) * 384] for at in range(4)]
    head_pieces = [head_pieces[0]] + [swapped(head_pieces[at], Z_BITS[at]) for at in (1, 2, 3)]
    forward = head_forward(head_pieces, places)
    mixed_out, (joint_sorted, mixed_sorted, totals_sorted) = forward[:4], forward[4:]
    mixed_rows = jnp.concatenate(
        [mixed_out[0]] + [swapped(mixed_out[at], Z_BITS[at]) for at in (1, 2, 3)], axis=1
    )

    def both_cores(part):
        turned = jnp.concatenate([part[own_rows:], part[:own_rows]], axis=0).astype(low)
        return part + swapped(turned, CORE_BIT).astype(full)

    def own_sum(part):
        return part[:own_rows] + swapped(part[own_rows:].astype(low), CORE_BIT).astype(full)

    middle = token_rows + (both_cores(product(mixed_rows, mixer_full)) + mixer_shift)
    scaled_two, inverse_two = norm_parts(middle)
    second = (scaled_two * gain_two + shift_two).astype(low)
    before = product(second, expand_full) + expand_shift
    active, gelu_pull = jax.vjp(gelu_tanh, before)
    active = active.astype(low)
    result = middle[:own_rows] + (own_sum(product(active, reduce_full)) + reduce_shift)

    reduce_gradient = inner_rows(active, upstream).astype(low).reshape(16, 128, D)
    reduce_sum = summed(reduce_gradient, slots)
    grad_before = gelu_pull(inner_cols(upstream, reduce_full))[0].astype(low)
    expand_gradient = inner_rows(second, grad_before).astype(low).reshape(16, 64, units)
    expand_sum = summed(expand_gradient, slots)
    expand_shift_gradient = jnp.sum(grad_before.astype(full), axis=0)
    grad_second = both_cores(inner_cols(grad_before, expand_full))
    upstream_full = upstream.astype(full)
    grad_middle = upstream_full + norm_pull(grad_second, scaled_two, inverse_two, gain_two)
    grad_branch = grad_middle.astype(low)
    mixer_gradient = inner_rows(mixed_rows, grad_branch).astype(low)
    grad_mixed = inner_cols(grad_branch, mixer_full).astype(low)
    grad_pieces = [grad_mixed[:, at * 128 : (at + 1) * 128] for at in range(4)]
    grad_pieces = [grad_pieces[0]] + [swapped(grad_pieces[at], Z_BITS[at]) for at in (1, 2, 3)]
    mixer_keep = jnp.where(even, mixer_gradient[:, : D // 2], mixer_gradient[:, D // 2 :])
    mixer_send = jnp.where(even, mixer_gradient[:, D // 2 :], mixer_gradient[:, : D // 2])
    mixer_whole = jnp.concatenate([mixer_keep, swapped(mixer_send, CORE_BIT)], axis=0)
    mixer_sum = summed(mixer_whole.reshape(16, 64, D // 2), mixer_slots)
    grad_out = head_backward(joint_sorted, mixed_sorted, totals_sorted, grad_pieces, places)
    grad_joint = jnp.concatenate(
        [grad_out[0]] + [swapped(grad_out[at], Z_BITS[at]) for at in (1, 2, 3)], axis=1
    )
    joint_gradient = inner_rows(normed, grad_joint).astype(low).reshape(16, 64, 1536)
    joint_sum = summed(joint_gradient, joint_slots, 4)
    joint_sums = product(
        (col_slots[:, None] == jnp.arange(4)[None, :]).astype(full),
        jnp.sum(grad_joint.astype(full), axis=0).reshape(4, 384),
    ).reshape(4, 3, 128)
    grad_normed = own_sum(inner_cols(grad_joint, joint_full))
    own_scaled = scaled_one[:own_rows]
    input_gradient = (
        grad_middle[:own_rows] + norm_pull(grad_normed, own_scaled, inverse_one[:own_rows], gain_one)
    ).astype(low)

    def one_core(values):
        values = values.reshape(1, -1)
        nothing = jnp.zeros_like(values)
        return jnp.where(
            even, jnp.concatenate([values, nothing]), jnp.concatenate([nothing, values])
        )

    expand_rows = one_core(expand_shift_gradient).reshape(2, 16, 128).transpose(1, 0, 2)
    sums = jnp.concatenate(
        [
            item.reshape(32, -1)
            for item in (
                jnp.sum(grad_normed * own_scaled, axis=0),
                jnp.sum(grad_normed, axis=0),
                one_core(joint_sums[:, 0]),
                one_core(joint_sums[:, 2]),
                jnp.sum(grad_branch[:own_rows].astype(full), axis=0),
                jnp.sum(grad_second[:own_rows] * scaled_two[:own_rows], axis=0),
                jnp.sum(grad_second[:own_rows], axis=0),
                jnp.sum(upstream_full[:own_rows], axis=0),
                expand_rows,
            )
        ],
        axis=1,
    )
    for mask in (CORE_BIT, Z_BITS[1], Z_BITS[2], X_BIT, Y_BIT):
        sums = sums + swapped(sums, mask)
    own_sums = lax.dynamic_slice_in_dim(sums, group * 8 + position, 1, axis=0)[0]
    vectors = [own_sums[at * count : (at + 1) * count] for at in range(8)] + [own_sums[8 * count :]]

    def finished(total):
        mine = jnp.where(even, total[:share], total[share:])
        theirs = swapped(jnp.where(even, total[share:], total[:share]), CORE_BIT)
        return jnp.where(even, jnp.stack([mine, theirs], axis=0), jnp.stack([theirs, mine], axis=0))

    joint_out = finished(joint_sum).reshape(2, share, 4, 3, 128).transpose(1, 3, 0, 2, 4)
    mixer_out = finished(mixer_sum).transpose(1, 0, 2)
    expand_out = finished(expand_sum).reshape(2, share, 16, 128).transpose(1, 2, 0, 3)
    return (
        result.astype(low)[None],
        input_gradient[None],
        vectors[0],
        vectors[1],
        joint_out.reshape(share, 3 * D),
        vectors[2],
        vectors[3],
        mixer_out.reshape(share, D),
        vectors[4],
        vectors[5],
        vectors[6],
        expand_out.reshape(share, 2 * units),
        vectors[8],
        reduce_sum,
        vectors[7],
    )


def solution(mesh):
    in_specs = (
        P("dp", "sp", None),
        P(),
        P(("dp", "sp")),
        P(("dp", "sp")),
        P(("dp", "sp"), None),
        P(("dp", "sp")),
        P(("dp", "sp")),
        P(("dp", "sp"), None),
        P(("dp", "sp")),
        P(("dp", "sp")),
        P(("dp", "sp")),
        P(("dp", "sp"), None),
        P(("dp", "sp")),
        P(("dp", "sp"), None),
        P(("dp", "sp")),
        P("dp", "sp", None),
    )
    out_specs = (
        P("dp", "sp", None),
        P("dp", "sp", None),
        P(("dp", "sp")),
        P(("dp", "sp")),
        P(("dp", "sp"), None),
        P(("dp", "sp")),
        P(("dp", "sp")),
        P(("dp", "sp"), None),
        P(("dp", "sp")),
        P(("dp", "sp")),
        P(("dp", "sp")),
        P(("dp", "sp"), None),
        P(("dp", "sp")),
        P(("dp", "sp"), None),
        P(("dp", "sp")),
    )
    whole_pairs = mesh.shape["dp"] == 4 and mesh.shape["sp"] == 8
    body = chip_body if whole_pairs else ring_body
    return jax.shard_map(body, mesh=mesh, in_specs=in_specs, out_specs=out_specs, check_vma=False)
```

```python
import jax
import jax.numpy as jnp
from jax import lax
from jax.experimental import pallas as pl
from jax.experimental.pallas import tpu as pltpu
from jax.sharding import Mesh
from jax.sharding import PartitionSpec as P

D = 1024
H = 16
HD = 64


EPS = 1e-05


def passed_along(value, axis, steps):
    count = lax.axis_size(axis)
    pairs = [(source, (source + steps) % count) for source in range(count)]
    return lax.ppermute(value, axis, pairs)


def layer_norm(values, scaling, offset):
    average = jnp.mean(values, axis=-1, keepdims=True)
    centred = values - average
    spread = jnp.mean(centred * centred, axis=-1, keepdims=True)
    return centred * lax.rsqrt(spread + EPS) * scaling + offset


def gelu_tanh(values):
    return jax.nn.gelu(values, approximate=True)


def product(left, right):
    return jnp.dot(left, right, preferred_element_type=jnp.float32)


def inner_rows(left, right):
    return lax.dot_general(
        left, right, (((0,), (0,)), ((), ())), preferred_element_type=jnp.float32
    )


def inner_cols(left, right):
    return lax.dot_general(
        left, right, (((1,), (1,)), ((), ())), preferred_element_type=jnp.float32
    )


def tile_forward(queries, key_rows, value_rows, visible, factor):
    scores = jnp.einsum("tqhd,tkhd->thqk", queries, key_rows, preferred_element_type=jnp.float32)
    powers = jnp.exp(scores * factor)
    if visible is not None:
        powers = jnp.where(visible[:, None], powers, 0.0)
    unnorm = jnp.einsum(
        "thqk,tkhd->tqhd",
        powers.astype(jnp.bfloat16),
        value_rows,
        preferred_element_type=jnp.float32,
    )
    return (unnorm, jnp.sum(powers, axis=-1))


def tile_backward(queries, grad_unnorm, grad_totals, key_rows, value_rows, visible, factor):
    scores = jnp.einsum("tqhd,tkhd->thqk", queries, key_rows, preferred_element_type=jnp.float32)
    powers = jnp.exp(scores * factor)
    if visible is not None:
        powers = jnp.where(visible[:, None], powers, 0.0)
    grad_powers = (
        jnp.einsum("tqhd,tkhd->thqk", grad_unnorm, value_rows, preferred_element_type=jnp.float32)
        + grad_totals[..., None]
    )
    grad_scores = (powers * grad_powers * factor).astype(jnp.bfloat16)
    grad_queries = jnp.einsum(
        "thqk,tkhd->tqhd", grad_scores, key_rows, preferred_element_type=jnp.float32
    )
    grad_keys = jnp.einsum(
        "thqk,tqhd->tkhd", grad_scores, queries, preferred_element_type=jnp.float32
    )
    grad_values = jnp.einsum(
        "thqk,tqhd->tkhd",
        powers.astype(jnp.bfloat16),
        grad_unnorm,
        preferred_element_type=jnp.float32,
    )
    return (grad_queries, grad_keys, grad_values)


def halves(stacked, half_rows, along):
    return (
        lax.slice_in_dim(stacked, 0, half_rows, axis=along),
        lax.slice_in_dim(stacked, half_rows, 2 * half_rows, axis=along),
    )


def query_stack(later_block, stacked, half_rows, along):
    lower_part, upper_part = halves(stacked, half_rows, along)
    return jnp.stack([upper_part, jnp.where(later_block, lower_part, upper_part)])


def key_stack(later_block, stacked, half_rows, along):
    lower_part, upper_part = halves(stacked, half_rows, along)
    return jnp.stack([lower_part, jnp.where(later_block, lower_part, upper_part)])


def query_spread(later_block, tile_pair, along):
    nothing = jnp.zeros_like(tile_pair[0])
    lower_part = jnp.where(later_block, tile_pair[1], nothing)
    upper_part = tile_pair[0] + jnp.where(later_block, nothing, tile_pair[1])
    return jnp.concatenate([lower_part, upper_part], axis=along)


def key_spread(later_block, tile_pair, along):
    nothing = jnp.zeros_like(tile_pair[0])
    lower_part = tile_pair[0] + jnp.where(later_block, tile_pair[1], nothing)
    upper_part = jnp.where(later_block, nothing, tile_pair[1])
    return jnp.concatenate([lower_part, upper_part], axis=along)


def pair_forward(later_block, queries, key_rows, value_rows, factor):
    half_rows = queries.shape[0] // 2
    unnorm, totals = tile_forward(
        query_stack(later_block, queries, half_rows, 0),
        key_stack(later_block, key_rows, half_rows, 0),
        key_stack(later_block, value_rows, half_rows, 0),
        None,
        factor,
    )
    return (query_spread(later_block, unnorm, 0), query_spread(later_block, totals, 1))


def pair_backward(later_block, queries, grad_unnorm, grad_totals, key_rows, value_rows, factor):
    half_rows = queries.shape[0] // 2
    grads = tile_backward(
        query_stack(later_block, queries, half_rows, 0),
        query_stack(later_block, grad_unnorm, half_rows, 0),
        query_stack(later_block, grad_totals, half_rows, 1),
        key_stack(later_block, key_rows, half_rows, 0),
        key_stack(later_block, value_rows, half_rows, 0),
        None,
        factor,
    )
    return (
        query_spread(later_block, grads[0], 0),
        key_spread(later_block, grads[1], 0),
        key_spread(later_block, grads[2], 0),
    )


def ring_body(
    inputs,
    block_order,
    first_gain,
    first_shift,
    joint_weight,
    query_bias,
    value_bias,
    mixer_weight,
    mixer_bias,
    second_gain,
    second_shift,
    expand_weight,
    expand_bias,
    reduce_weight,
    reduce_bias,
    cotangent,
):
    owned_shards = (
        first_gain,
        first_shift,
        joint_weight,
        query_bias,
        value_bias,
        mixer_weight,
        mixer_bias,
        second_gain,
        second_shift,
        expand_weight,
        expand_bias,
        reduce_weight,
        reduce_bias,
    )
    gathered = (
        lax.all_gather(owned_shards[0], ("dp", "sp"), axis=0, tiled=True),
        lax.all_gather(owned_shards[1], ("dp", "sp"), axis=0, tiled=True),
        lax.all_gather(owned_shards[2], ("dp", "sp"), axis=0, tiled=True),
        lax.all_gather(owned_shards[3], ("dp", "sp"), axis=0, tiled=True),
        lax.all_gather(owned_shards[4], ("dp", "sp"), axis=0, tiled=True),
        lax.all_gather(owned_shards[5], ("dp", "sp"), axis=0, tiled=True),
        lax.all_gather(owned_shards[6], ("dp", "sp"), axis=0, tiled=True),
        lax.all_gather(owned_shards[7], ("dp", "sp"), axis=0, tiled=True),
        lax.all_gather(owned_shards[8], ("dp", "sp"), axis=0, tiled=True),
        lax.all_gather(owned_shards[9], ("dp", "sp"), axis=0, tiled=True),
        lax.all_gather(owned_shards[10], ("dp", "sp"), axis=0, tiled=True),
        lax.all_gather(owned_shards[11], ("dp", "sp"), axis=0, tiled=True),
        lax.all_gather(owned_shards[12], ("dp", "sp"), axis=0, tiled=True),
    )
    (
        gain_one,
        shift_one,
        joint_full,
        query_shift,
        value_shift,
        mixer_full,
        mixer_shift,
        gain_two,
        shift_two,
        expand_full,
        expand_shift,
        reduce_full,
        reduce_shift,
    ) = gathered
    factor = HD ** (-0.5)
    members = lax.axis_size("sp")
    position = lax.axis_index("sp")
    token_rows = inputs[0].astype(jnp.float32)
    row_count = token_rows.shape[0]
    half_rows = row_count // 2
    own_low = block_order[2 * position]
    offsets = jnp.arange(half_rows, dtype=jnp.int32)
    own_places = jnp.concatenate(
        [own_low * half_rows + offsets, block_order[2 * position + 1] * half_rows + offsets]
    )
    visible = (own_places[None, :] <= own_places[:, None])[None]
    normed, first_pull = jax.vjp(
        layer_norm, token_rows, gain_one.astype(jnp.float32), shift_one.astype(jnp.float32)
    )
    normed_low = normed.astype(jnp.bfloat16)
    joint_shift = jnp.concatenate([query_shift, jnp.zeros_like(query_shift), value_shift]).astype(
        jnp.float32
    )
    joint_rows = (product(normed_low, joint_full) + joint_shift).astype(jnp.bfloat16)
    queries = joint_rows[:, :D].reshape(row_count, H, HD)
    key_rows = joint_rows[:, D : 2 * D].reshape(row_count, H, HD)
    value_rows = joint_rows[:, 2 * D :].reshape(row_count, H, HD)
    unnorm, totals = tile_forward(queries[None], key_rows[None], value_rows[None], visible, factor)

    def forward_turn(turn_index, state_in):
        moving_keys, moving_values, unnorm_sum, totals_sum = state_in
        moving_keys, moving_values = passed_along((moving_keys, moving_values), "sp", 1)
        source = (position - turn_index) % members
        later_block = own_low > block_order[2 * source]
        extra_unnorm, extra_totals = pair_forward(
            later_block, queries, moving_keys, moving_values, factor
        )
        return (moving_keys, moving_values, unnorm_sum + extra_unnorm, totals_sum + extra_totals)

    final_state = lax.fori_loop(
        1, members, forward_turn, (key_rows, value_rows, unnorm[0], totals[0])
    )
    unnorm = final_state[2]
    totals_rows = jnp.transpose(final_state[3])
    mixed = unnorm / totals_rows[:, :, None]
    mixed_rows = mixed.reshape(row_count, D).astype(jnp.bfloat16)
    middle = token_rows + (product(mixed_rows, mixer_full) + mixer_shift.astype(jnp.float32))
    second, second_pull = jax.vjp(
        layer_norm, middle, gain_two.astype(jnp.float32), shift_two.astype(jnp.float32)
    )
    second_low = second.astype(jnp.bfloat16)
    before = product(second_low, expand_full) + expand_shift.astype(jnp.float32)
    active, gelu_pull = jax.vjp(gelu_tanh, before)
    active_low = active.astype(jnp.bfloat16)
    result = middle + (product(active_low, reduce_full) + reduce_shift.astype(jnp.float32))
    joint_back, mixer_back, expand_back, reduce_back = (
        lax.all_gather(joint_weight, ("dp", "sp"), axis=0, tiled=True),
        lax.all_gather(mixer_weight, ("dp", "sp"), axis=0, tiled=True),
        lax.all_gather(expand_weight, ("dp", "sp"), axis=0, tiled=True),
        lax.all_gather(reduce_weight, ("dp", "sp"), axis=0, tiled=True),
    )
    upstream = cotangent[0]
    upstream_full = upstream.astype(jnp.float32)
    reduce_gradient = inner_rows(active_low, upstream)
    reduce_shift_gradient = jnp.sum(upstream_full, axis=0)
    grad_active = inner_cols(upstream, reduce_back)
    grad_before = gelu_pull(grad_active)[0].astype(jnp.bfloat16)
    expand_gradient = inner_rows(second_low, grad_before)
    expand_shift_gradient = jnp.sum(grad_before.astype(jnp.float32), axis=0)
    grad_second = inner_cols(grad_before, expand_back)
    grad_middle_norm, gain_two_gradient, shift_two_gradient = second_pull(grad_second)
    grad_middle = upstream_full + grad_middle_norm
    grad_branch = grad_middle.astype(jnp.bfloat16)
    mixer_gradient = inner_rows(mixed_rows, grad_branch)
    mixer_shift_gradient = jnp.sum(grad_branch.astype(jnp.float32), axis=0)
    grad_mixed = inner_cols(grad_branch, mixer_back).astype(jnp.bfloat16).reshape(row_count, H, HD)
    grad_mixed_full = grad_mixed.astype(jnp.float32)
    grad_unnorm = (grad_mixed_full / totals_rows[:, :, None]).astype(jnp.bfloat16)
    grad_totals = jnp.transpose(-jnp.sum(grad_mixed_full * mixed, axis=-1) / totals_rows)
    own_grads = tile_backward(
        queries[None],
        grad_unnorm[None],
        grad_totals[None],
        key_rows[None],
        value_rows[None],
        visible,
        factor,
    )

    def keys_turn(turn_index, state_in):
        moving_keys, moving_values, key_carry, value_carry, query_sum = state_in
        moving_keys, moving_values = passed_along((moving_keys, moving_values), "sp", 1)
        key_carry, value_carry = (
            passed_along(key_carry.astype(jnp.bfloat16), "sp", 1).astype(key_carry.dtype),
            passed_along(value_carry.astype(jnp.bfloat16), "sp", 1).astype(value_carry.dtype),
        )
        source = (position - turn_index) % members
        later_block = own_low > block_order[2 * source]
        extra_query, extra_key, extra_value = pair_backward(
            later_block, queries, grad_unnorm, grad_totals, moving_keys, moving_values, factor
        )
        return (
            moving_keys,
            moving_values,
            key_carry + extra_key,
            value_carry + extra_value,
            query_sum + extra_query,
        )

    final_back = lax.fori_loop(
        1,
        members,
        keys_turn,
        (key_rows, value_rows, own_grads[1][0], own_grads[2][0], own_grads[0][0]),
    )
    key_sum, value_sum = (
        passed_along(final_back[2].astype(jnp.bfloat16), "sp", 1).astype(jnp.float32),
        passed_along(final_back[3].astype(jnp.bfloat16), "sp", 1).astype(jnp.float32),
    )
    query_sum = final_back[4]
    grad_joint = jnp.concatenate(
        [
            query_sum.reshape(row_count, D),
            key_sum.reshape(row_count, D),
            value_sum.reshape(row_count, D),
        ],
        axis=1,
    ).astype(jnp.bfloat16)
    joint_gradient = inner_rows(normed_low, grad_joint)
    joint_sums = jnp.sum(grad_joint.astype(jnp.float32), axis=0)
    query_shift_gradient = joint_sums[:D]
    value_shift_gradient = joint_sums[2 * D :]
    grad_normed = inner_cols(grad_joint, joint_back)
    grad_rows_norm, gain_one_gradient, shift_one_gradient = first_pull(grad_normed)
    input_gradient = (grad_middle + grad_rows_norm).astype(jnp.bfloat16)
    gradient_sums = (
        lax.psum_scatter(gain_one_gradient, ("dp", "sp"), scatter_dimension=0, tiled=True),
        lax.psum_scatter(shift_one_gradient, ("dp", "sp"), scatter_dimension=0, tiled=True),
        lax.psum_scatter(joint_gradient, ("dp", "sp"), scatter_dimension=0, tiled=True),
        lax.psum_scatter(query_shift_gradient, ("dp", "sp"), scatter_dimension=0, tiled=True),
        lax.psum_scatter(value_shift_gradient, ("dp", "sp"), scatter_dimension=0, tiled=True),
        lax.psum_scatter(mixer_gradient, ("dp", "sp"), scatter_dimension=0, tiled=True),
        lax.psum_scatter(mixer_shift_gradient, ("dp", "sp"), scatter_dimension=0, tiled=True),
        lax.psum_scatter(gain_two_gradient, ("dp", "sp"), scatter_dimension=0, tiled=True),
        lax.psum_scatter(shift_two_gradient, ("dp", "sp"), scatter_dimension=0, tiled=True),
        lax.psum_scatter(expand_gradient, ("dp", "sp"), scatter_dimension=0, tiled=True),
        lax.psum_scatter(expand_shift_gradient, ("dp", "sp"), scatter_dimension=0, tiled=True),
        lax.psum_scatter(reduce_gradient, ("dp", "sp"), scatter_dimension=0, tiled=True),
        lax.psum_scatter(reduce_shift_gradient, ("dp", "sp"), scatter_dimension=0, tiled=True),
    )
    return (result.astype(jnp.bfloat16)[None], input_gradient[None]) + tuple(gradient_sums)


ALL = ("dp", "z", "core")
CHIPS = ("dp", "z")
CORE_BIT = 1
Z_BITS = (0, 2, 4, 6)
X_BIT = 8
Y_BIT = 16
TILE = 512
BLOCK_ROWS = 128


def swapped(value, mask):
    count = lax.axis_size(ALL)
    return lax.ppermute(value, ALL, [(source, source ^ mask) for source in range(count)])


def placed_kernel(slot_ref, *refs, col_blocks):
    pieces, out_ref, sem = refs[:-2], refs[-2], refs[-1]
    width = out_ref.shape[2] // col_blocks
    copies = []
    for piece in pieces:
        for within in range(piece.shape[0]):
            row = slot_ref[len(copies) // col_blocks]
            for col in range(col_blocks):
                if col_blocks == 1:
                    source, target = piece.at[within], out_ref.at[row]
                else:
                    source = piece.at[within, :, pl.ds(col * width, width)]
                    to = pl.multiple_of(slot_ref[16 + col] * width, 128)
                    target = out_ref.at[row, :, pl.ds(to, width)]
                copy = pltpu.make_async_copy(source, target, sem.at[len(copies)])
                copy.start()
                copies.append(copy)
    for copy in copies:
        copy.wait()


def placed(pieces, slots, col_blocks=1):
    rows, cols = pieces[0].shape[1:]
    return pl.pallas_call(
        lambda *refs: placed_kernel(*refs, col_blocks=col_blocks),
        out_shape=jax.ShapeDtypeStruct((16, rows, cols), pieces[0].dtype),
        in_specs=[pl.BlockSpec(memory_space=pltpu.SMEM)]
        + [pl.BlockSpec(memory_space=pl.ANY)] * len(pieces),
        out_specs=pl.BlockSpec(memory_space=pltpu.VMEM),
        scratch_shapes=[pltpu.SemaphoreType.DMA((16 * col_blocks,))],
        name="placed",
    )(slots, *pieces)


def spread_kernel(slot_ref, whole_ref, *refs, groups, col_blocks):
    outs, sem = refs[:-1], refs[-1]
    width = whole_ref.shape[2] // col_blocks
    copies = []
    for out_ref, members in zip(outs, groups):
        for place, at in enumerate(members):
            row = slot_ref[at]
            for col in range(col_blocks):
                if col_blocks == 1:
                    source, target = whole_ref.at[row], out_ref.at[place]
                else:
                    to = pl.multiple_of(slot_ref[16 + col] * width, 128)
                    source = whole_ref.at[row, :, pl.ds(to, width)]
                    target = out_ref.at[place, :, pl.ds(col * width, width)]
                copy = pltpu.make_async_copy(source, target, sem.at[len(copies)])
                copy.start()
                copies.append(copy)
    for copy in copies:
        copy.wait()


def spread(whole, slots, groups, col_blocks=1):
    rows, cols = whole.shape[1:]
    return pl.pallas_call(
        lambda *refs: spread_kernel(*refs, groups=groups, col_blocks=col_blocks),
        out_shape=[jax.ShapeDtypeStruct((len(group), rows, cols), whole.dtype) for group in groups],
        in_specs=[pl.BlockSpec(memory_space=pltpu.SMEM), pl.BlockSpec(memory_space=pl.ANY)],
        out_specs=[pl.BlockSpec(memory_space=pltpu.VMEM)] * len(groups),
        scratch_shapes=[pltpu.SemaphoreType.DMA((16 * col_blocks,))],
        name="spread",
    )(slots, whole)


def collected(line):
    found = {}
    for along in range(4):
        first, second = (X_BIT, Y_BIT) if along < 2 else (Y_BIT, X_BIT)
        found[0, along] = line[along]
        found[first >> 3, along] = swapped(line[along], first)
        found[second >> 3, along] = swapped(line[along], second)
        found[3, along] = swapped(found[first >> 3, along], second)
    return [found[across, along][None] for across in range(4) for along in range(4)]


def collected_small(line):
    stacked = jnp.stack(line)
    beside = swapped(stacked, X_BIT)
    return [stacked, beside, swapped(stacked, Y_BIT), swapped(beside, Y_BIT)]


def summed_along(parts):
    total = parts[0]
    for along in (1, 2, 3):
        total = total + swapped(parts[along].astype(jnp.bfloat16), Z_BITS[along]).astype(jnp.float32)
    return total


def summed(whole, slots, col_blocks):
    low, full = jnp.bfloat16, jnp.float32
    groups = ((0, 1, 4, 5), (8, 9, 12, 13), (2, 3, 10, 11), (6, 7, 14, 15))
    keep_a, send_a, keep_b, send_b = spread(whole, slots, groups, col_blocks)
    got_a = swapped(send_a, Y_BIT)
    got_b = swapped(send_b, X_BIT)
    onward_a = (keep_a[2:].astype(full) + got_a[2:].astype(full)).astype(low)
    onward_b = (keep_b[2:].astype(full) + got_b[2:].astype(full)).astype(low)
    here_a = keep_a[:2].astype(full) + got_a[:2].astype(full)
    here_b = keep_b[:2].astype(full) + got_b[:2].astype(full)
    here_a = here_a + swapped(onward_a, X_BIT).astype(full)
    here_b = here_b + swapped(onward_b, Y_BIT).astype(full)
    return summed_along((here_a[0], here_a[1], here_b[0], here_b[1]))


def summed_small(whole, slots):
    low, full = jnp.bfloat16, jnp.float32
    keep, send = spread(whole, slots, (tuple(range(8)), tuple(range(8, 16))))
    got = swapped(send, Y_BIT)
    onward = (keep[4:].astype(full) + got[4:].astype(full)).astype(low)
    here = keep[:4].astype(full) + got[:4].astype(full)
    return summed_along(here + swapped(onward, X_BIT).astype(full))


def lanes_low(rows):
    return lax.broadcasted_iota(jnp.int32, (rows, 2 * HD), 1) < HD


def head_forward_kernel(place_ref, *refs):
    pieces, sends, (joint_ref, mixed_ref, totals_ref), (acc_ref,) = (
        refs[:4],
        refs[4:8],
        refs[8:11],
        refs[11:],
    )
    wide = 2 * HD
    for at in range(16):
        to = pl.multiple_of(place_ref[at] * BLOCK_ROWS, BLOCK_ROWS)
        joint_ref[pl.ds(to, BLOCK_ROWS), :] = pieces[at // 4][
            (at % 4) * BLOCK_ROWS : (at % 4 + 1) * BLOCK_ROWS, :
        ]
    first = lanes_low(TILE)
    sides = (first, jnp.logical_not(first))
    row_ids = lax.broadcasted_iota(jnp.int32, (TILE, TILE), 0)
    col_ids = lax.broadcasted_iota(jnp.int32, (TILE, TILE), 1)
    causal = col_ids <= row_ids

    def tile_part(queries, key_at, masked):
        key_at = pl.multiple_of(key_at, TILE)
        key_rows = joint_ref[pl.ds(key_at, TILE), wide : 2 * wide]
        value_rows = joint_ref[pl.ds(key_at, TILE), 2 * wide :]
        for side in range(2):
            powers = jnp.exp(inner_cols(queries[side], key_rows))
            if masked:
                powers = jnp.where(causal, powers, 0.0)
            extended = jnp.where(sides[side], value_rows, jnp.ones_like(value_rows))
            acc_ref[side] += product(powers.astype(jnp.bfloat16), extended)

    def query_tile(index, carry):
        query_at = pl.multiple_of(index * TILE, TILE)
        scaled = joint_ref[pl.ds(query_at, TILE), :wide] * jnp.bfloat16(HD**-0.5)
        nothing = jnp.zeros_like(scaled)
        queries = [jnp.where(side, scaled, nothing) for side in sides]
        acc_ref[...] = jnp.zeros_like(acc_ref)

        def key_tile(key_index, inner):
            tile_part(queries, key_index * TILE, False)
            return inner

        lax.fori_loop(0, index, key_tile, 0)
        tile_part(queries, query_at, True)
        low_acc, high_acc = acc_ref[0], acc_ref[1]
        unnorm = jnp.where(first, low_acc, high_acc)
        totals = pltpu.roll(jnp.where(first, high_acc, low_acc), HD, 1)
        totals_ref[pl.ds(query_at, TILE), :] = totals
        mixed_ref[pl.ds(query_at, TILE), :] = unnorm / totals
        return carry

    lax.fori_loop(0, joint_ref.shape[0] // TILE, query_tile, 0)
    for at in range(16):
        to = pl.multiple_of(place_ref[at] * BLOCK_ROWS, BLOCK_ROWS)
        sends[at // 4][(at % 4) * BLOCK_ROWS : (at % 4 + 1) * BLOCK_ROWS, :] = mixed_ref[
            pl.ds(to, BLOCK_ROWS), :
        ].astype(jnp.bfloat16)


def head_forward(pieces, places):
    rows, wide = pieces[0].shape
    total_rows = 4 * rows
    vmem = pl.BlockSpec(memory_space=pltpu.VMEM)
    return pl.pallas_call(
        head_forward_kernel,
        out_shape=[jax.ShapeDtypeStruct((rows, 2 * HD), jnp.bfloat16)] * 4
        + [
            jax.ShapeDtypeStruct((total_rows, wide), jnp.bfloat16),
            jax.ShapeDtypeStruct((total_rows, 2 * HD), jnp.float32),
            jax.ShapeDtypeStruct((total_rows, 2 * HD), jnp.float32),
        ],
        in_specs=[pl.BlockSpec(memory_space=pltpu.SMEM)] + [vmem] * 4,
        out_specs=[vmem] * 7,
        scratch_shapes=[pltpu.VMEM((2, TILE, 2 * HD), jnp.float32)],
        name="head_forward",
    )(places, *pieces)


def head_backward_kernel(place_ref, joint_ref, mixed_ref, totals_ref, *refs):
    pieces, sends, (grad_ref, side_ref, query_ref, key_ref, value_ref, joint_grad) = (
        refs[:4],
        refs[4:8],
        refs[8:],
    )
    wide = 2 * HD
    total_rows = joint_ref.shape[0]
    for at in range(16):
        to = pl.multiple_of(place_ref[at] * BLOCK_ROWS, BLOCK_ROWS)
        grad_ref[pl.ds(to, BLOCK_ROWS), :] = pieces[at // 4][
            (at % 4) * BLOCK_ROWS : (at % 4 + 1) * BLOCK_ROWS, :
        ].astype(jnp.float32)
    first = lanes_low(TILE)
    sides = (first, jnp.logical_not(first))
    lane_ids = lax.broadcasted_iota(jnp.int32, (TILE, wide), 1)
    key_ids = lax.broadcasted_iota(jnp.int32, (TILE, TILE), 0)
    query_ids = lax.broadcasted_iota(jnp.int32, (TILE, TILE), 1)
    causal = key_ids <= query_ids

    def prepare(index, carry):
        at = pl.multiple_of(index * TILE, TILE)
        grad_mixed = grad_ref[pl.ds(at, TILE), :]
        totals = totals_ref[pl.ds(at, TILE), :]
        grad_unnorm = (grad_mixed / totals).astype(jnp.bfloat16).astype(jnp.float32)
        weighed = grad_mixed * mixed_ref[pl.ds(at, TILE), :] / totals
        for side in range(2):
            grad_totals = -jnp.sum(
                jnp.where(sides[side], weighed, 0.0), axis=1, keepdims=True
            )
            coarse = grad_totals.astype(jnp.bfloat16).astype(jnp.float32)
            fine = grad_totals - coarse
            base = (1 - side) * HD
            extra = jnp.where(
                lane_ids == base, coarse, jnp.where(lane_ids == base + 1, fine, 0.0)
            )
            side_ref[side, pl.ds(at, TILE), :] = jnp.where(
                sides[side], grad_unnorm, extra
            ).astype(jnp.bfloat16)
        return carry

    lax.fori_loop(0, total_rows // TILE, prepare, 0)
    query_ref[...] = jnp.zeros_like(query_ref)

    def tile_part(query_at, key_rows, values, masked):
        query_at = pl.multiple_of(query_at, TILE)
        scaled = joint_ref[pl.ds(query_at, TILE), :wide] * jnp.bfloat16(HD**-0.5)
        nothing = jnp.zeros_like(scaled)
        for side in range(2):
            powers = jnp.exp(inner_cols(key_rows, jnp.where(sides[side], scaled, nothing)))
            if masked:
                powers = jnp.where(causal, powers, 0.0)
            upstream = side_ref[side, pl.ds(query_at, TILE), :]
            grad_scores = (powers * inner_cols(values[side], upstream)).astype(jnp.bfloat16)
            value_ref[side] += product(powers.astype(jnp.bfloat16), upstream)
            key_ref[side] += product(grad_scores, scaled)
            query_ref[side, pl.ds(query_at, TILE), :] += inner_rows(grad_scores, key_rows)

    def key_tile(index, carry):
        key_at = pl.multiple_of(index * TILE, TILE)
        key_rows = joint_ref[pl.ds(key_at, TILE), wide : 2 * wide]
        value_rows = joint_ref[pl.ds(key_at, TILE), 2 * wide :]
        values = [jnp.where(side, value_rows, jnp.ones_like(value_rows)) for side in sides]
        key_ref[...] = jnp.zeros_like(key_ref)
        value_ref[...] = jnp.zeros_like(value_ref)
        tile_part(key_at, key_rows, values, True)

        def query_tile(query_index, inner):
            tile_part(query_index * TILE, key_rows, values, False)
            return inner

        lax.fori_loop(index + 1, total_rows // TILE, query_tile, 0)
        joint_grad[pl.ds(key_at, TILE), wide : 2 * wide] = jnp.where(
            first, key_ref[0], key_ref[1]
        ).astype(jnp.bfloat16)
        joint_grad[pl.ds(key_at, TILE), 2 * wide :] = jnp.where(
            first, value_ref[0], value_ref[1]
        ).astype(jnp.bfloat16)
        return carry

    lax.fori_loop(0, total_rows // TILE, key_tile, 0)

    def finish(index, carry):
        at = pl.multiple_of(index * TILE, TILE)
        joint_grad[pl.ds(at, TILE), :wide] = (
            jnp.where(first, query_ref[0, pl.ds(at, TILE), :], query_ref[1, pl.ds(at, TILE), :])
            * HD**-0.5
        ).astype(jnp.bfloat16)
        return carry

    lax.fori_loop(0, total_rows // TILE, finish, 0)
    for at in range(16):
        to = pl.multiple_of(place_ref[at] * BLOCK_ROWS, BLOCK_ROWS)
        sends[at // 4][(at % 4) * BLOCK_ROWS : (at % 4 + 1) * BLOCK_ROWS, :] = joint_grad[
            pl.ds(to, BLOCK_ROWS), :
        ]


def head_backward(joint_sorted, mixed_sorted, totals_sorted, pieces, places):
    rows = pieces[0].shape[0]
    total_rows, wide = joint_sorted.shape
    vmem = pl.BlockSpec(memory_space=pltpu.VMEM)
    return pl.pallas_call(
        head_backward_kernel,
        out_shape=[jax.ShapeDtypeStruct((rows, wide), jnp.bfloat16)] * 4,
        in_specs=[pl.BlockSpec(memory_space=pltpu.SMEM)] + [vmem] * 7,
        out_specs=[vmem] * 4,
        scratch_shapes=[
            pltpu.VMEM((total_rows, 2 * HD), jnp.float32),
            pltpu.VMEM((2, total_rows, 2 * HD), jnp.bfloat16),
            pltpu.VMEM((2, total_rows, 2 * HD), jnp.float32),
            pltpu.VMEM((2, TILE, 2 * HD), jnp.float32),
            pltpu.VMEM((2, TILE, 2 * HD), jnp.float32),
            pltpu.VMEM((total_rows, wide), jnp.bfloat16),
        ],
        name="head_backward",
    )(places, joint_sorted, mixed_sorted, totals_sorted, *pieces)


def norm_parts(values):
    average = jnp.mean(values, axis=-1, keepdims=True)
    centred = values - average
    spread_of = jnp.mean(centred * centred, axis=-1, keepdims=True)
    inverse = lax.rsqrt(spread_of + EPS)
    return centred * inverse, inverse


def norm_pull(grad, scaled, inverse, gain):
    lifted = grad * gain
    return (
        lifted
        - jnp.mean(lifted, axis=-1, keepdims=True)
        - scaled * jnp.mean(lifted * scaled, axis=-1, keepdims=True)
    ) * inverse


def chip_body(
    inputs,
    block_order,
    first_gain,
    first_shift,
    joint_weight,
    query_bias,
    value_bias,
    mixer_weight,
    mixer_bias,
    second_gain,
    second_shift,
    expand_weight,
    expand_bias,
    reduce_weight,
    reduce_bias,
    cotangent,
):
    low, full = jnp.bfloat16, jnp.float32
    group = lax.axis_index("dp")
    core = lax.axis_index("core")
    depth = lax.axis_index("z")
    even = core == 0
    own_rows = inputs.shape[1]
    share = joint_weight.shape[0]

    def own_first(value):
        return jnp.concatenate([value, swapped(value, CORE_BIT)], axis=0)

    def chip_order(mine, theirs):
        return jnp.where(
            even,
            jnp.concatenate([mine, theirs], axis=0),
            jnp.concatenate([theirs, mine], axis=0),
        )

    def cores_exchanged(parts):
        mine = jnp.where(even, parts[0], parts[1])
        theirs = jnp.where(even, parts[1], parts[0])
        return chip_order(mine, swapped(theirs, CORE_BIT))

    chip_ids = jnp.arange(16, dtype=jnp.int32)
    across, along = chip_ids // 4, chip_ids % 4
    slots = (across ^ group) * 4 + (along ^ depth)
    col_slots = jnp.arange(4, dtype=jnp.int32) ^ depth
    joint_slots = jnp.concatenate([slots, col_slots])
    mixer_slots = ((slots // 8) ^ core) * 8 + (((slots // 2) % 4) ^ depth) * 2 + slots % 2
    places = block_order[
        ((chip_ids // 4) ^ depth) * 4 + (((chip_ids // 2) % 2) ^ core) * 2 + chip_ids % 2
    ]

    def line_of(piece):
        return [piece] + [swapped(piece, bits) for bits in Z_BITS[1:]]

    units = expand_weight.shape[1] // 2
    joint_parts = joint_weight.reshape(share, 3, 2, 4, 128).transpose(2, 0, 3, 1, 4).reshape(2, share, 1536)
    joint_line = line_of(cores_exchanged((joint_parts[0], joint_parts[1])))
    joint_full = placed(collected(joint_line), joint_slots, 4).reshape(D, 1536)
    expand_parts = expand_weight.reshape(share, 16, 2, 128)
    expand_own = cores_exchanged(
        (expand_parts[:, :, 0].reshape(share, units), expand_parts[:, :, 1].reshape(share, units))
    )
    hidden_own = jnp.concatenate([expand_own[:, : units // 2], expand_own[:, units // 2 :], reduce_weight])
    hidden_full = lax.all_gather(hidden_own, CHIPS, axis=0, tiled=False)
    expand_full = hidden_full[:, :128].reshape(16, 2, 64, D).transpose(0, 2, 1, 3).reshape(D, units)
    reduce_full = hidden_full[:, 128:].reshape(units, D)

    count = share
    small = jnp.stack(
        [
            jnp.pad(item, (0, 128 - item.shape[0]))
            for item in (
                first_gain,
                first_shift,
                query_bias,
                value_bias,
                mixer_bias,
                second_gain,
                second_shift,
                reduce_bias,
                expand_bias,
            )
        ]
    )
    small, _ = lax.optimization_barrier((small, joint_line[3]))
    small_line = jnp.stack(line_of(chip_order(small[None], swapped(small, CORE_BIT)[None])))
    small_all = jnp.stack(
        [small_line] + [swapped(small_line, bits) for bits in (X_BIT, Y_BIT, X_BIT + Y_BIT)]
    ).reshape(16, -1)
    pick = (slots[None, :] == chip_ids[:, None]).astype(low)
    small_all = product(pick, small_all).reshape(32, 9, 128).transpose(1, 0, 2)
    rows_of = small_all[:8, :, :count].reshape(8, 32 * count)
    (
        gain_one,
        shift_one,
        query_shift,
        value_shift,
        mixer_shift,
        gain_two,
        shift_two,
        reduce_shift,
    ) = [rows_of[at] for at in range(8)]
    expand_shift = small_all[8].reshape(16, 2, 128)
    expand_shift = jnp.where(even, expand_shift[:, 0], expand_shift[:, 1]).reshape(-1)

    mixer_own = cores_exchanged((mixer_weight[:, : D // 2], mixer_weight[:, D // 2 :]))
    mixer_own, joint_full = lax.optimization_barrier((mixer_own, joint_full))
    mixer_cols = placed(collected_small(line_of(mixer_own)), mixer_slots).reshape(2, D // 2, D // 2)
    mixer_mine, mixer_theirs = mixer_cols[0], swapped(mixer_cols[1], CORE_BIT)
    mixer_full = jnp.where(
        even,
        jnp.concatenate([mixer_mine, mixer_theirs], axis=1),
        jnp.concatenate([mixer_theirs, mixer_mine], axis=1),
    )

    token_rows = own_first(inputs[0]).astype(full)
    upstream = own_first(cotangent[0])
    scaled_one, inverse_one = norm_parts(token_rows)
    normed = (scaled_one * gain_one + shift_one).astype(low)
    halves_of = [
        jnp.where(even, item[: D // 2], item[D // 2 :]).reshape(4, 1, 128)
        for item in (query_shift, value_shift)
    ]
    joint_shift = jnp.concatenate([halves_of[0], jnp.zeros_like(halves_of[0]), halves_of[1]], axis=1)
    joint_shift = product(
        (col_slots[:, None] == jnp.arange(4)[None, :]).astype(low), joint_shift.reshape(4, 384).astype(low)
    ).reshape(-1)
    joint_rows = (product(normed, joint_full) + joint_shift).astype(low)
    head_pieces = [joint_rows[:, at * 384 : (at + 1) * 384] for at in range(4)]
    head_pieces = [head_pieces[0]] + [swapped(head_pieces[at], Z_BITS[at]) for at in (1, 2, 3)]
    forward = head_forward(head_pieces, places)
    mixed_out, (joint_sorted, mixed_sorted, totals_sorted) = forward[:4], forward[4:]
    mixed_rows = jnp.concatenate(
        [mixed_out[0]] + [swapped(mixed_out[at], Z_BITS[at]) for at in (1, 2, 3)], axis=1
    )

    def both_cores(part):
        turned = jnp.concatenate([part[own_rows:], part[:own_rows]], axis=0).astype(low)
        return part + swapped(turned, CORE_BIT).astype(full)

    def own_sum(part):
        return part[:own_rows] + swapped(part[own_rows:].astype(low), CORE_BIT).astype(full)

    middle = token_rows + (both_cores(product(mixed_rows, mixer_full)) + mixer_shift)
    scaled_two, inverse_two = norm_parts(middle)
    second = (scaled_two * gain_two + shift_two).astype(low)
    before = product(second, expand_full) + expand_shift
    active, gelu_pull = jax.vjp(gelu_tanh, before)
    active = active.astype(low)
    result = middle[:own_rows] + (own_sum(product(active, reduce_full)) + reduce_shift)

    reduce_gradient = inner_rows(active, upstream).astype(low).reshape(16, 128, D)
    grad_before = gelu_pull(inner_cols(upstream, reduce_full))[0].astype(low)
    expand_gradient = inner_rows(second, grad_before).astype(low)
    expand_gradient = expand_gradient.reshape(16, 64, 2, D).transpose(0, 2, 1, 3).reshape(16, 128, D)
    hidden_gradient = jnp.concatenate([expand_gradient, reduce_gradient], axis=1)
    hidden_sum = lax.psum_scatter(hidden_gradient, CHIPS, scatter_dimension=0, tiled=False)
    reduce_sum = hidden_sum[128:].astype(full)
    expand_sum = jnp.concatenate([hidden_sum[:64], hidden_sum[64:128]], axis=1)
    expand_shift_gradient = jnp.sum(grad_before.astype(full), axis=0)
    grad_second = both_cores(inner_cols(grad_before, expand_full))
    upstream_full = upstream.astype(full)
    grad_middle = upstream_full + norm_pull(grad_second, scaled_two, inverse_two, gain_two)
    grad_branch = grad_middle.astype(low)
    mixer_gradient = inner_rows(mixed_rows, grad_branch).astype(low)
    grad_mixed = inner_cols(grad_branch, mixer_full).astype(low)
    grad_pieces = [grad_mixed[:, at * 128 : (at + 1) * 128] for at in range(4)]
    grad_pieces = [grad_pieces[0]] + [swapped(grad_pieces[at], Z_BITS[at]) for at in (1, 2, 3)]
    mixer_keep = jnp.where(even, mixer_gradient[:, : D // 2], mixer_gradient[:, D // 2 :])
    mixer_send = jnp.where(even, mixer_gradient[:, D // 2 :], mixer_gradient[:, : D // 2])
    mixer_whole = jnp.concatenate([mixer_keep, swapped(mixer_send, CORE_BIT)], axis=0)
    mixer_sum = summed_small(mixer_whole.reshape(16, 64, D // 2), mixer_slots)
    grad_out = head_backward(joint_sorted, mixed_sorted, totals_sorted, grad_pieces, places)
    grad_joint = jnp.concatenate(
        [grad_out[0]] + [swapped(grad_out[at], Z_BITS[at]) for at in (1, 2, 3)], axis=1
    )
    joint_gradient = inner_rows(normed, grad_joint).astype(low).reshape(16, 64, 1536)
    joint_sum = summed(joint_gradient, joint_slots, 4)
    joint_sums = product(
        (col_slots[:, None] == jnp.arange(4)[None, :]).astype(full),
        jnp.sum(grad_joint.astype(full), axis=0).reshape(4, 384),
    ).reshape(4, 3, 128)
    grad_normed = own_sum(inner_cols(grad_joint, joint_full))
    own_scaled = scaled_one[:own_rows]
    input_gradient = (
        grad_middle[:own_rows] + norm_pull(grad_normed, own_scaled, inverse_one[:own_rows], gain_one)
    ).astype(low)

    def one_core(values):
        values = values.reshape(1, -1)
        nothing = jnp.zeros_like(values)
        return jnp.where(
            even, jnp.concatenate([values, nothing]), jnp.concatenate([nothing, values])
        )

    expand_rows = one_core(expand_shift_gradient).reshape(2, 16, 128).transpose(1, 0, 2)
    sums = jnp.concatenate(
        [
            item.reshape(32, -1)
            for item in (
                jnp.sum(grad_normed * own_scaled, axis=0),
                jnp.sum(grad_normed, axis=0),
                one_core(joint_sums[:, 0]),
                one_core(joint_sums[:, 2]),
                jnp.sum(grad_branch[:own_rows].astype(full), axis=0),
                jnp.sum(grad_second[:own_rows] * scaled_two[:own_rows], axis=0),
                jnp.sum(grad_second[:own_rows], axis=0),
                jnp.sum(upstream_full[:own_rows], axis=0),
                expand_rows,
            )
        ],
        axis=1,
    )
    for mask in (CORE_BIT, Z_BITS[1], Z_BITS[2], X_BIT, Y_BIT):
        sums = sums + swapped(sums, mask)
    own_sums = lax.dynamic_slice_in_dim(sums, group * 8 + depth * 2 + core, 1, axis=0)[0]
    vectors = [own_sums[at * count : (at + 1) * count] for at in range(8)] + [own_sums[8 * count :]]

    def finished(total):
        mine = jnp.where(even, total[:share], total[share:])
        theirs = swapped(jnp.where(even, total[share:], total[:share]), CORE_BIT)
        return jnp.where(even, jnp.stack([mine, theirs], axis=0), jnp.stack([theirs, mine], axis=0))

    joint_out = finished(joint_sum).reshape(2, share, 4, 3, 128).transpose(1, 3, 0, 2, 4)
    mixer_out = finished(mixer_sum).transpose(1, 0, 2)
    expand_out = finished(expand_sum).reshape(2, share, 16, 128).transpose(1, 2, 0, 3).astype(full)
    return (
        result.astype(low)[None],
        input_gradient[None],
        vectors[0],
        vectors[1],
        joint_out.reshape(share, 3 * D),
        vectors[2],
        vectors[3],
        mixer_out.reshape(share, D),
        vectors[4],
        vectors[5],
        vectors[6],
        expand_out.reshape(share, 2 * units),
        vectors[8],
        reduce_sum,
        vectors[7],
    )


def solution(mesh):
    dp_size, sp_size = mesh.shape["dp"], mesh.shape["sp"]
    if dp_size == 4 and sp_size == 8:
        mesh = Mesh(mesh.devices.reshape(dp_size, sp_size // 2, 2), ALL)
        body, line = chip_body, ("z", "core")
    else:
        body, line = ring_body, ("sp",)
    rows = P("dp", line, None)
    vector = P(("dp",) + line)
    matrix = P(("dp",) + line, None)
    in_specs = (
        rows,
        P(),
        vector,
        vector,
        matrix,
        vector,
        vector,
        matrix,
        vector,
        vector,
        vector,
        matrix,
        vector,
        matrix,
        vector,
        rows,
    )
    out_specs = (
        rows,
        rows,
        vector,
        vector,
        matrix,
        vector,
        vector,
        matrix,
        vector,
        vector,
        vector,
        matrix,
        vector,
        matrix,
        vector,
    )
    return jax.shard_map(body, mesh=mesh, in_specs=in_specs, out_specs=out_specs, check_vma=False)
```

```python
import jax
import jax.numpy as jnp
from jax import lax
from jax.experimental import pallas as pl
from jax.experimental.pallas import tpu as pltpu
from jax.sharding import Mesh
from jax.sharding import PartitionSpec as P

D = 1024
H = 16
HD = 64


EPS = 1e-05


def passed_along(value, axis, steps):
    count = lax.axis_size(axis)
    pairs = [(source, (source + steps) % count) for source in range(count)]
    return lax.ppermute(value, axis, pairs)


def layer_norm(values, scaling, offset):
    average = jnp.mean(values, axis=-1, keepdims=True)
    centred = values - average
    spread = jnp.mean(centred * centred, axis=-1, keepdims=True)
    return centred * lax.rsqrt(spread + EPS) * scaling + offset


def gelu_tanh(values):
    return jax.nn.gelu(values, approximate=True)


def product(left, right):
    return jnp.dot(left, right, preferred_element_type=jnp.float32)


def inner_rows(left, right):
    return lax.dot_general(
        left, right, (((0,), (0,)), ((), ())), preferred_element_type=jnp.float32
    )


def inner_cols(left, right):
    return lax.dot_general(
        left, right, (((1,), (1,)), ((), ())), preferred_element_type=jnp.float32
    )


def tile_forward(queries, key_rows, value_rows, visible, factor):
    scores = jnp.einsum("tqhd,tkhd->thqk", queries, key_rows, preferred_element_type=jnp.float32)
    powers = jnp.exp(scores * factor)
    if visible is not None:
        powers = jnp.where(visible[:, None], powers, 0.0)
    unnorm = jnp.einsum(
        "thqk,tkhd->tqhd",
        powers.astype(jnp.bfloat16),
        value_rows,
        preferred_element_type=jnp.float32,
    )
    return (unnorm, jnp.sum(powers, axis=-1))


def tile_backward(queries, grad_unnorm, grad_totals, key_rows, value_rows, visible, factor):
    scores = jnp.einsum("tqhd,tkhd->thqk", queries, key_rows, preferred_element_type=jnp.float32)
    powers = jnp.exp(scores * factor)
    if visible is not None:
        powers = jnp.where(visible[:, None], powers, 0.0)
    grad_powers = (
        jnp.einsum("tqhd,tkhd->thqk", grad_unnorm, value_rows, preferred_element_type=jnp.float32)
        + grad_totals[..., None]
    )
    grad_scores = (powers * grad_powers * factor).astype(jnp.bfloat16)
    grad_queries = jnp.einsum(
        "thqk,tkhd->tqhd", grad_scores, key_rows, preferred_element_type=jnp.float32
    )
    grad_keys = jnp.einsum(
        "thqk,tqhd->tkhd", grad_scores, queries, preferred_element_type=jnp.float32
    )
    grad_values = jnp.einsum(
        "thqk,tqhd->tkhd",
        powers.astype(jnp.bfloat16),
        grad_unnorm,
        preferred_element_type=jnp.float32,
    )
    return (grad_queries, grad_keys, grad_values)


def halves(stacked, half_rows, along):
    return (
        lax.slice_in_dim(stacked, 0, half_rows, axis=along),
        lax.slice_in_dim(stacked, half_rows, 2 * half_rows, axis=along),
    )


def query_stack(later_block, stacked, half_rows, along):
    lower_part, upper_part = halves(stacked, half_rows, along)
    return jnp.stack([upper_part, jnp.where(later_block, lower_part, upper_part)])


def key_stack(later_block, stacked, half_rows, along):
    lower_part, upper_part = halves(stacked, half_rows, along)
    return jnp.stack([lower_part, jnp.where(later_block, lower_part, upper_part)])


def query_spread(later_block, tile_pair, along):
    nothing = jnp.zeros_like(tile_pair[0])
    lower_part = jnp.where(later_block, tile_pair[1], nothing)
    upper_part = tile_pair[0] + jnp.where(later_block, nothing, tile_pair[1])
    return jnp.concatenate([lower_part, upper_part], axis=along)


def key_spread(later_block, tile_pair, along):
    nothing = jnp.zeros_like(tile_pair[0])
    lower_part = tile_pair[0] + jnp.where(later_block, tile_pair[1], nothing)
    upper_part = jnp.where(later_block, nothing, tile_pair[1])
    return jnp.concatenate([lower_part, upper_part], axis=along)


def pair_forward(later_block, queries, key_rows, value_rows, factor):
    half_rows = queries.shape[0] // 2
    unnorm, totals = tile_forward(
        query_stack(later_block, queries, half_rows, 0),
        key_stack(later_block, key_rows, half_rows, 0),
        key_stack(later_block, value_rows, half_rows, 0),
        None,
        factor,
    )
    return (query_spread(later_block, unnorm, 0), query_spread(later_block, totals, 1))


def pair_backward(later_block, queries, grad_unnorm, grad_totals, key_rows, value_rows, factor):
    half_rows = queries.shape[0] // 2
    grads = tile_backward(
        query_stack(later_block, queries, half_rows, 0),
        query_stack(later_block, grad_unnorm, half_rows, 0),
        query_stack(later_block, grad_totals, half_rows, 1),
        key_stack(later_block, key_rows, half_rows, 0),
        key_stack(later_block, value_rows, half_rows, 0),
        None,
        factor,
    )
    return (
        query_spread(later_block, grads[0], 0),
        key_spread(later_block, grads[1], 0),
        key_spread(later_block, grads[2], 0),
    )


def ring_body(
    inputs,
    block_order,
    first_gain,
    first_shift,
    joint_weight,
    query_bias,
    value_bias,
    mixer_weight,
    mixer_bias,
    second_gain,
    second_shift,
    expand_weight,
    expand_bias,
    reduce_weight,
    reduce_bias,
    cotangent,
):
    owned_shards = (
        first_gain,
        first_shift,
        joint_weight,
        query_bias,
        value_bias,
        mixer_weight,
        mixer_bias,
        second_gain,
        second_shift,
        expand_weight,
        expand_bias,
        reduce_weight,
        reduce_bias,
    )
    gathered = (
        lax.all_gather(owned_shards[0], ("dp", "sp"), axis=0, tiled=True),
        lax.all_gather(owned_shards[1], ("dp", "sp"), axis=0, tiled=True),
        lax.all_gather(owned_shards[2], ("dp", "sp"), axis=0, tiled=True),
        lax.all_gather(owned_shards[3], ("dp", "sp"), axis=0, tiled=True),
        lax.all_gather(owned_shards[4], ("dp", "sp"), axis=0, tiled=True),
        lax.all_gather(owned_shards[5], ("dp", "sp"), axis=0, tiled=True),
        lax.all_gather(owned_shards[6], ("dp", "sp"), axis=0, tiled=True),
        lax.all_gather(owned_shards[7], ("dp", "sp"), axis=0, tiled=True),
        lax.all_gather(owned_shards[8], ("dp", "sp"), axis=0, tiled=True),
        lax.all_gather(owned_shards[9], ("dp", "sp"), axis=0, tiled=True),
        lax.all_gather(owned_shards[10], ("dp", "sp"), axis=0, tiled=True),
        lax.all_gather(owned_shards[11], ("dp", "sp"), axis=0, tiled=True),
        lax.all_gather(owned_shards[12], ("dp", "sp"), axis=0, tiled=True),
    )
    (
        gain_one,
        shift_one,
        joint_full,
        query_shift,
        value_shift,
        mixer_full,
        mixer_shift,
        gain_two,
        shift_two,
        expand_full,
        expand_shift,
        reduce_full,
        reduce_shift,
    ) = gathered
    factor = HD ** (-0.5)
    members = lax.axis_size("sp")
    position = lax.axis_index("sp")
    token_rows = inputs[0].astype(jnp.float32)
    row_count = token_rows.shape[0]
    half_rows = row_count // 2
    own_low = block_order[2 * position]
    offsets = jnp.arange(half_rows, dtype=jnp.int32)
    own_places = jnp.concatenate(
        [own_low * half_rows + offsets, block_order[2 * position + 1] * half_rows + offsets]
    )
    visible = (own_places[None, :] <= own_places[:, None])[None]
    normed, first_pull = jax.vjp(
        layer_norm, token_rows, gain_one.astype(jnp.float32), shift_one.astype(jnp.float32)
    )
    normed_low = normed.astype(jnp.bfloat16)
    joint_shift = jnp.concatenate([query_shift, jnp.zeros_like(query_shift), value_shift]).astype(
        jnp.float32
    )
    joint_rows = (product(normed_low, joint_full) + joint_shift).astype(jnp.bfloat16)
    queries = joint_rows[:, :D].reshape(row_count, H, HD)
    key_rows = joint_rows[:, D : 2 * D].reshape(row_count, H, HD)
    value_rows = joint_rows[:, 2 * D :].reshape(row_count, H, HD)
    unnorm, totals = tile_forward(queries[None], key_rows[None], value_rows[None], visible, factor)

    def forward_turn(turn_index, state_in):
        moving_keys, moving_values, unnorm_sum, totals_sum = state_in
        moving_keys, moving_values = passed_along((moving_keys, moving_values), "sp", 1)
        source = (position - turn_index) % members
        later_block = own_low > block_order[2 * source]
        extra_unnorm, extra_totals = pair_forward(
            later_block, queries, moving_keys, moving_values, factor
        )
        return (moving_keys, moving_values, unnorm_sum + extra_unnorm, totals_sum + extra_totals)

    final_state = lax.fori_loop(
        1, members, forward_turn, (key_rows, value_rows, unnorm[0], totals[0])
    )
    unnorm = final_state[2]
    totals_rows = jnp.transpose(final_state[3])
    mixed = unnorm / totals_rows[:, :, None]
    mixed_rows = mixed.reshape(row_count, D).astype(jnp.bfloat16)
    middle = token_rows + (product(mixed_rows, mixer_full) + mixer_shift.astype(jnp.float32))
    second, second_pull = jax.vjp(
        layer_norm, middle, gain_two.astype(jnp.float32), shift_two.astype(jnp.float32)
    )
    second_low = second.astype(jnp.bfloat16)
    before = product(second_low, expand_full) + expand_shift.astype(jnp.float32)
    active, gelu_pull = jax.vjp(gelu_tanh, before)
    active_low = active.astype(jnp.bfloat16)
    result = middle + (product(active_low, reduce_full) + reduce_shift.astype(jnp.float32))
    joint_back, mixer_back, expand_back, reduce_back = (
        lax.all_gather(joint_weight, ("dp", "sp"), axis=0, tiled=True),
        lax.all_gather(mixer_weight, ("dp", "sp"), axis=0, tiled=True),
        lax.all_gather(expand_weight, ("dp", "sp"), axis=0, tiled=True),
        lax.all_gather(reduce_weight, ("dp", "sp"), axis=0, tiled=True),
    )
    upstream = cotangent[0]
    upstream_full = upstream.astype(jnp.float32)
    reduce_gradient = inner_rows(active_low, upstream)
    reduce_shift_gradient = jnp.sum(upstream_full, axis=0)
    grad_active = inner_cols(upstream, reduce_back)
    grad_before = gelu_pull(grad_active)[0].astype(jnp.bfloat16)
    expand_gradient = inner_rows(second_low, grad_before)
    expand_shift_gradient = jnp.sum(grad_before.astype(jnp.float32), axis=0)
    grad_second = inner_cols(grad_before, expand_back)
    grad_middle_norm, gain_two_gradient, shift_two_gradient = second_pull(grad_second)
    grad_middle = upstream_full + grad_middle_norm
    grad_branch = grad_middle.astype(jnp.bfloat16)
    mixer_gradient = inner_rows(mixed_rows, grad_branch)
    mixer_shift_gradient = jnp.sum(grad_branch.astype(jnp.float32), axis=0)
    grad_mixed = inner_cols(grad_branch, mixer_back).astype(jnp.bfloat16).reshape(row_count, H, HD)
    grad_mixed_full = grad_mixed.astype(jnp.float32)
    grad_unnorm = (grad_mixed_full / totals_rows[:, :, None]).astype(jnp.bfloat16)
    grad_totals = jnp.transpose(-jnp.sum(grad_mixed_full * mixed, axis=-1) / totals_rows)
    own_grads = tile_backward(
        queries[None],
        grad_unnorm[None],
        grad_totals[None],
        key_rows[None],
        value_rows[None],
        visible,
        factor,
    )

    def keys_turn(turn_index, state_in):
        moving_keys, moving_values, key_carry, value_carry, query_sum = state_in
        moving_keys, moving_values = passed_along((moving_keys, moving_values), "sp", 1)
        key_carry, value_carry = (
            passed_along(key_carry.astype(jnp.bfloat16), "sp", 1).astype(key_carry.dtype),
            passed_along(value_carry.astype(jnp.bfloat16), "sp", 1).astype(value_carry.dtype),
        )
        source = (position - turn_index) % members
        later_block = own_low > block_order[2 * source]
        extra_query, extra_key, extra_value = pair_backward(
            later_block, queries, grad_unnorm, grad_totals, moving_keys, moving_values, factor
        )
        return (
            moving_keys,
            moving_values,
            key_carry + extra_key,
            value_carry + extra_value,
            query_sum + extra_query,
        )

    final_back = lax.fori_loop(
        1,
        members,
        keys_turn,
        (key_rows, value_rows, own_grads[1][0], own_grads[2][0], own_grads[0][0]),
    )
    key_sum, value_sum = (
        passed_along(final_back[2].astype(jnp.bfloat16), "sp", 1).astype(jnp.float32),
        passed_along(final_back[3].astype(jnp.bfloat16), "sp", 1).astype(jnp.float32),
    )
    query_sum = final_back[4]
    grad_joint = jnp.concatenate(
        [
            query_sum.reshape(row_count, D),
            key_sum.reshape(row_count, D),
            value_sum.reshape(row_count, D),
        ],
        axis=1,
    ).astype(jnp.bfloat16)
    joint_gradient = inner_rows(normed_low, grad_joint)
    joint_sums = jnp.sum(grad_joint.astype(jnp.float32), axis=0)
    query_shift_gradient = joint_sums[:D]
    value_shift_gradient = joint_sums[2 * D :]
    grad_normed = inner_cols(grad_joint, joint_back)
    grad_rows_norm, gain_one_gradient, shift_one_gradient = first_pull(grad_normed)
    input_gradient = (grad_middle + grad_rows_norm).astype(jnp.bfloat16)
    gradient_sums = (
        lax.psum_scatter(gain_one_gradient, ("dp", "sp"), scatter_dimension=0, tiled=True),
        lax.psum_scatter(shift_one_gradient, ("dp", "sp"), scatter_dimension=0, tiled=True),
        lax.psum_scatter(joint_gradient, ("dp", "sp"), scatter_dimension=0, tiled=True),
        lax.psum_scatter(query_shift_gradient, ("dp", "sp"), scatter_dimension=0, tiled=True),
        lax.psum_scatter(value_shift_gradient, ("dp", "sp"), scatter_dimension=0, tiled=True),
        lax.psum_scatter(mixer_gradient, ("dp", "sp"), scatter_dimension=0, tiled=True),
        lax.psum_scatter(mixer_shift_gradient, ("dp", "sp"), scatter_dimension=0, tiled=True),
        lax.psum_scatter(gain_two_gradient, ("dp", "sp"), scatter_dimension=0, tiled=True),
        lax.psum_scatter(shift_two_gradient, ("dp", "sp"), scatter_dimension=0, tiled=True),
        lax.psum_scatter(expand_gradient, ("dp", "sp"), scatter_dimension=0, tiled=True),
        lax.psum_scatter(expand_shift_gradient, ("dp", "sp"), scatter_dimension=0, tiled=True),
        lax.psum_scatter(reduce_gradient, ("dp", "sp"), scatter_dimension=0, tiled=True),
        lax.psum_scatter(reduce_shift_gradient, ("dp", "sp"), scatter_dimension=0, tiled=True),
    )
    return (result.astype(jnp.bfloat16)[None], input_gradient[None]) + tuple(gradient_sums)


ALL = ("dp", "z", "core")
CHIPS = ("dp", "z")
CORE_BIT = 1
Z_BITS = (0, 2, 4, 6)
X_BIT = 8
Y_BIT = 16
TILE = 512
BLOCK_ROWS = 128


def swapped(value, mask):
    count = lax.axis_size(ALL)
    return lax.ppermute(value, ALL, [(source, source ^ mask) for source in range(count)])


def moved_kernel(table_ref, *refs, plan, source_count):
    sources, targets, sem = refs[:source_count], refs[source_count:-1], refs[-1]
    copies = []
    for source, source_at, target, target_at in plan:
        copy = pltpu.make_async_copy(
            sources[source].at[source_at(table_ref)],
            targets[target].at[target_at(table_ref)],
            sem.at[len(copies)],
        )
        copy.start()
        copies.append(copy)
    for copy in copies:
        copy.wait()


def moved(table, sources, plan, shapes):
    return pl.pallas_call(
        lambda *refs: moved_kernel(*refs, plan=plan, source_count=len(sources)),
        out_shape=[jax.ShapeDtypeStruct(shape, jnp.bfloat16) for shape in shapes],
        in_specs=[pl.BlockSpec(memory_space=pltpu.SMEM)]
        + [pl.BlockSpec(memory_space=pl.ANY)] * len(sources),
        out_specs=[pl.BlockSpec(memory_space=pltpu.VMEM)] * len(shapes),
        scratch_shapes=[pltpu.SemaphoreType.DMA((len(plan),))],
        name="moved",
    )(table, *sources)


def slot(at):
    return lambda table: (table[at],)


def slot_rows(at, start, count):
    return lambda table: (table[at], pl.ds(start, count))


def slot_part(at, start, count, left, width):
    return lambda table: (table[at], pl.ds(start, count), pl.ds(left, width))


def looked(entry, count, column_at, width):
    return lambda table: (
        entry,
        pl.ds(0, count),
        pl.ds(pl.multiple_of(table[column_at] * width, 128), width),
    )


def fixed(*index):
    return lambda table: index


def line_of(piece):
    return [piece] + [swapped(piece, bits) for bits in Z_BITS[1:]]


def collected(line):
    found = {}
    for along in range(4):
        first, second = (X_BIT, Y_BIT) if along < 2 else (Y_BIT, X_BIT)
        found[0, along] = line[along]
        found[first >> 3, along] = swapped(line[along], first)
        found[second >> 3, along] = swapped(line[along], second)
        found[3, along] = swapped(found[first >> 3, along], second)
    arrays = [found[across, along][None] for across in range(4) for along in range(4)]
    return arrays, [(at, 0) for at in range(16)]


def collected_pairs(line):
    near, far = jnp.stack(line[:2]), jnp.stack(line[2:])
    near_x, far_y = swapped(near, X_BIT), swapped(far, Y_BIT)
    arrays = [
        near,
        near_x,
        swapped(near, Y_BIT),
        swapped(near_x, Y_BIT),
        far,
        swapped(far, X_BIT),
        far_y,
        swapped(far_y, X_BIT),
    ]
    return arrays, [((at % 4 // 2) * 4 + at // 4, at % 2) for at in range(16)]


def collected_small(line):
    stacked = jnp.stack(line)
    beside = swapped(stacked, X_BIT)
    arrays = [stacked, beside, swapped(stacked, Y_BIT), swapped(beside, Y_BIT)]
    return arrays, [(at // 4, at % 4) for at in range(16)]


GROUPS = ((0, 1, 4, 5), (8, 9, 12, 13), (2, 3, 10, 11), (6, 7, 14, 15))
GROUP_OF = {at: (group, place) for group, held in enumerate(GROUPS) for place, at in enumerate(held)}


def summed(grouped):
    low, full = jnp.bfloat16, jnp.float32
    keep_a, send_a, keep_b, send_b = grouped
    got_a = swapped(send_a, Y_BIT)
    got_b = swapped(send_b, X_BIT)
    onward_a = (keep_a[2:].astype(full) + got_a[2:].astype(full)).astype(low)
    onward_b = (keep_b[2:].astype(full) + got_b[2:].astype(full)).astype(low)
    here_a = keep_a[:2].astype(full) + got_a[:2].astype(full)
    here_b = keep_b[:2].astype(full) + got_b[:2].astype(full)
    here_a = here_a + swapped(onward_a, X_BIT).astype(full)
    here_b = here_b + swapped(onward_b, Y_BIT).astype(full)
    total = here_a[0]
    for along, part in ((1, here_a[1]), (2, here_b[0]), (3, here_b[1])):
        total = total + swapped(part.astype(low), Z_BITS[along]).astype(full)
    return total


def lanes_low(rows):
    return lax.broadcasted_iota(jnp.int32, (rows, 2 * HD), 1) < HD


def head_forward_kernel(place_ref, *refs):
    pieces, sends, (joint_ref, mixed_ref, totals_ref), (acc_ref,) = (
        refs[:4],
        refs[4:8],
        refs[8:11],
        refs[11:],
    )
    wide = 2 * HD
    for at in range(16):
        to = pl.multiple_of(place_ref[at] * BLOCK_ROWS, BLOCK_ROWS)
        joint_ref[pl.ds(to, BLOCK_ROWS), :] = pieces[at // 4][
            (at % 4) * BLOCK_ROWS : (at % 4 + 1) * BLOCK_ROWS, :
        ]
    first = lanes_low(TILE)
    sides = (first, jnp.logical_not(first))
    row_ids = lax.broadcasted_iota(jnp.int32, (TILE, TILE), 0)
    col_ids = lax.broadcasted_iota(jnp.int32, (TILE, TILE), 1)
    causal = col_ids <= row_ids

    def tile_part(queries, key_at, masked):
        key_at = pl.multiple_of(key_at, TILE)
        key_rows = joint_ref[pl.ds(key_at, TILE), wide : 2 * wide]
        value_rows = joint_ref[pl.ds(key_at, TILE), 2 * wide :]
        for side in range(2):
            powers = jnp.exp(inner_cols(queries[side], key_rows))
            if masked:
                powers = jnp.where(causal, powers, 0.0)
            extended = jnp.where(sides[side], value_rows, jnp.ones_like(value_rows))
            acc_ref[side] += product(powers.astype(jnp.bfloat16), extended)

    def query_tile(index, carry):
        query_at = pl.multiple_of(index * TILE, TILE)
        scaled = joint_ref[pl.ds(query_at, TILE), :wide] * jnp.bfloat16(HD**-0.5)
        nothing = jnp.zeros_like(scaled)
        queries = [jnp.where(side, scaled, nothing) for side in sides]
        acc_ref[...] = jnp.zeros_like(acc_ref)

        def key_tile(key_index, inner):
            tile_part(queries, key_index * TILE, False)
            return inner

        lax.fori_loop(0, index, key_tile, 0)
        tile_part(queries, query_at, True)
        low_acc, high_acc = acc_ref[0], acc_ref[1]
        unnorm = jnp.where(first, low_acc, high_acc)
        totals = pltpu.roll(jnp.where(first, high_acc, low_acc), HD, 1)
        totals_ref[pl.ds(query_at, TILE), :] = totals
        mixed_ref[pl.ds(query_at, TILE), :] = unnorm / totals
        return carry

    lax.fori_loop(0, joint_ref.shape[0] // TILE, query_tile, 0)
    for at in range(16):
        to = pl.multiple_of(place_ref[at] * BLOCK_ROWS, BLOCK_ROWS)
        sends[at // 4][(at % 4) * BLOCK_ROWS : (at % 4 + 1) * BLOCK_ROWS, :] = mixed_ref[
            pl.ds(to, BLOCK_ROWS), :
        ].astype(jnp.bfloat16)


def head_forward(pieces, places):
    rows, wide = pieces[0].shape
    total_rows = 4 * rows
    vmem = pl.BlockSpec(memory_space=pltpu.VMEM)
    return pl.pallas_call(
        head_forward_kernel,
        out_shape=[jax.ShapeDtypeStruct((rows, 2 * HD), jnp.bfloat16)] * 4
        + [
            jax.ShapeDtypeStruct((total_rows, wide), jnp.bfloat16),
            jax.ShapeDtypeStruct((total_rows, 2 * HD), jnp.float32),
            jax.ShapeDtypeStruct((total_rows, 2 * HD), jnp.float32),
        ],
        in_specs=[pl.BlockSpec(memory_space=pltpu.SMEM)] + [vmem] * 4,
        out_specs=[vmem] * 7,
        scratch_shapes=[pltpu.VMEM((2, TILE, 2 * HD), jnp.float32)],
        name="head_forward",
    )(places, *pieces)


def head_backward_kernel(place_ref, joint_ref, mixed_ref, totals_ref, *refs):
    pieces, sends, (grad_ref, side_ref, query_ref, key_ref, value_ref, joint_grad) = (
        refs[:4],
        refs[4:8],
        refs[8:],
    )
    wide = 2 * HD
    total_rows = joint_ref.shape[0]
    for at in range(16):
        to = pl.multiple_of(place_ref[at] * BLOCK_ROWS, BLOCK_ROWS)
        grad_ref[pl.ds(to, BLOCK_ROWS), :] = pieces[at // 4][
            (at % 4) * BLOCK_ROWS : (at % 4 + 1) * BLOCK_ROWS, :
        ].astype(jnp.float32)
    first = lanes_low(TILE)
    sides = (first, jnp.logical_not(first))
    lane_ids = lax.broadcasted_iota(jnp.int32, (TILE, wide), 1)
    key_ids = lax.broadcasted_iota(jnp.int32, (TILE, TILE), 0)
    query_ids = lax.broadcasted_iota(jnp.int32, (TILE, TILE), 1)
    causal = key_ids <= query_ids

    def prepare(index, carry):
        at = pl.multiple_of(index * TILE, TILE)
        grad_mixed = grad_ref[pl.ds(at, TILE), :]
        totals = totals_ref[pl.ds(at, TILE), :]
        grad_unnorm = (grad_mixed / totals).astype(jnp.bfloat16).astype(jnp.float32)
        weighed = grad_mixed * mixed_ref[pl.ds(at, TILE), :] / totals
        for side in range(2):
            grad_totals = -jnp.sum(
                jnp.where(sides[side], weighed, 0.0), axis=1, keepdims=True
            )
            coarse = grad_totals.astype(jnp.bfloat16).astype(jnp.float32)
            fine = grad_totals - coarse
            base = (1 - side) * HD
            extra = jnp.where(
                lane_ids == base, coarse, jnp.where(lane_ids == base + 1, fine, 0.0)
            )
            side_ref[side, pl.ds(at, TILE), :] = jnp.where(
                sides[side], grad_unnorm, extra
            ).astype(jnp.bfloat16)
        return carry

    lax.fori_loop(0, total_rows // TILE, prepare, 0)
    query_ref[...] = jnp.zeros_like(query_ref)

    def tile_part(query_at, key_rows, values, masked):
        query_at = pl.multiple_of(query_at, TILE)
        scaled = joint_ref[pl.ds(query_at, TILE), :wide] * jnp.bfloat16(HD**-0.5)
        nothing = jnp.zeros_like(scaled)
        for side in range(2):
            powers = jnp.exp(inner_cols(key_rows, jnp.where(sides[side], scaled, nothing)))
            if masked:
                powers = jnp.where(causal, powers, 0.0)
            upstream = side_ref[side, pl.ds(query_at, TILE), :]
            grad_scores = (powers * inner_cols(values[side], upstream)).astype(jnp.bfloat16)
            value_ref[side] += product(powers.astype(jnp.bfloat16), upstream)
            key_ref[side] += product(grad_scores, scaled)
            query_ref[side, pl.ds(query_at, TILE), :] += inner_rows(grad_scores, key_rows)

    def key_tile(index, carry):
        key_at = pl.multiple_of(index * TILE, TILE)
        key_rows = joint_ref[pl.ds(key_at, TILE), wide : 2 * wide]
        value_rows = joint_ref[pl.ds(key_at, TILE), 2 * wide :]
        values = [jnp.where(side, value_rows, jnp.ones_like(value_rows)) for side in sides]
        key_ref[...] = jnp.zeros_like(key_ref)
        value_ref[...] = jnp.zeros_like(value_ref)
        tile_part(key_at, key_rows, values, True)

        def query_tile(query_index, inner):
            tile_part(query_index * TILE, key_rows, values, False)
            return inner

        lax.fori_loop(index + 1, total_rows // TILE, query_tile, 0)
        joint_grad[pl.ds(key_at, TILE), wide : 2 * wide] = jnp.where(
            first, key_ref[0], key_ref[1]
        ).astype(jnp.bfloat16)
        joint_grad[pl.ds(key_at, TILE), 2 * wide :] = jnp.where(
            first, value_ref[0], value_ref[1]
        ).astype(jnp.bfloat16)
        return carry

    lax.fori_loop(0, total_rows // TILE, key_tile, 0)

    def finish(index, carry):
        at = pl.multiple_of(index * TILE, TILE)
        joint_grad[pl.ds(at, TILE), :wide] = (
            jnp.where(first, query_ref[0, pl.ds(at, TILE), :], query_ref[1, pl.ds(at, TILE), :])
            * HD**-0.5
        ).astype(jnp.bfloat16)
        return carry

    lax.fori_loop(0, total_rows // TILE, finish, 0)
    for at in range(16):
        to = pl.multiple_of(place_ref[at] * BLOCK_ROWS, BLOCK_ROWS)
        sends[at // 4][(at % 4) * BLOCK_ROWS : (at % 4 + 1) * BLOCK_ROWS, :] = joint_grad[
            pl.ds(to, BLOCK_ROWS), :
        ]


def head_backward(joint_sorted, mixed_sorted, totals_sorted, pieces, places):
    rows = pieces[0].shape[0]
    total_rows, wide = joint_sorted.shape
    vmem = pl.BlockSpec(memory_space=pltpu.VMEM)
    return pl.pallas_call(
        head_backward_kernel,
        out_shape=[jax.ShapeDtypeStruct((rows, wide), jnp.bfloat16)] * 4,
        in_specs=[pl.BlockSpec(memory_space=pltpu.SMEM)] + [vmem] * 7,
        out_specs=[vmem] * 4,
        scratch_shapes=[
            pltpu.VMEM((total_rows, 2 * HD), jnp.float32),
            pltpu.VMEM((2, total_rows, 2 * HD), jnp.bfloat16),
            pltpu.VMEM((2, total_rows, 2 * HD), jnp.float32),
            pltpu.VMEM((2, TILE, 2 * HD), jnp.float32),
            pltpu.VMEM((2, TILE, 2 * HD), jnp.float32),
            pltpu.VMEM((total_rows, wide), jnp.bfloat16),
        ],
        name="head_backward",
    )(places, joint_sorted, mixed_sorted, totals_sorted, *pieces)


def norm_parts(values):
    average = jnp.mean(values, axis=-1, keepdims=True)
    centred = values - average
    spread_of = jnp.mean(centred * centred, axis=-1, keepdims=True)
    inverse = lax.rsqrt(spread_of + EPS)
    return centred * inverse, inverse


def norm_pull(grad, scaled, inverse, gain):
    lifted = grad * gain
    return (
        lifted
        - jnp.mean(lifted, axis=-1, keepdims=True)
        - scaled * jnp.mean(lifted * scaled, axis=-1, keepdims=True)
    ) * inverse


def chip_body(
    inputs,
    block_order,
    first_gain,
    first_shift,
    joint_weight,
    query_bias,
    value_bias,
    mixer_weight,
    mixer_bias,
    second_gain,
    second_shift,
    expand_weight,
    expand_bias,
    reduce_weight,
    reduce_bias,
    cotangent,
):
    low, full = jnp.bfloat16, jnp.float32
    group = lax.axis_index("dp")
    core = lax.axis_index("core")
    depth = lax.axis_index("z")
    even = core == 0
    own_rows = inputs.shape[1]
    share = joint_weight.shape[0]

    def chip_order(mine, theirs):
        return jnp.where(
            even,
            jnp.concatenate([mine, theirs], axis=0),
            jnp.concatenate([theirs, mine], axis=0),
        )

    def cores_exchanged(parts):
        mine = jnp.where(even, parts[0], parts[1])
        theirs = jnp.where(even, parts[1], parts[0])
        return chip_order(mine, swapped(theirs, CORE_BIT))

    def by_depth(value):
        value = jnp.where(depth % 2 == 0, value, value.reshape((2, 2) + value.shape[1:])[:, ::-1].reshape(value.shape))
        return jnp.where(depth < 2, value, jnp.concatenate([value[2:], value[:2]], axis=0))

    chip_ids = jnp.arange(16, dtype=jnp.int32)
    across, along = chip_ids // 4, chip_ids % 4
    slots = (across ^ group) * 4 + (along ^ depth)
    col_slots = jnp.arange(4, dtype=jnp.int32) ^ depth
    mixer_slots = ((slots // 8) ^ core) * 8 + (((slots // 2) % 4) ^ depth) * 2 + slots % 2
    table = jnp.concatenate([slots, col_slots, mixer_slots])
    places = block_order[
        ((chip_ids // 4) ^ depth) * 4 + (((chip_ids // 2) % 2) ^ core) * 2 + chip_ids % 2
    ]

    tokens = inputs[0]
    pair = jnp.concatenate([tokens, cotangent[0]], axis=0)
    pair_got = swapped(pair, CORE_BIT)

    units = expand_weight.shape[1] // 2
    small = jnp.concatenate(
        [
            jnp.concatenate(
                [
                    first_gain,
                    first_shift,
                    query_bias,
                    value_bias,
                    mixer_bias,
                    second_gain,
                    second_shift,
                    reduce_bias,
                ]
            ),
            expand_bias,
        ]
    ).reshape(1, 384)
    joint_parts = joint_weight.reshape(share, 3, 2, 4, 128).transpose(2, 0, 3, 1, 4).reshape(2, share, 1536)
    small_rows = jnp.pad(small, ((0, 7), (0, 1536 - 384)))
    joint_mine = jnp.where(even, joint_parts[0], joint_parts[1])
    joint_theirs = jnp.where(even, joint_parts[1], joint_parts[0])
    joint_got = swapped(jnp.concatenate([joint_theirs, small_rows]), CORE_BIT)
    small_got = joint_got[share:, :384]
    small_pair = jnp.concatenate(
        [
            jnp.where(even, small_rows[:, :384], small_got),
            jnp.where(even, small_got, small_rows[:, :384]),
            jnp.zeros((8, 768), low),
        ],
        axis=1,
    )
    joint_own = jnp.concatenate([chip_order(joint_mine, joint_got[:share]), small_pair])
    joint_line = line_of(joint_own)
    joint_arrays, joint_at = collected(joint_line)
    joint_plan = []
    for at, (array, entry) in enumerate(joint_at):
        for col in range(4):
            source_at = looked(entry, 64, 16 + col, 384)
            joint_plan.append((array, source_at, col, slot(at)))
            joint_plan.append((array, source_at, 4, slot_part(at, 0, 64, col * 384, 384)))
        joint_plan.append((array, fixed(entry, pl.ds(64, 8), pl.ds(0, 768)), 5, slot(at)))
    joint_done = moved(
        table,
        joint_arrays,
        joint_plan,
        [(16, 64, 384)] * 4 + [(16, 64, 1536), (16, 8, 768)],
    )
    joint_columns = [part.reshape(D, 384) for part in joint_done[:4]]
    joint_full = joint_done[4].reshape(D, 1536)
    small_all = joint_done[5][:, 0].reshape(32, 384)
    count = share
    rows_of = small_all[:, : 8 * count].reshape(32, 8, count).transpose(1, 0, 2).reshape(8, 32 * count)
    (
        gain_one,
        shift_one,
        query_shift,
        value_shift,
        mixer_shift,
        gain_two,
        shift_two,
        reduce_shift,
    ) = [rows_of[at] for at in range(8)]
    expand_shift = small_all[:, 8 * count :].reshape(16, 2, 128)
    expand_shift = jnp.where(even, expand_shift[:, 0], expand_shift[:, 1]).reshape(-1)

    expand_parts = expand_weight.reshape(share, 16, 2, 128)
    expand_own = cores_exchanged(
        (expand_parts[:, :, 0].reshape(share, units), expand_parts[:, :, 1].reshape(share, units))
    )
    mixer_own = cores_exchanged((mixer_weight[:, : D // 2], mixer_weight[:, D // 2 :]))
    hidden_own = jnp.concatenate([expand_own[:, :D], expand_own[:, D:], reduce_weight])
    mixer_own, hidden_own, _ = lax.optimization_barrier((mixer_own, hidden_own, joint_line[1:]))
    mixer_arrays, mixer_at = collected_small(line_of(mixer_own))
    hidden_arrays, hidden_at = collected_pairs(line_of(hidden_own))
    mixer_cols = moved(
        table,
        mixer_arrays,
        [(array, fixed(entry), 0, slot(20 + at)) for at, (array, entry) in enumerate(mixer_at)],
        [(16, 64, D // 2)],
    )[0].reshape(2, D // 2, D // 2)
    mixer_mine, mixer_theirs = mixer_cols[0], swapped(mixer_cols[1], CORE_BIT)
    mixer_full = jnp.where(
        even,
        jnp.concatenate([mixer_mine, mixer_theirs], axis=1),
        jnp.concatenate([mixer_theirs, mixer_mine], axis=1),
    )
    hidden_plan = []
    for at, (array, entry) in enumerate(hidden_at):
        hidden_plan.append((array, fixed(entry, pl.ds(0, 64)), 0, slot_part(at, 0, 64, 0, D)))
        hidden_plan.append((array, fixed(entry, pl.ds(64, 64)), 0, slot_part(at, 0, 64, D, D)))
        hidden_plan.append((array, fixed(entry, pl.ds(128, 128)), 1, slot(at)))
    expand_full, reduce_full = moved(table, hidden_arrays, hidden_plan, [(16, 64, units), (16, 128, D)])
    expand_full, reduce_full = expand_full.reshape(D, units), reduce_full.reshape(units, D)

    token_rows = jnp.concatenate([tokens, pair_got[:own_rows]], axis=0).astype(full)
    upstream = jnp.concatenate([cotangent[0], pair_got[own_rows:]], axis=0)
    scaled_one, inverse_one = norm_parts(token_rows)
    normed = (scaled_one * gain_one + shift_one).astype(low)
    halves_of = [
        jnp.where(even, item[: D // 2], item[D // 2 :]).reshape(4, 1, 128)
        for item in (query_shift, value_shift)
    ]
    joint_shift = by_depth(jnp.concatenate([halves_of[0], jnp.zeros_like(halves_of[0]), halves_of[1]], axis=1))
    joint_shift = joint_shift.reshape(4, 384)
    head_pieces = [(product(normed, joint_columns[at]) + joint_shift[at]).astype(low) for at in range(4)]
    head_pieces = [head_pieces[0]] + [swapped(head_pieces[at], Z_BITS[at]) for at in (1, 2, 3)]
    forward = head_forward(head_pieces, places)
    mixed_out, (joint_sorted, mixed_sorted, totals_sorted) = forward[:4], forward[4:]
    mixed_rows = jnp.concatenate(
        [mixed_out[0]] + [swapped(mixed_out[at], Z_BITS[at]) for at in (1, 2, 3)], axis=1
    )

    def both_cores(part):
        turned = jnp.concatenate([part[own_rows:], part[:own_rows]], axis=0).astype(low)
        return part + swapped(turned, CORE_BIT).astype(full)

    def own_sum(part):
        return part[:own_rows] + swapped(part[own_rows:].astype(low), CORE_BIT).astype(full)

    middle = token_rows + (both_cores(product(mixed_rows, mixer_full)) + mixer_shift)
    scaled_two, inverse_two = norm_parts(middle)
    second = (scaled_two * gain_two + shift_two).astype(low)
    before = product(second, expand_full) + expand_shift
    active, gelu_pull = jax.vjp(gelu_tanh, before)
    active = active.astype(low)
    result = middle[:own_rows] + (own_sum(product(active, reduce_full)) + reduce_shift)

    reduce_gradient = inner_rows(active, upstream).astype(low).reshape(16, 128, D)
    grad_before = gelu_pull(inner_cols(upstream, reduce_full))[0].astype(low)
    expand_gradient = inner_rows(second, grad_before).astype(low).reshape(16, 64, units)
    expand_shift_gradient = jnp.sum(grad_before.astype(full), axis=0)
    grad_second = both_cores(inner_cols(grad_before, expand_full))
    upstream_full = upstream.astype(full)
    grad_middle = upstream_full + norm_pull(grad_second, scaled_two, inverse_two, gain_two)
    grad_branch = grad_middle.astype(low)
    mixer_gradient = inner_rows(mixed_rows, grad_branch).astype(low)
    grad_mixed = inner_cols(grad_branch, mixer_full).astype(low)
    grad_pieces = [grad_mixed[:, at * 128 : (at + 1) * 128] for at in range(4)]
    grad_pieces = [grad_pieces[0]] + [swapped(grad_pieces[at], Z_BITS[at]) for at in (1, 2, 3)]
    mixer_keep = jnp.where(even, mixer_gradient[:, : D // 2], mixer_gradient[:, D // 2 :])
    mixer_send = jnp.where(even, mixer_gradient[:, D // 2 :], mixer_gradient[:, : D // 2])
    mixer_got = swapped(mixer_send, CORE_BIT)
    hidden_plan = []
    for at in range(16):
        to, place = GROUP_OF[at]
        hidden_plan.append((0, slot_part(at, 0, 64, 0, D), to, fixed(place, pl.ds(0, 64))))
        hidden_plan.append((0, slot_part(at, 0, 64, D, D), to, fixed(place, pl.ds(64, 64))))
        hidden_plan.append((1, slot(at), to, fixed(place, pl.ds(128, 128))))
        for half in range(2):
            hidden_plan.append(
                (
                    2,
                    slot_rows(20 + at, half * 32, 32),
                    to,
                    fixed(place, pl.ds(256, 32), pl.ds(half * (D // 2), D // 2)),
                )
            )
    mixer_whole = jnp.concatenate([mixer_keep, mixer_got], axis=0).reshape(16, 64, D // 2)
    hidden_sum = summed(
        moved(table, (expand_gradient, reduce_gradient, mixer_whole), hidden_plan, [(4, 288, D)] * 4)
    )
    grad_out = head_backward(joint_sorted, mixed_sorted, totals_sorted, grad_pieces, places)
    grad_joint = jnp.concatenate(
        [grad_out[0]] + [swapped(grad_out[at], Z_BITS[at]) for at in (1, 2, 3)], axis=1
    )
    joint_gradient = inner_rows(normed, grad_joint).astype(low).reshape(16, 64, 1536)
    grad_normed_part = inner_cols(grad_joint, joint_full)
    joint_sums = by_depth(jnp.sum(grad_joint.astype(full), axis=0).reshape(4, 3, 128))

    def one_core(values):
        values = values.reshape(1, -1)
        nothing = jnp.zeros_like(values)
        return jnp.where(
            even, jnp.concatenate([values, nothing], axis=1), jnp.concatenate([nothing, values], axis=1)
        )[0]

    expand_rows = expand_shift_gradient.reshape(16, 1, 128)
    expand_rows = jnp.where(
        even,
        jnp.concatenate([expand_rows, jnp.zeros_like(expand_rows)], axis=1),
        jnp.concatenate([jnp.zeros_like(expand_rows), expand_rows], axis=1),
    ).reshape(32, 128)
    sums = jnp.stack(
        [
            jnp.sum(grad_normed_part * scaled_one, axis=0),
            jnp.sum(grad_normed_part, axis=0),
            one_core(joint_sums[:, 0]),
            one_core(joint_sums[:, 2]),
            jnp.sum(grad_branch[:own_rows].astype(full), axis=0),
            jnp.sum(grad_second[:own_rows] * scaled_two[:own_rows], axis=0),
            jnp.sum(grad_second[:own_rows], axis=0),
            jnp.sum(upstream_full[:own_rows], axis=0),
        ]
    )
    sums = sums.astype(low).reshape(8, 32, count).transpose(1, 0, 2).reshape(32, 8 * count)
    sums = jnp.concatenate([sums, expand_rows.astype(low)], axis=1).reshape(16, 1, 768)
    sums = jnp.pad(sums, ((0, 0), (0, 7), (0, 0)))
    joint_plan = []
    for at in range(16):
        to, place = GROUP_OF[at]
        for col in range(4):
            left = looked(place, 64, 16 + col, 384)
            joint_plan.append((0, slot_part(at, 0, 64, col * 384, 384), to, left))
        joint_plan.append((1, slot(at), to, fixed(place, pl.ds(64, 8), pl.ds(0, 768))))
    joint_sum = summed(moved(table, (joint_gradient, sums), joint_plan, [(4, 72, 1536)] * 4))
    grad_normed = own_sum(grad_normed_part)
    input_gradient = (
        grad_middle[:own_rows]
        + norm_pull(grad_normed, scaled_one[:own_rows], inverse_one[:own_rows], gain_one)
    ).astype(low)

    def paired(first_core, second_core):
        mine = jnp.where(even, first_core, second_core)
        got = swapped(jnp.where(even, second_core, first_core), CORE_BIT)
        return mine, got

    mixer_mine, mixer_got = paired(hidden_sum[256:, : D // 2], hidden_sum[256:, D // 2 :])
    mixer_out = jnp.where(
        even,
        jnp.concatenate([mixer_mine, mixer_got], axis=1),
        jnp.concatenate([mixer_got, mixer_mine], axis=1),
    )
    expand_pairs = hidden_sum[:128].reshape(2, 2, share, 8, 128)
    expand_mine, expand_got = paired(expand_pairs[:, 0], expand_pairs[:, 1])
    expand_out = jnp.where(
        even, jnp.stack([expand_mine, expand_got], axis=3), jnp.stack([expand_got, expand_mine], axis=3)
    )
    expand_out = expand_out.transpose(1, 0, 2, 3, 4).reshape(share, 2 * units)
    joint_mine = jnp.where(even, joint_sum[:share], joint_sum[share : 2 * share])
    joint_got = swapped(
        jnp.concatenate(
            [jnp.where(even, joint_sum[share : 2 * share], joint_sum[:share]), joint_sum[2 * share :]]
        ),
        CORE_BIT,
    )
    joint_mine_parts = joint_mine.reshape(share, 4, 3, 128)
    joint_got_parts = joint_got[:share].reshape(share, 4, 3, 128)
    joint_out = jnp.where(
        even,
        jnp.stack([joint_mine_parts, joint_got_parts], axis=1),
        jnp.stack([joint_got_parts, joint_mine_parts], axis=1),
    )
    joint_out = joint_out.transpose(0, 3, 1, 2, 4).reshape(share, 3 * D)
    own_sums = joint_sum[2 * share, :768] + joint_got[share, :768]
    own_sums = jnp.where(even, own_sums[:384], own_sums[384:])
    vectors = [own_sums[at * count : (at + 1) * count] for at in range(8)] + [own_sums[8 * count :]]
    return (
        result.astype(low)[None],
        input_gradient[None],
        vectors[0],
        vectors[1],
        joint_out,
        vectors[2],
        vectors[3],
        mixer_out,
        vectors[4],
        vectors[5],
        vectors[6],
        expand_out,
        vectors[8],
        hidden_sum[128:256],
        vectors[7],
    )


def solution(mesh):
    dp_size, sp_size = mesh.shape["dp"], mesh.shape["sp"]
    if dp_size == 4 and sp_size == 8:
        mesh = Mesh(mesh.devices.reshape(dp_size, sp_size // 2, 2), ALL)
        body, line = chip_body, ("z", "core")
    else:
        body, line = ring_body, ("sp",)
    rows = P("dp", line, None)
    vector = P(("dp",) + line)
    matrix = P(("dp",) + line, None)
    in_specs = (
        rows,
        P(),
        vector,
        vector,
        matrix,
        vector,
        vector,
        matrix,
        vector,
        vector,
        vector,
        matrix,
        vector,
        matrix,
        vector,
        rows,
    )
    out_specs = (
        rows,
        rows,
        vector,
        vector,
        matrix,
        vector,
        vector,
        matrix,
        vector,
        vector,
        vector,
        matrix,
        vector,
        matrix,
        vector,
    )
    return jax.shard_map(body, mesh=mesh, in_specs=in_specs, out_specs=out_specs, check_vma=False)
```

```python
import jax
import jax.numpy as jnp
from jax import lax
from jax.experimental import pallas as pl
from jax.experimental.pallas import tpu as pltpu
from jax.sharding import Mesh
from jax.sharding import PartitionSpec as P

D = 1024
H = 16
HD = 64


EPS = 1e-05


def passed_along(value, axis, steps):
    count = lax.axis_size(axis)
    pairs = [(source, (source + steps) % count) for source in range(count)]
    return lax.ppermute(value, axis, pairs)


def layer_norm(values, scaling, offset):
    average = jnp.mean(values, axis=-1, keepdims=True)
    centred = values - average
    spread = jnp.mean(centred * centred, axis=-1, keepdims=True)
    return centred * lax.rsqrt(spread + EPS) * scaling + offset


def gelu_tanh(values):
    return jax.nn.gelu(values, approximate=True)


def product(left, right):
    return jnp.dot(left, right, preferred_element_type=jnp.float32)


def inner_rows(left, right):
    return lax.dot_general(
        left, right, (((0,), (0,)), ((), ())), preferred_element_type=jnp.float32
    )


def inner_cols(left, right):
    return lax.dot_general(
        left, right, (((1,), (1,)), ((), ())), preferred_element_type=jnp.float32
    )


def tile_forward(queries, key_rows, value_rows, visible, factor):
    scores = jnp.einsum("tqhd,tkhd->thqk", queries, key_rows, preferred_element_type=jnp.float32)
    powers = jnp.exp(scores * factor)
    if visible is not None:
        powers = jnp.where(visible[:, None], powers, 0.0)
    unnorm = jnp.einsum(
        "thqk,tkhd->tqhd",
        powers.astype(jnp.bfloat16),
        value_rows,
        preferred_element_type=jnp.float32,
    )
    return (unnorm, jnp.sum(powers, axis=-1))


def tile_backward(queries, grad_unnorm, grad_totals, key_rows, value_rows, visible, factor):
    scores = jnp.einsum("tqhd,tkhd->thqk", queries, key_rows, preferred_element_type=jnp.float32)
    powers = jnp.exp(scores * factor)
    if visible is not None:
        powers = jnp.where(visible[:, None], powers, 0.0)
    grad_powers = (
        jnp.einsum("tqhd,tkhd->thqk", grad_unnorm, value_rows, preferred_element_type=jnp.float32)
        + grad_totals[..., None]
    )
    grad_scores = (powers * grad_powers * factor).astype(jnp.bfloat16)
    grad_queries = jnp.einsum(
        "thqk,tkhd->tqhd", grad_scores, key_rows, preferred_element_type=jnp.float32
    )
    grad_keys = jnp.einsum(
        "thqk,tqhd->tkhd", grad_scores, queries, preferred_element_type=jnp.float32
    )
    grad_values = jnp.einsum(
        "thqk,tqhd->tkhd",
        powers.astype(jnp.bfloat16),
        grad_unnorm,
        preferred_element_type=jnp.float32,
    )
    return (grad_queries, grad_keys, grad_values)


def halves(stacked, half_rows, along):
    return (
        lax.slice_in_dim(stacked, 0, half_rows, axis=along),
        lax.slice_in_dim(stacked, half_rows, 2 * half_rows, axis=along),
    )


def query_stack(later_block, stacked, half_rows, along):
    lower_part, upper_part = halves(stacked, half_rows, along)
    return jnp.stack([upper_part, jnp.where(later_block, lower_part, upper_part)])


def key_stack(later_block, stacked, half_rows, along):
    lower_part, upper_part = halves(stacked, half_rows, along)
    return jnp.stack([lower_part, jnp.where(later_block, lower_part, upper_part)])


def query_spread(later_block, tile_pair, along):
    nothing = jnp.zeros_like(tile_pair[0])
    lower_part = jnp.where(later_block, tile_pair[1], nothing)
    upper_part = tile_pair[0] + jnp.where(later_block, nothing, tile_pair[1])
    return jnp.concatenate([lower_part, upper_part], axis=along)


def key_spread(later_block, tile_pair, along):
    nothing = jnp.zeros_like(tile_pair[0])
    lower_part = tile_pair[0] + jnp.where(later_block, tile_pair[1], nothing)
    upper_part = jnp.where(later_block, nothing, tile_pair[1])
    return jnp.concatenate([lower_part, upper_part], axis=along)


def pair_forward(later_block, queries, key_rows, value_rows, factor):
    half_rows = queries.shape[0] // 2
    unnorm, totals = tile_forward(
        query_stack(later_block, queries, half_rows, 0),
        key_stack(later_block, key_rows, half_rows, 0),
        key_stack(later_block, value_rows, half_rows, 0),
        None,
        factor,
    )
    return (query_spread(later_block, unnorm, 0), query_spread(later_block, totals, 1))


def pair_backward(later_block, queries, grad_unnorm, grad_totals, key_rows, value_rows, factor):
    half_rows = queries.shape[0] // 2
    grads = tile_backward(
        query_stack(later_block, queries, half_rows, 0),
        query_stack(later_block, grad_unnorm, half_rows, 0),
        query_stack(later_block, grad_totals, half_rows, 1),
        key_stack(later_block, key_rows, half_rows, 0),
        key_stack(later_block, value_rows, half_rows, 0),
        None,
        factor,
    )
    return (
        query_spread(later_block, grads[0], 0),
        key_spread(later_block, grads[1], 0),
        key_spread(later_block, grads[2], 0),
    )


def ring_body(
    inputs,
    block_order,
    first_gain,
    first_shift,
    joint_weight,
    query_bias,
    value_bias,
    mixer_weight,
    mixer_bias,
    second_gain,
    second_shift,
    expand_weight,
    expand_bias,
    reduce_weight,
    reduce_bias,
    cotangent,
):
    owned_shards = (
        first_gain,
        first_shift,
        joint_weight,
        query_bias,
        value_bias,
        mixer_weight,
        mixer_bias,
        second_gain,
        second_shift,
        expand_weight,
        expand_bias,
        reduce_weight,
        reduce_bias,
    )
    gathered = (
        lax.all_gather(owned_shards[0], ("dp", "sp"), axis=0, tiled=True),
        lax.all_gather(owned_shards[1], ("dp", "sp"), axis=0, tiled=True),
        lax.all_gather(owned_shards[2], ("dp", "sp"), axis=0, tiled=True),
        lax.all_gather(owned_shards[3], ("dp", "sp"), axis=0, tiled=True),
        lax.all_gather(owned_shards[4], ("dp", "sp"), axis=0, tiled=True),
        lax.all_gather(owned_shards[5], ("dp", "sp"), axis=0, tiled=True),
        lax.all_gather(owned_shards[6], ("dp", "sp"), axis=0, tiled=True),
        lax.all_gather(owned_shards[7], ("dp", "sp"), axis=0, tiled=True),
        lax.all_gather(owned_shards[8], ("dp", "sp"), axis=0, tiled=True),
        lax.all_gather(owned_shards[9], ("dp", "sp"), axis=0, tiled=True),
        lax.all_gather(owned_shards[10], ("dp", "sp"), axis=0, tiled=True),
        lax.all_gather(owned_shards[11], ("dp", "sp"), axis=0, tiled=True),
        lax.all_gather(owned_shards[12], ("dp", "sp"), axis=0, tiled=True),
    )
    (
        gain_one,
        shift_one,
        joint_full,
        query_shift,
        value_shift,
        mixer_full,
        mixer_shift,
        gain_two,
        shift_two,
        expand_full,
        expand_shift,
        reduce_full,
        reduce_shift,
    ) = gathered
    factor = HD ** (-0.5)
    members = lax.axis_size("sp")
    position = lax.axis_index("sp")
    token_rows = inputs[0].astype(jnp.float32)
    row_count = token_rows.shape[0]
    half_rows = row_count // 2
    own_low = block_order[2 * position]
    offsets = jnp.arange(half_rows, dtype=jnp.int32)
    own_places = jnp.concatenate(
        [own_low * half_rows + offsets, block_order[2 * position + 1] * half_rows + offsets]
    )
    visible = (own_places[None, :] <= own_places[:, None])[None]
    normed, first_pull = jax.vjp(
        layer_norm, token_rows, gain_one.astype(jnp.float32), shift_one.astype(jnp.float32)
    )
    normed_low = normed.astype(jnp.bfloat16)
    joint_shift = jnp.concatenate([query_shift, jnp.zeros_like(query_shift), value_shift]).astype(
        jnp.float32
    )
    joint_rows = (product(normed_low, joint_full) + joint_shift).astype(jnp.bfloat16)
    queries = joint_rows[:, :D].reshape(row_count, H, HD)
    key_rows = joint_rows[:, D : 2 * D].reshape(row_count, H, HD)
    value_rows = joint_rows[:, 2 * D :].reshape(row_count, H, HD)
    unnorm, totals = tile_forward(queries[None], key_rows[None], value_rows[None], visible, factor)

    def forward_turn(turn_index, state_in):
        moving_keys, moving_values, unnorm_sum, totals_sum = state_in
        moving_keys, moving_values = passed_along((moving_keys, moving_values), "sp", 1)
        source = (position - turn_index) % members
        later_block = own_low > block_order[2 * source]
        extra_unnorm, extra_totals = pair_forward(
            later_block, queries, moving_keys, moving_values, factor
        )
        return (moving_keys, moving_values, unnorm_sum + extra_unnorm, totals_sum + extra_totals)

    final_state = lax.fori_loop(
        1, members, forward_turn, (key_rows, value_rows, unnorm[0], totals[0])
    )
    unnorm = final_state[2]
    totals_rows = jnp.transpose(final_state[3])
    mixed = unnorm / totals_rows[:, :, None]
    mixed_rows = mixed.reshape(row_count, D).astype(jnp.bfloat16)
    middle = token_rows + (product(mixed_rows, mixer_full) + mixer_shift.astype(jnp.float32))
    second, second_pull = jax.vjp(
        layer_norm, middle, gain_two.astype(jnp.float32), shift_two.astype(jnp.float32)
    )
    second_low = second.astype(jnp.bfloat16)
    before = product(second_low, expand_full) + expand_shift.astype(jnp.float32)
    active, gelu_pull = jax.vjp(gelu_tanh, before)
    active_low = active.astype(jnp.bfloat16)
    result = middle + (product(active_low, reduce_full) + reduce_shift.astype(jnp.float32))
    joint_back, mixer_back, expand_back, reduce_back = (
        lax.all_gather(joint_weight, ("dp", "sp"), axis=0, tiled=True),
        lax.all_gather(mixer_weight, ("dp", "sp"), axis=0, tiled=True),
        lax.all_gather(expand_weight, ("dp", "sp"), axis=0, tiled=True),
        lax.all_gather(reduce_weight, ("dp", "sp"), axis=0, tiled=True),
    )
    upstream = cotangent[0]
    upstream_full = upstream.astype(jnp.float32)
    reduce_gradient = inner_rows(active_low, upstream)
    reduce_shift_gradient = jnp.sum(upstream_full, axis=0)
    grad_active = inner_cols(upstream, reduce_back)
    grad_before = gelu_pull(grad_active)[0].astype(jnp.bfloat16)
    expand_gradient = inner_rows(second_low, grad_before)
    expand_shift_gradient = jnp.sum(grad_before.astype(jnp.float32), axis=0)
    grad_second = inner_cols(grad_before, expand_back)
    grad_middle_norm, gain_two_gradient, shift_two_gradient = second_pull(grad_second)
    grad_middle = upstream_full + grad_middle_norm
    grad_branch = grad_middle.astype(jnp.bfloat16)
    mixer_gradient = inner_rows(mixed_rows, grad_branch)
    mixer_shift_gradient = jnp.sum(grad_branch.astype(jnp.float32), axis=0)
    grad_mixed = inner_cols(grad_branch, mixer_back).astype(jnp.bfloat16).reshape(row_count, H, HD)
    grad_mixed_full = grad_mixed.astype(jnp.float32)
    grad_unnorm = (grad_mixed_full / totals_rows[:, :, None]).astype(jnp.bfloat16)
    grad_totals = jnp.transpose(-jnp.sum(grad_mixed_full * mixed, axis=-1) / totals_rows)
    own_grads = tile_backward(
        queries[None],
        grad_unnorm[None],
        grad_totals[None],
        key_rows[None],
        value_rows[None],
        visible,
        factor,
    )

    def keys_turn(turn_index, state_in):
        moving_keys, moving_values, key_carry, value_carry, query_sum = state_in
        moving_keys, moving_values = passed_along((moving_keys, moving_values), "sp", 1)
        key_carry, value_carry = (
            passed_along(key_carry.astype(jnp.bfloat16), "sp", 1).astype(key_carry.dtype),
            passed_along(value_carry.astype(jnp.bfloat16), "sp", 1).astype(value_carry.dtype),
        )
        source = (position - turn_index) % members
        later_block = own_low > block_order[2 * source]
        extra_query, extra_key, extra_value = pair_backward(
            later_block, queries, grad_unnorm, grad_totals, moving_keys, moving_values, factor
        )
        return (
            moving_keys,
            moving_values,
            key_carry + extra_key,
            value_carry + extra_value,
            query_sum + extra_query,
        )

    final_back = lax.fori_loop(
        1,
        members,
        keys_turn,
        (key_rows, value_rows, own_grads[1][0], own_grads[2][0], own_grads[0][0]),
    )
    key_sum, value_sum = (
        passed_along(final_back[2].astype(jnp.bfloat16), "sp", 1).astype(jnp.float32),
        passed_along(final_back[3].astype(jnp.bfloat16), "sp", 1).astype(jnp.float32),
    )
    query_sum = final_back[4]
    grad_joint = jnp.concatenate(
        [
            query_sum.reshape(row_count, D),
            key_sum.reshape(row_count, D),
            value_sum.reshape(row_count, D),
        ],
        axis=1,
    ).astype(jnp.bfloat16)
    joint_gradient = inner_rows(normed_low, grad_joint)
    joint_sums = jnp.sum(grad_joint.astype(jnp.float32), axis=0)
    query_shift_gradient = joint_sums[:D]
    value_shift_gradient = joint_sums[2 * D :]
    grad_normed = inner_cols(grad_joint, joint_back)
    grad_rows_norm, gain_one_gradient, shift_one_gradient = first_pull(grad_normed)
    input_gradient = (grad_middle + grad_rows_norm).astype(jnp.bfloat16)
    gradient_sums = (
        lax.psum_scatter(gain_one_gradient, ("dp", "sp"), scatter_dimension=0, tiled=True),
        lax.psum_scatter(shift_one_gradient, ("dp", "sp"), scatter_dimension=0, tiled=True),
        lax.psum_scatter(joint_gradient, ("dp", "sp"), scatter_dimension=0, tiled=True),
        lax.psum_scatter(query_shift_gradient, ("dp", "sp"), scatter_dimension=0, tiled=True),
        lax.psum_scatter(value_shift_gradient, ("dp", "sp"), scatter_dimension=0, tiled=True),
        lax.psum_scatter(mixer_gradient, ("dp", "sp"), scatter_dimension=0, tiled=True),
        lax.psum_scatter(mixer_shift_gradient, ("dp", "sp"), scatter_dimension=0, tiled=True),
        lax.psum_scatter(gain_two_gradient, ("dp", "sp"), scatter_dimension=0, tiled=True),
        lax.psum_scatter(shift_two_gradient, ("dp", "sp"), scatter_dimension=0, tiled=True),
        lax.psum_scatter(expand_gradient, ("dp", "sp"), scatter_dimension=0, tiled=True),
        lax.psum_scatter(expand_shift_gradient, ("dp", "sp"), scatter_dimension=0, tiled=True),
        lax.psum_scatter(reduce_gradient, ("dp", "sp"), scatter_dimension=0, tiled=True),
        lax.psum_scatter(reduce_shift_gradient, ("dp", "sp"), scatter_dimension=0, tiled=True),
    )
    return (result.astype(jnp.bfloat16)[None], input_gradient[None]) + tuple(gradient_sums)


ALL = ("dp", "z", "core")
CHIPS = ("dp", "z")
CORE_BIT = 1
Z_BITS = (0, 2, 4, 6)
X_BIT = 8
Y_BIT = 16
TILE = 512
BLOCK_ROWS = 128


def swapped(value, mask):
    count = lax.axis_size(ALL)
    return lax.ppermute(value, ALL, [(source, source ^ mask) for source in range(count)])


def moved_kernel(table_ref, *refs, plan, source_count):
    sources, targets, sem = refs[:source_count], refs[source_count:-1], refs[-1]
    copies = []
    for source, source_at, target, target_at in plan:
        copy = pltpu.make_async_copy(
            sources[source].at[source_at(table_ref)],
            targets[target].at[target_at(table_ref)],
            sem.at[len(copies)],
        )
        copy.start()
        copies.append(copy)
    for copy in copies:
        copy.wait()


def moved(table, sources, plan, shapes):
    return pl.pallas_call(
        lambda *refs: moved_kernel(*refs, plan=plan, source_count=len(sources)),
        out_shape=[jax.ShapeDtypeStruct(shape, jnp.bfloat16) for shape in shapes],
        in_specs=[pl.BlockSpec(memory_space=pltpu.SMEM)]
        + [pl.BlockSpec(memory_space=pl.ANY)] * len(sources),
        out_specs=[pl.BlockSpec(memory_space=pltpu.VMEM)] * len(shapes),
        scratch_shapes=[pltpu.SemaphoreType.DMA((len(plan),))],
        name="moved",
    )(table, *sources)


def slot(at):
    return lambda table: (table[at],)


def slot_rows(at, start, count):
    return lambda table: (table[at], pl.ds(start, count))


def slot_part(at, start, count, left, width):
    return lambda table: (table[at], pl.ds(start, count), pl.ds(left, width))


def looked(entry, count, column_at, width):
    return lambda table: (
        entry,
        pl.ds(0, count),
        pl.ds(pl.multiple_of(table[column_at] * width, 128), width),
    )


def fixed(*index):
    return lambda table: index


def after(value, *others):
    return lax.optimization_barrier((value, others))[0]


def line_of(piece):
    return [piece] + [swapped(piece, bits) for bits in Z_BITS[1:]]


def collected(line):
    stacked = jnp.stack(line)
    beside, above = swapped(stacked, X_BIT), swapped(stacked, Y_BIT)
    arrays = [stacked, beside, above, swapped(beside[:2], Y_BIT), swapped(above[2:], X_BIT)]
    held = [(at // 4, at % 4) for at in range(12)] + [(3, 0), (3, 1), (4, 0), (4, 1)]
    return arrays, held


def collected_small(line):
    stacked = jnp.stack(line)
    beside = swapped(stacked, X_BIT)
    arrays = [stacked, beside, swapped(stacked, Y_BIT), swapped(beside, Y_BIT)]
    return arrays, [(at // 4, at % 4) for at in range(16)]


GROUPS = ((0, 1, 4, 5), (8, 9, 12, 13), (2, 3, 10, 11), (6, 7, 14, 15))
GROUP_OF = {at: (group, place) for group, held in enumerate(GROUPS) for place, at in enumerate(held)}


def summed_first(grouped):
    low, full = jnp.bfloat16, jnp.float32
    keep_a, send_a, keep_b, send_b = grouped
    got_a = swapped(send_a, Y_BIT)
    got_b = swapped(send_b, X_BIT)
    onward_a = (keep_a[2:].astype(full) + got_a[2:].astype(full)).astype(low)
    onward_b = (keep_b[2:].astype(full) + got_b[2:].astype(full)).astype(low)
    here_a = keep_a[:2].astype(full) + got_a[:2].astype(full)
    here_b = keep_b[:2].astype(full) + got_b[:2].astype(full)
    return onward_a, onward_b, here_a, here_b


def summed_second(state):
    low, full = jnp.bfloat16, jnp.float32
    onward_a, onward_b, here_a, here_b = state
    here_a = here_a + swapped(onward_a, X_BIT).astype(full)
    here_b = here_b + swapped(onward_b, Y_BIT).astype(full)
    return here_a[0], here_a[1].astype(low), here_b[0].astype(low), here_b[1].astype(low)


def summed_third(state, *others):
    got = [swapped(state[along], Z_BITS[along]) for along in (1, 2, 3)]
    if others:
        got = after(got, *others)
    total = state[0]
    for piece in got:
        total = total + piece.astype(jnp.float32)
    return total


def lanes_low(rows):
    return lax.broadcasted_iota(jnp.int32, (rows, 2 * HD), 1) < HD


def head_forward_kernel(place_ref, *refs):
    pieces, sends, (joint_ref, mixed_ref, totals_ref), (acc_ref,) = (
        refs[:4],
        refs[4:8],
        refs[8:11],
        refs[11:],
    )
    wide = 2 * HD
    for at in range(16):
        to = pl.multiple_of(place_ref[at] * BLOCK_ROWS, BLOCK_ROWS)
        joint_ref[pl.ds(to, BLOCK_ROWS), :] = pieces[at // 4][
            (at % 4) * BLOCK_ROWS : (at % 4 + 1) * BLOCK_ROWS, :
        ]
    first = lanes_low(TILE)
    sides = (first, jnp.logical_not(first))
    row_ids = lax.broadcasted_iota(jnp.int32, (TILE, TILE), 0)
    col_ids = lax.broadcasted_iota(jnp.int32, (TILE, TILE), 1)
    causal = col_ids <= row_ids

    def tile_part(queries, key_at, masked):
        key_at = pl.multiple_of(key_at, TILE)
        key_rows = joint_ref[pl.ds(key_at, TILE), wide : 2 * wide]
        value_rows = joint_ref[pl.ds(key_at, TILE), 2 * wide :]
        for side in range(2):
            powers = jnp.exp(inner_cols(queries[side], key_rows))
            if masked:
                powers = jnp.where(causal, powers, 0.0)
            extended = jnp.where(sides[side], value_rows, jnp.ones_like(value_rows))
            acc_ref[side] += product(powers.astype(jnp.bfloat16), extended)

    def query_tile(index, carry):
        query_at = pl.multiple_of(index * TILE, TILE)
        scaled = joint_ref[pl.ds(query_at, TILE), :wide] * jnp.bfloat16(HD**-0.5)
        nothing = jnp.zeros_like(scaled)
        queries = [jnp.where(side, scaled, nothing) for side in sides]
        acc_ref[...] = jnp.zeros_like(acc_ref)

        def key_tile(key_index, inner):
            tile_part(queries, key_index * TILE, False)
            return inner

        lax.fori_loop(0, index, key_tile, 0)
        tile_part(queries, query_at, True)
        low_acc, high_acc = acc_ref[0], acc_ref[1]
        unnorm = jnp.where(first, low_acc, high_acc)
        totals = pltpu.roll(jnp.where(first, high_acc, low_acc), HD, 1)
        totals_ref[pl.ds(query_at, TILE), :] = totals
        mixed_ref[pl.ds(query_at, TILE), :] = unnorm / totals
        return carry

    lax.fori_loop(0, joint_ref.shape[0] // TILE, query_tile, 0)
    for at in range(16):
        to = pl.multiple_of(place_ref[at] * BLOCK_ROWS, BLOCK_ROWS)
        sends[at // 4][(at % 4) * BLOCK_ROWS : (at % 4 + 1) * BLOCK_ROWS, :] = mixed_ref[
            pl.ds(to, BLOCK_ROWS), :
        ].astype(jnp.bfloat16)


def head_forward(pieces, places):
    rows, wide = pieces[0].shape
    total_rows = 4 * rows
    vmem = pl.BlockSpec(memory_space=pltpu.VMEM)
    return pl.pallas_call(
        head_forward_kernel,
        out_shape=[jax.ShapeDtypeStruct((rows, 2 * HD), jnp.bfloat16)] * 4
        + [
            jax.ShapeDtypeStruct((total_rows, wide), jnp.bfloat16),
            jax.ShapeDtypeStruct((total_rows, 2 * HD), jnp.float32),
            jax.ShapeDtypeStruct((total_rows, 2 * HD), jnp.float32),
        ],
        in_specs=[pl.BlockSpec(memory_space=pltpu.SMEM)] + [vmem] * 4,
        out_specs=[vmem] * 7,
        scratch_shapes=[pltpu.VMEM((2, TILE, 2 * HD), jnp.float32)],
        cost_estimate=pl.CostEstimate(
            flops=12 * total_rows * total_rows * 2 * HD,
            bytes_accessed=8 * total_rows * wide,
            transcendentals=2 * total_rows * total_rows,
        ),
        name="head_forward",
    )(places, *pieces)


def head_backward_kernel(place_ref, joint_ref, mixed_ref, totals_ref, *refs):
    pieces, sends, (grad_ref, side_ref, query_ref, key_ref, value_ref, joint_grad) = (
        refs[:4],
        refs[4:8],
        refs[8:],
    )
    wide = 2 * HD
    total_rows = joint_ref.shape[0]
    for at in range(16):
        to = pl.multiple_of(place_ref[at] * BLOCK_ROWS, BLOCK_ROWS)
        grad_ref[pl.ds(to, BLOCK_ROWS), :] = pieces[at // 4][
            (at % 4) * BLOCK_ROWS : (at % 4 + 1) * BLOCK_ROWS, :
        ].astype(jnp.float32)
    first = lanes_low(TILE)
    sides = (first, jnp.logical_not(first))
    lane_ids = lax.broadcasted_iota(jnp.int32, (TILE, wide), 1)
    key_ids = lax.broadcasted_iota(jnp.int32, (TILE, TILE), 0)
    query_ids = lax.broadcasted_iota(jnp.int32, (TILE, TILE), 1)
    causal = key_ids <= query_ids

    def prepare(index, carry):
        at = pl.multiple_of(index * TILE, TILE)
        grad_mixed = grad_ref[pl.ds(at, TILE), :]
        totals = totals_ref[pl.ds(at, TILE), :]
        grad_unnorm = (grad_mixed / totals).astype(jnp.bfloat16).astype(jnp.float32)
        weighed = grad_mixed * mixed_ref[pl.ds(at, TILE), :] / totals
        for side in range(2):
            grad_totals = -jnp.sum(
                jnp.where(sides[side], weighed, 0.0), axis=1, keepdims=True
            )
            coarse = grad_totals.astype(jnp.bfloat16).astype(jnp.float32)
            fine = grad_totals - coarse
            base = (1 - side) * HD
            extra = jnp.where(
                lane_ids == base, coarse, jnp.where(lane_ids == base + 1, fine, 0.0)
            )
            side_ref[side, pl.ds(at, TILE), :] = jnp.where(
                sides[side], grad_unnorm, extra
            ).astype(jnp.bfloat16)
        return carry

    lax.fori_loop(0, total_rows // TILE, prepare, 0)
    query_ref[...] = jnp.zeros_like(query_ref)

    def tile_part(query_at, key_rows, values, masked):
        query_at = pl.multiple_of(query_at, TILE)
        scaled = joint_ref[pl.ds(query_at, TILE), :wide] * jnp.bfloat16(HD**-0.5)
        nothing = jnp.zeros_like(scaled)
        for side in range(2):
            powers = jnp.exp(inner_cols(key_rows, jnp.where(sides[side], scaled, nothing)))
            if masked:
                powers = jnp.where(causal, powers, 0.0)
            upstream = side_ref[side, pl.ds(query_at, TILE), :]
            grad_scores = (powers * inner_cols(values[side], upstream)).astype(jnp.bfloat16)
            value_ref[side] += product(powers.astype(jnp.bfloat16), upstream)
            key_ref[side] += product(grad_scores, scaled)
            query_ref[side, pl.ds(query_at, TILE), :] += inner_rows(grad_scores, key_rows)

    def key_tile(index, carry):
        key_at = pl.multiple_of(index * TILE, TILE)
        key_rows = joint_ref[pl.ds(key_at, TILE), wide : 2 * wide]
        value_rows = joint_ref[pl.ds(key_at, TILE), 2 * wide :]
        values = [jnp.where(side, value_rows, jnp.ones_like(value_rows)) for side in sides]
        key_ref[...] = jnp.zeros_like(key_ref)
        value_ref[...] = jnp.zeros_like(value_ref)
        tile_part(key_at, key_rows, values, True)

        def query_tile(query_index, inner):
            tile_part(query_index * TILE, key_rows, values, False)
            return inner

        lax.fori_loop(index + 1, total_rows // TILE, query_tile, 0)
        joint_grad[pl.ds(key_at, TILE), wide : 2 * wide] = jnp.where(
            first, key_ref[0], key_ref[1]
        ).astype(jnp.bfloat16)
        joint_grad[pl.ds(key_at, TILE), 2 * wide :] = jnp.where(
            first, value_ref[0], value_ref[1]
        ).astype(jnp.bfloat16)
        return carry

    lax.fori_loop(0, total_rows // TILE, key_tile, 0)

    def finish(index, carry):
        at = pl.multiple_of(index * TILE, TILE)
        joint_grad[pl.ds(at, TILE), :wide] = (
            jnp.where(first, query_ref[0, pl.ds(at, TILE), :], query_ref[1, pl.ds(at, TILE), :])
            * HD**-0.5
        ).astype(jnp.bfloat16)
        return carry

    lax.fori_loop(0, total_rows // TILE, finish, 0)
    for at in range(16):
        to = pl.multiple_of(place_ref[at] * BLOCK_ROWS, BLOCK_ROWS)
        sends[at // 4][(at % 4) * BLOCK_ROWS : (at % 4 + 1) * BLOCK_ROWS, :] = joint_grad[
            pl.ds(to, BLOCK_ROWS), :
        ]


def head_backward(joint_sorted, mixed_sorted, totals_sorted, pieces, places):
    rows = pieces[0].shape[0]
    total_rows, wide = joint_sorted.shape
    vmem = pl.BlockSpec(memory_space=pltpu.VMEM)
    return pl.pallas_call(
        head_backward_kernel,
        out_shape=[jax.ShapeDtypeStruct((rows, wide), jnp.bfloat16)] * 4,
        in_specs=[pl.BlockSpec(memory_space=pltpu.SMEM)] + [vmem] * 7,
        out_specs=[vmem] * 4,
        scratch_shapes=[
            pltpu.VMEM((total_rows, 2 * HD), jnp.float32),
            pltpu.VMEM((2, total_rows, 2 * HD), jnp.bfloat16),
            pltpu.VMEM((2, total_rows, 2 * HD), jnp.float32),
            pltpu.VMEM((2, TILE, 2 * HD), jnp.float32),
            pltpu.VMEM((2, TILE, 2 * HD), jnp.float32),
            pltpu.VMEM((total_rows, wide), jnp.bfloat16),
        ],
        cost_estimate=pl.CostEstimate(
            flops=30 * total_rows * total_rows * 2 * HD,
            bytes_accessed=8 * total_rows * wide,
            transcendentals=2 * total_rows * total_rows,
        ),
        name="head_backward",
    )(places, joint_sorted, mixed_sorted, totals_sorted, *pieces)


def norm_parts(values):
    average = jnp.mean(values, axis=-1, keepdims=True)
    centred = values - average
    spread_of = jnp.mean(centred * centred, axis=-1, keepdims=True)
    inverse = lax.rsqrt(spread_of + EPS)
    return centred * inverse, inverse


def norm_pull(grad, scaled, inverse, gain):
    lifted = grad * gain
    return (
        lifted
        - jnp.mean(lifted, axis=-1, keepdims=True)
        - scaled * jnp.mean(lifted * scaled, axis=-1, keepdims=True)
    ) * inverse


def chip_body(
    inputs,
    block_order,
    first_gain,
    first_shift,
    joint_weight,
    query_bias,
    value_bias,
    mixer_weight,
    mixer_bias,
    second_gain,
    second_shift,
    expand_weight,
    expand_bias,
    reduce_weight,
    reduce_bias,
    cotangent,
):
    low, full = jnp.bfloat16, jnp.float32
    group = lax.axis_index("dp")
    core = lax.axis_index("core")
    depth = lax.axis_index("z")
    even = core == 0
    own_rows = inputs.shape[1]
    share = joint_weight.shape[0]

    def chip_order(mine, theirs):
        return jnp.where(
            even,
            jnp.concatenate([mine, theirs], axis=0),
            jnp.concatenate([theirs, mine], axis=0),
        )

    def cores_exchanged(parts):
        mine = jnp.where(even, parts[0], parts[1])
        theirs = jnp.where(even, parts[1], parts[0])
        return chip_order(mine, swapped(theirs, CORE_BIT))

    def by_depth(value):
        value = jnp.where(depth % 2 == 0, value, value.reshape((2, 2) + value.shape[1:])[:, ::-1].reshape(value.shape))
        return jnp.where(depth < 2, value, jnp.concatenate([value[2:], value[:2]], axis=0))

    chip_ids = jnp.arange(16, dtype=jnp.int32)
    across, along = chip_ids // 4, chip_ids % 4
    slots = (across ^ group) * 4 + (along ^ depth)
    col_slots = jnp.arange(4, dtype=jnp.int32) ^ depth
    mixer_slots = ((slots // 8) ^ core) * 8 + (((slots // 2) % 4) ^ depth) * 2 + slots % 2
    table = jnp.concatenate([slots, col_slots, mixer_slots])
    places = block_order[
        ((chip_ids // 4) ^ depth) * 4 + (((chip_ids // 2) % 2) ^ core) * 2 + chip_ids % 2
    ]

    tokens = inputs[0]
    pair = jnp.concatenate([tokens, cotangent[0]], axis=0)
    pair_got = swapped(pair, CORE_BIT)

    units = expand_weight.shape[1] // 2
    small = jnp.concatenate(
        [
            jnp.concatenate(
                [
                    first_gain,
                    first_shift,
                    query_bias,
                    value_bias,
                    mixer_bias,
                    second_gain,
                    second_shift,
                    reduce_bias,
                ]
            ),
            expand_bias,
        ]
    ).reshape(1, 384)
    joint_parts = joint_weight.reshape(share, 3, 2, 4, 128).transpose(2, 0, 3, 1, 4).reshape(2, share, 1536)
    small_rows = jnp.pad(small, ((0, 7), (0, 1536 - 384)))
    joint_mine = jnp.where(even, joint_parts[0], joint_parts[1])
    joint_theirs = jnp.where(even, joint_parts[1], joint_parts[0])
    joint_got = swapped(jnp.concatenate([joint_theirs, small_rows]), CORE_BIT)
    small_got = joint_got[share:, :384]
    small_pair = jnp.concatenate(
        [
            jnp.where(even, small_rows[:, :384], small_got),
            jnp.where(even, small_got, small_rows[:, :384]),
            jnp.zeros((8, 768), low),
        ],
        axis=1,
    )
    joint_own = jnp.concatenate([chip_order(joint_mine, joint_got[:share]), small_pair])
    joint_line = line_of(joint_own)
    joint_arrays, joint_at = collected(joint_line)

    expand_parts = expand_weight.reshape(share, 16, 2, 128)
    expand_own = cores_exchanged(
        (expand_parts[:, :, 0].reshape(share, units), expand_parts[:, :, 1].reshape(share, units))
    )
    mixer_own = cores_exchanged((mixer_weight[:, : D // 2], mixer_weight[:, D // 2 :]))
    hidden_own = jnp.concatenate([expand_own[:, :D], expand_own[:, D:], reduce_weight])
    mixer_line = line_of(after(mixer_own, *joint_line[1:]))
    hidden_line = line_of(after(hidden_own, *mixer_line[1:]))
    mixer_arrays, mixer_at = collected_small(after(mixer_line, *joint_arrays[1:3]))
    token_rows = jnp.concatenate([tokens, pair_got[:own_rows]], axis=0).astype(full)
    upstream = jnp.concatenate([cotangent[0], pair_got[own_rows:]], axis=0)
    scaled_one, inverse_one = norm_parts(token_rows)
    joint_arrays = after(joint_arrays, scaled_one)
    joint_plan = []
    for at, (array, entry) in enumerate(joint_at):
        for col in range(4):
            source_at = looked(entry, 64, 16 + col, 384)
            joint_plan.append((array, source_at, 0, slot_part(at, 0, 64, col * 384, 384)))
        joint_plan.append((array, fixed(entry, pl.ds(64, 8), pl.ds(0, 768)), 1, slot(at)))
    joint_done = moved(
        table,
        joint_arrays,
        joint_plan,
        [(16, 64, 1536), (16, 8, 768)],
    )
    joint_full = joint_done[0].reshape(D, 1536)
    small_all = joint_done[1][:, 0].reshape(32, 384)
    count = share
    rows_of = small_all[:, : 8 * count].reshape(32, 8, count).transpose(1, 0, 2).reshape(8, 32 * count)
    (
        gain_one,
        shift_one,
        query_shift,
        value_shift,
        mixer_shift,
        gain_two,
        shift_two,
        reduce_shift,
    ) = [rows_of[at] for at in range(8)]
    expand_shift = small_all[:, 8 * count :].reshape(16, 2, 128)
    expand_shift = jnp.where(even, expand_shift[:, 0], expand_shift[:, 1]).reshape(-1)

    normed = (scaled_one * gain_one + shift_one).astype(low)
    halves_of = [
        jnp.where(even, item[: D // 2], item[D // 2 :]).reshape(4, 1, 128)
        for item in (query_shift, value_shift)
    ]
    joint_shift = by_depth(jnp.concatenate([halves_of[0], jnp.zeros_like(halves_of[0]), halves_of[1]], axis=1))
    joint_rows = (product(normed, joint_full) + joint_shift.reshape(1536)).astype(low)
    hidden_line = after(hidden_line, joint_rows)
    joint_rows = after(joint_rows, hidden_line[3], mixer_arrays)
    hidden_arrays, hidden_at = collected(hidden_line)
    head_pieces = [joint_rows[:, at * 384 : (at + 1) * 384] for at in range(4)]
    head_pieces = [head_pieces[0]] + [swapped(head_pieces[at], Z_BITS[at]) for at in (1, 2, 3)]
    hidden_plan = []
    for at, (array, entry) in enumerate(hidden_at):
        hidden_plan.append((array, fixed(entry, pl.ds(0, 64)), 0, slot_part(at, 0, 64, 0, D)))
        hidden_plan.append((array, fixed(entry, pl.ds(64, 64)), 0, slot_part(at, 0, 64, D, D)))
        hidden_plan.append((array, fixed(entry, pl.ds(128, 128)), 1, slot(at)))
    expand_full, reduce_full = moved(table, hidden_arrays, hidden_plan, [(16, 64, units), (16, 128, D)])
    expand_full, reduce_full = expand_full.reshape(D, units), reduce_full.reshape(units, D)
    mixer_cols = moved(
        table,
        mixer_arrays,
        [(array, fixed(entry), 0, slot(20 + at)) for at, (array, entry) in enumerate(mixer_at)],
        [(16, 64, D // 2)],
    )[0].reshape(2, D // 2, D // 2)
    mixer_mine, mixer_theirs = mixer_cols[0], swapped(mixer_cols[1], CORE_BIT)
    mixer_full = jnp.where(
        even,
        jnp.concatenate([mixer_mine, mixer_theirs], axis=1),
        jnp.concatenate([mixer_theirs, mixer_mine], axis=1),
    )
    forward = head_forward(head_pieces, places)
    mixed_out, (joint_sorted, mixed_sorted, totals_sorted) = forward[:4], forward[4:]
    mixed_out = after(mixed_out, hidden_arrays[1], hidden_arrays[2])
    mixed_rows = jnp.concatenate(
        [mixed_out[0]] + [swapped(mixed_out[at], Z_BITS[at]) for at in (1, 2, 3)], axis=1
    )

    def both_cores(part):
        turned = jnp.concatenate([part[own_rows:], part[:own_rows]], axis=0).astype(low)
        return part + swapped(turned, CORE_BIT).astype(full)

    def own_sum(part):
        return part[:own_rows] + swapped(part[own_rows:].astype(low), CORE_BIT).astype(full)

    middle = token_rows + (both_cores(product(mixed_rows, mixer_full)) + mixer_shift)
    scaled_two, inverse_two = norm_parts(middle)
    second = (scaled_two * gain_two + shift_two).astype(low)
    before = product(second, expand_full) + expand_shift
    active, gelu_pull = jax.vjp(gelu_tanh, before)
    active = active.astype(low)
    result = middle[:own_rows] + (own_sum(product(active, reduce_full)) + reduce_shift)

    reduce_gradient = inner_rows(active, upstream).astype(low).reshape(16, 128, D)
    grad_before = gelu_pull(inner_cols(upstream, reduce_full))[0].astype(low)
    expand_gradient = inner_rows(second, grad_before).astype(low).reshape(16, 64, units)
    expand_shift_gradient = jnp.sum(grad_before.astype(full), axis=0)
    grad_second = both_cores(inner_cols(grad_before, expand_full))
    upstream_full = upstream.astype(full)
    grad_middle = upstream_full + norm_pull(grad_second, scaled_two, inverse_two, gain_two)
    grad_branch = grad_middle.astype(low)
    mixer_gradient = inner_rows(mixed_rows, grad_branch).astype(low)
    grad_mixed = inner_cols(grad_branch, mixer_full).astype(low)
    grad_pieces = [grad_mixed[:, at * 128 : (at + 1) * 128] for at in range(4)]
    grad_pieces = [grad_pieces[0]] + [swapped(grad_pieces[at], Z_BITS[at]) for at in (1, 2, 3)]
    mixer_keep = jnp.where(even, mixer_gradient[:, : D // 2], mixer_gradient[:, D // 2 :])
    mixer_send = jnp.where(even, mixer_gradient[:, D // 2 :], mixer_gradient[:, : D // 2])
    mixer_got = swapped(mixer_send, CORE_BIT)
    mixer_whole = jnp.concatenate([mixer_keep, mixer_got], axis=0).reshape(16, 64, D // 2)
    hidden_plan = []
    for at in range(16):
        to, place = GROUP_OF[at]
        hidden_plan.append((0, slot_part(at, 0, 64, 0, D), to, fixed(place, pl.ds(0, 64))))
        hidden_plan.append((0, slot_part(at, 0, 64, D, D), to, fixed(place, pl.ds(64, 64))))
        hidden_plan.append((1, slot(at), to, fixed(place, pl.ds(128, 128))))
        for half in range(2):
            left = fixed(place, pl.ds(256, 32), pl.ds(half * (D // 2), D // 2))
            hidden_plan.append((2, slot_rows(20 + at, half * 32, 32), to, left))
    grouped = moved(
        table, (expand_gradient, reduce_gradient, mixer_whole), hidden_plan, [(4, 288, D)] * 4
    )
    hidden_state = summed_first(grouped)
    grad_pieces = after(grad_pieces, grouped)
    grad_out = head_backward(joint_sorted, mixed_sorted, totals_sorted, grad_pieces, places)
    grad_got = [swapped(grad_out[at], Z_BITS[at]) for at in (1, 2, 3)]
    grad_got = after(grad_got, hidden_state)
    hidden_state = summed_second(hidden_state)
    grad_joint = jnp.concatenate([grad_out[0]] + grad_got, axis=1)
    joint_gradient = inner_rows(normed, grad_joint).astype(low).reshape(16, 64, 1536)
    grad_normed_part = inner_cols(grad_joint, joint_full)
    joint_sums = by_depth(jnp.sum(grad_joint.astype(full), axis=0).reshape(4, 3, 128))

    def one_core(values):
        values = values.reshape(1, -1)
        nothing = jnp.zeros_like(values)
        return jnp.where(
            even, jnp.concatenate([values, nothing], axis=1), jnp.concatenate([nothing, values], axis=1)
        )[0]

    expand_rows = expand_shift_gradient.reshape(16, 1, 128)
    expand_rows = jnp.where(
        even,
        jnp.concatenate([expand_rows, jnp.zeros_like(expand_rows)], axis=1),
        jnp.concatenate([jnp.zeros_like(expand_rows), expand_rows], axis=1),
    ).reshape(32, 128)
    sums = jnp.stack(
        [
            jnp.sum(grad_normed_part * scaled_one, axis=0),
            jnp.sum(grad_normed_part, axis=0),
            one_core(joint_sums[:, 0]),
            one_core(joint_sums[:, 2]),
            jnp.sum(grad_branch[:own_rows].astype(full), axis=0),
            jnp.sum(grad_second[:own_rows] * scaled_two[:own_rows], axis=0),
            jnp.sum(grad_second[:own_rows], axis=0),
            jnp.sum(upstream_full[:own_rows], axis=0),
        ]
    )
    sums = sums.astype(low).reshape(8, 32, count).transpose(1, 0, 2).reshape(32, 8 * count)
    sums = jnp.concatenate([sums, expand_rows.astype(low)], axis=1).reshape(16, 1, 768)
    sums = jnp.pad(sums, ((0, 0), (0, 7), (0, 0)))
    joint_gradient = after(joint_gradient, hidden_state)
    joint_plan = []
    for at in range(16):
        to, place = GROUP_OF[at]
        for col in range(4):
            left = looked(place, 64, 16 + col, 384)
            joint_plan.append((0, slot_part(at, 0, 64, col * 384, 384), to, left))
        joint_plan.append((1, slot(at), to, fixed(place, pl.ds(64, 8), pl.ds(0, 768))))
    joint_state = summed_second(
        summed_first(moved(table, (joint_gradient, sums), joint_plan, [(4, 72, 1536)] * 4))
    )
    hidden_sum = summed_third(hidden_state, joint_state)
    joint_sum = summed_third(joint_state)
    grad_normed = own_sum(grad_normed_part)
    input_gradient = (
        grad_middle[:own_rows]
        + norm_pull(grad_normed, scaled_one[:own_rows], inverse_one[:own_rows], gain_one)
    ).astype(low)

    def paired(first_core, second_core):
        mine = jnp.where(even, first_core, second_core)
        got = swapped(jnp.where(even, second_core, first_core), CORE_BIT)
        return mine, got

    mixer_mine, mixer_got = paired(hidden_sum[256:, : D // 2], hidden_sum[256:, D // 2 :])
    mixer_out = jnp.where(
        even,
        jnp.concatenate([mixer_mine, mixer_got], axis=1),
        jnp.concatenate([mixer_got, mixer_mine], axis=1),
    )
    expand_pairs = hidden_sum[:128].reshape(2, 2, share, 8, 128)
    expand_mine, expand_got = paired(expand_pairs[:, 0], expand_pairs[:, 1])
    expand_out = jnp.where(
        even, jnp.stack([expand_mine, expand_got], axis=3), jnp.stack([expand_got, expand_mine], axis=3)
    )
    expand_out = expand_out.transpose(1, 0, 2, 3, 4).reshape(share, 2 * units)
    joint_mine = jnp.where(even, joint_sum[:share], joint_sum[share : 2 * share])
    joint_got = swapped(
        jnp.concatenate(
            [jnp.where(even, joint_sum[share : 2 * share], joint_sum[:share]), joint_sum[2 * share :]]
        ),
        CORE_BIT,
    )
    joint_mine_parts = joint_mine.reshape(share, 4, 3, 128)
    joint_got_parts = joint_got[:share].reshape(share, 4, 3, 128)
    joint_out = jnp.where(
        even,
        jnp.stack([joint_mine_parts, joint_got_parts], axis=1),
        jnp.stack([joint_got_parts, joint_mine_parts], axis=1),
    )
    joint_out = joint_out.transpose(0, 3, 1, 2, 4).reshape(share, 3 * D)
    own_sums = joint_sum[2 * share, :768] + joint_got[share, :768]
    own_sums = jnp.where(even, own_sums[:384], own_sums[384:])
    vectors = [own_sums[at * count : (at + 1) * count] for at in range(8)] + [own_sums[8 * count :]]
    return (
        result.astype(low)[None],
        input_gradient[None],
        vectors[0],
        vectors[1],
        joint_out,
        vectors[2],
        vectors[3],
        mixer_out,
        vectors[4],
        vectors[5],
        vectors[6],
        expand_out,
        vectors[8],
        hidden_sum[128:256],
        vectors[7],
    )


def solution(mesh):
    dp_size, sp_size = mesh.shape["dp"], mesh.shape["sp"]
    if dp_size == 4 and sp_size == 8:
        mesh = Mesh(mesh.devices.reshape(dp_size, sp_size // 2, 2), ALL)
        body, line = chip_body, ("z", "core")
    else:
        body, line = ring_body, ("sp",)
    rows = P("dp", line, None)
    vector = P(("dp",) + line)
    matrix = P(("dp",) + line, None)
    in_specs = (
        rows,
        P(),
        vector,
        vector,
        matrix,
        vector,
        vector,
        matrix,
        vector,
        vector,
        vector,
        matrix,
        vector,
        matrix,
        vector,
        rows,
    )
    out_specs = (
        rows,
        rows,
        vector,
        vector,
        matrix,
        vector,
        vector,
        matrix,
        vector,
        vector,
        vector,
        matrix,
        vector,
        matrix,
        vector,
    )
    return jax.shard_map(body, mesh=mesh, in_specs=in_specs, out_specs=out_specs, check_vma=False)
```

```python
import math

import jax
import jax.numpy as jnp
from jax import lax
from jax.experimental import pallas as pl
from jax.experimental.pallas import tpu as pltpu
from jax.sharding import Mesh
from jax.sharding import PartitionSpec as P

D = 1024
H = 16
HD = 64


EPS = 1e-05


def passed_along(value, axis, steps):
    count = lax.axis_size(axis)
    pairs = [(source, (source + steps) % count) for source in range(count)]
    return lax.ppermute(value, axis, pairs)


def layer_norm(values, scaling, offset):
    average = jnp.mean(values, axis=-1, keepdims=True)
    centred = values - average
    spread = jnp.mean(centred * centred, axis=-1, keepdims=True)
    return centred * lax.rsqrt(spread + EPS) * scaling + offset


def gelu_tanh(values):
    return jax.nn.gelu(values, approximate=True)


def product(left, right):
    return jnp.dot(left, right, preferred_element_type=jnp.float32)


def inner_rows(left, right):
    return lax.dot_general(
        left, right, (((0,), (0,)), ((), ())), preferred_element_type=jnp.float32
    )


def inner_cols(left, right):
    return lax.dot_general(
        left, right, (((1,), (1,)), ((), ())), preferred_element_type=jnp.float32
    )


def tile_forward(queries, key_rows, value_rows, visible, factor):
    scores = jnp.einsum("tqhd,tkhd->thqk", queries, key_rows, preferred_element_type=jnp.float32)
    powers = jnp.exp(scores * factor)
    if visible is not None:
        powers = jnp.where(visible[:, None], powers, 0.0)
    unnorm = jnp.einsum(
        "thqk,tkhd->tqhd",
        powers.astype(jnp.bfloat16),
        value_rows,
        preferred_element_type=jnp.float32,
    )
    return (unnorm, jnp.sum(powers, axis=-1))


def tile_backward(queries, grad_unnorm, grad_totals, key_rows, value_rows, visible, factor):
    scores = jnp.einsum("tqhd,tkhd->thqk", queries, key_rows, preferred_element_type=jnp.float32)
    powers = jnp.exp(scores * factor)
    if visible is not None:
        powers = jnp.where(visible[:, None], powers, 0.0)
    grad_powers = (
        jnp.einsum("tqhd,tkhd->thqk", grad_unnorm, value_rows, preferred_element_type=jnp.float32)
        + grad_totals[..., None]
    )
    grad_scores = (powers * grad_powers * factor).astype(jnp.bfloat16)
    grad_queries = jnp.einsum(
        "thqk,tkhd->tqhd", grad_scores, key_rows, preferred_element_type=jnp.float32
    )
    grad_keys = jnp.einsum(
        "thqk,tqhd->tkhd", grad_scores, queries, preferred_element_type=jnp.float32
    )
    grad_values = jnp.einsum(
        "thqk,tqhd->tkhd",
        powers.astype(jnp.bfloat16),
        grad_unnorm,
        preferred_element_type=jnp.float32,
    )
    return (grad_queries, grad_keys, grad_values)


def halves(stacked, half_rows, along):
    return (
        lax.slice_in_dim(stacked, 0, half_rows, axis=along),
        lax.slice_in_dim(stacked, half_rows, 2 * half_rows, axis=along),
    )


def query_stack(later_block, stacked, half_rows, along):
    lower_part, upper_part = halves(stacked, half_rows, along)
    return jnp.stack([upper_part, jnp.where(later_block, lower_part, upper_part)])


def key_stack(later_block, stacked, half_rows, along):
    lower_part, upper_part = halves(stacked, half_rows, along)
    return jnp.stack([lower_part, jnp.where(later_block, lower_part, upper_part)])


def query_spread(later_block, tile_pair, along):
    nothing = jnp.zeros_like(tile_pair[0])
    lower_part = jnp.where(later_block, tile_pair[1], nothing)
    upper_part = tile_pair[0] + jnp.where(later_block, nothing, tile_pair[1])
    return jnp.concatenate([lower_part, upper_part], axis=along)


def key_spread(later_block, tile_pair, along):
    nothing = jnp.zeros_like(tile_pair[0])
    lower_part = tile_pair[0] + jnp.where(later_block, tile_pair[1], nothing)
    upper_part = jnp.where(later_block, nothing, tile_pair[1])
    return jnp.concatenate([lower_part, upper_part], axis=along)


def pair_forward(later_block, queries, key_rows, value_rows, factor):
    half_rows = queries.shape[0] // 2
    unnorm, totals = tile_forward(
        query_stack(later_block, queries, half_rows, 0),
        key_stack(later_block, key_rows, half_rows, 0),
        key_stack(later_block, value_rows, half_rows, 0),
        None,
        factor,
    )
    return (query_spread(later_block, unnorm, 0), query_spread(later_block, totals, 1))


def pair_backward(later_block, queries, grad_unnorm, grad_totals, key_rows, value_rows, factor):
    half_rows = queries.shape[0] // 2
    grads = tile_backward(
        query_stack(later_block, queries, half_rows, 0),
        query_stack(later_block, grad_unnorm, half_rows, 0),
        query_stack(later_block, grad_totals, half_rows, 1),
        key_stack(later_block, key_rows, half_rows, 0),
        key_stack(later_block, value_rows, half_rows, 0),
        None,
        factor,
    )
    return (
        query_spread(later_block, grads[0], 0),
        key_spread(later_block, grads[1], 0),
        key_spread(later_block, grads[2], 0),
    )


def ring_body(
    inputs,
    block_order,
    first_gain,
    first_shift,
    joint_weight,
    query_bias,
    value_bias,
    mixer_weight,
    mixer_bias,
    second_gain,
    second_shift,
    expand_weight,
    expand_bias,
    reduce_weight,
    reduce_bias,
    cotangent,
):
    owned_shards = (
        first_gain,
        first_shift,
        joint_weight,
        query_bias,
        value_bias,
        mixer_weight,
        mixer_bias,
        second_gain,
        second_shift,
        expand_weight,
        expand_bias,
        reduce_weight,
        reduce_bias,
    )
    gathered = (
        lax.all_gather(owned_shards[0], ("dp", "sp"), axis=0, tiled=True),
        lax.all_gather(owned_shards[1], ("dp", "sp"), axis=0, tiled=True),
        lax.all_gather(owned_shards[2], ("dp", "sp"), axis=0, tiled=True),
        lax.all_gather(owned_shards[3], ("dp", "sp"), axis=0, tiled=True),
        lax.all_gather(owned_shards[4], ("dp", "sp"), axis=0, tiled=True),
        lax.all_gather(owned_shards[5], ("dp", "sp"), axis=0, tiled=True),
        lax.all_gather(owned_shards[6], ("dp", "sp"), axis=0, tiled=True),
        lax.all_gather(owned_shards[7], ("dp", "sp"), axis=0, tiled=True),
        lax.all_gather(owned_shards[8], ("dp", "sp"), axis=0, tiled=True),
        lax.all_gather(owned_shards[9], ("dp", "sp"), axis=0, tiled=True),
        lax.all_gather(owned_shards[10], ("dp", "sp"), axis=0, tiled=True),
        lax.all_gather(owned_shards[11], ("dp", "sp"), axis=0, tiled=True),
        lax.all_gather(owned_shards[12], ("dp", "sp"), axis=0, tiled=True),
    )
    (
        gain_one,
        shift_one,
        joint_full,
        query_shift,
        value_shift,
        mixer_full,
        mixer_shift,
        gain_two,
        shift_two,
        expand_full,
        expand_shift,
        reduce_full,
        reduce_shift,
    ) = gathered
    factor = HD ** (-0.5)
    members = lax.axis_size("sp")
    position = lax.axis_index("sp")
    token_rows = inputs[0].astype(jnp.float32)
    row_count = token_rows.shape[0]
    half_rows = row_count // 2
    own_low = block_order[2 * position]
    offsets = jnp.arange(half_rows, dtype=jnp.int32)
    own_places = jnp.concatenate(
        [own_low * half_rows + offsets, block_order[2 * position + 1] * half_rows + offsets]
    )
    visible = (own_places[None, :] <= own_places[:, None])[None]
    normed, first_pull = jax.vjp(
        layer_norm, token_rows, gain_one.astype(jnp.float32), shift_one.astype(jnp.float32)
    )
    normed_low = normed.astype(jnp.bfloat16)
    joint_shift = jnp.concatenate([query_shift, jnp.zeros_like(query_shift), value_shift]).astype(
        jnp.float32
    )
    joint_rows = (product(normed_low, joint_full) + joint_shift).astype(jnp.bfloat16)
    queries = joint_rows[:, :D].reshape(row_count, H, HD)
    key_rows = joint_rows[:, D : 2 * D].reshape(row_count, H, HD)
    value_rows = joint_rows[:, 2 * D :].reshape(row_count, H, HD)
    unnorm, totals = tile_forward(queries[None], key_rows[None], value_rows[None], visible, factor)

    def forward_turn(turn_index, state_in):
        moving_keys, moving_values, unnorm_sum, totals_sum = state_in
        moving_keys, moving_values = passed_along((moving_keys, moving_values), "sp", 1)
        source = (position - turn_index) % members
        later_block = own_low > block_order[2 * source]
        extra_unnorm, extra_totals = pair_forward(
            later_block, queries, moving_keys, moving_values, factor
        )
        return (moving_keys, moving_values, unnorm_sum + extra_unnorm, totals_sum + extra_totals)

    final_state = lax.fori_loop(
        1, members, forward_turn, (key_rows, value_rows, unnorm[0], totals[0])
    )
    unnorm = final_state[2]
    totals_rows = jnp.transpose(final_state[3])
    mixed = unnorm / totals_rows[:, :, None]
    mixed_rows = mixed.reshape(row_count, D).astype(jnp.bfloat16)
    middle = token_rows + (product(mixed_rows, mixer_full) + mixer_shift.astype(jnp.float32))
    second, second_pull = jax.vjp(
        layer_norm, middle, gain_two.astype(jnp.float32), shift_two.astype(jnp.float32)
    )
    second_low = second.astype(jnp.bfloat16)
    before = product(second_low, expand_full) + expand_shift.astype(jnp.float32)
    active, gelu_pull = jax.vjp(gelu_tanh, before)
    active_low = active.astype(jnp.bfloat16)
    result = middle + (product(active_low, reduce_full) + reduce_shift.astype(jnp.float32))
    joint_back, mixer_back, expand_back, reduce_back = (
        lax.all_gather(joint_weight, ("dp", "sp"), axis=0, tiled=True),
        lax.all_gather(mixer_weight, ("dp", "sp"), axis=0, tiled=True),
        lax.all_gather(expand_weight, ("dp", "sp"), axis=0, tiled=True),
        lax.all_gather(reduce_weight, ("dp", "sp"), axis=0, tiled=True),
    )
    upstream = cotangent[0]
    upstream_full = upstream.astype(jnp.float32)
    reduce_gradient = inner_rows(active_low, upstream)
    reduce_shift_gradient = jnp.sum(upstream_full, axis=0)
    grad_active = inner_cols(upstream, reduce_back)
    grad_before = gelu_pull(grad_active)[0].astype(jnp.bfloat16)
    expand_gradient = inner_rows(second_low, grad_before)
    expand_shift_gradient = jnp.sum(grad_before.astype(jnp.float32), axis=0)
    grad_second = inner_cols(grad_before, expand_back)
    grad_middle_norm, gain_two_gradient, shift_two_gradient = second_pull(grad_second)
    grad_middle = upstream_full + grad_middle_norm
    grad_branch = grad_middle.astype(jnp.bfloat16)
    mixer_gradient = inner_rows(mixed_rows, grad_branch)
    mixer_shift_gradient = jnp.sum(grad_branch.astype(jnp.float32), axis=0)
    grad_mixed = inner_cols(grad_branch, mixer_back).astype(jnp.bfloat16).reshape(row_count, H, HD)
    grad_mixed_full = grad_mixed.astype(jnp.float32)
    grad_unnorm = (grad_mixed_full / totals_rows[:, :, None]).astype(jnp.bfloat16)
    grad_totals = jnp.transpose(-jnp.sum(grad_mixed_full * mixed, axis=-1) / totals_rows)
    own_grads = tile_backward(
        queries[None],
        grad_unnorm[None],
        grad_totals[None],
        key_rows[None],
        value_rows[None],
        visible,
        factor,
    )

    def keys_turn(turn_index, state_in):
        moving_keys, moving_values, key_carry, value_carry, query_sum = state_in
        moving_keys, moving_values = passed_along((moving_keys, moving_values), "sp", 1)
        key_carry, value_carry = (
            passed_along(key_carry.astype(jnp.bfloat16), "sp", 1).astype(key_carry.dtype),
            passed_along(value_carry.astype(jnp.bfloat16), "sp", 1).astype(value_carry.dtype),
        )
        source = (position - turn_index) % members
        later_block = own_low > block_order[2 * source]
        extra_query, extra_key, extra_value = pair_backward(
            later_block, queries, grad_unnorm, grad_totals, moving_keys, moving_values, factor
        )
        return (
            moving_keys,
            moving_values,
            key_carry + extra_key,
            value_carry + extra_value,
            query_sum + extra_query,
        )

    final_back = lax.fori_loop(
        1,
        members,
        keys_turn,
        (key_rows, value_rows, own_grads[1][0], own_grads[2][0], own_grads[0][0]),
    )
    key_sum, value_sum = (
        passed_along(final_back[2].astype(jnp.bfloat16), "sp", 1).astype(jnp.float32),
        passed_along(final_back[3].astype(jnp.bfloat16), "sp", 1).astype(jnp.float32),
    )
    query_sum = final_back[4]
    grad_joint = jnp.concatenate(
        [
            query_sum.reshape(row_count, D),
            key_sum.reshape(row_count, D),
            value_sum.reshape(row_count, D),
        ],
        axis=1,
    ).astype(jnp.bfloat16)
    joint_gradient = inner_rows(normed_low, grad_joint)
    joint_sums = jnp.sum(grad_joint.astype(jnp.float32), axis=0)
    query_shift_gradient = joint_sums[:D]
    value_shift_gradient = joint_sums[2 * D :]
    grad_normed = inner_cols(grad_joint, joint_back)
    grad_rows_norm, gain_one_gradient, shift_one_gradient = first_pull(grad_normed)
    input_gradient = (grad_middle + grad_rows_norm).astype(jnp.bfloat16)
    gradient_sums = (
        lax.psum_scatter(gain_one_gradient, ("dp", "sp"), scatter_dimension=0, tiled=True),
        lax.psum_scatter(shift_one_gradient, ("dp", "sp"), scatter_dimension=0, tiled=True),
        lax.psum_scatter(joint_gradient, ("dp", "sp"), scatter_dimension=0, tiled=True),
        lax.psum_scatter(query_shift_gradient, ("dp", "sp"), scatter_dimension=0, tiled=True),
        lax.psum_scatter(value_shift_gradient, ("dp", "sp"), scatter_dimension=0, tiled=True),
        lax.psum_scatter(mixer_gradient, ("dp", "sp"), scatter_dimension=0, tiled=True),
        lax.psum_scatter(mixer_shift_gradient, ("dp", "sp"), scatter_dimension=0, tiled=True),
        lax.psum_scatter(gain_two_gradient, ("dp", "sp"), scatter_dimension=0, tiled=True),
        lax.psum_scatter(shift_two_gradient, ("dp", "sp"), scatter_dimension=0, tiled=True),
        lax.psum_scatter(expand_gradient, ("dp", "sp"), scatter_dimension=0, tiled=True),
        lax.psum_scatter(expand_shift_gradient, ("dp", "sp"), scatter_dimension=0, tiled=True),
        lax.psum_scatter(reduce_gradient, ("dp", "sp"), scatter_dimension=0, tiled=True),
        lax.psum_scatter(reduce_shift_gradient, ("dp", "sp"), scatter_dimension=0, tiled=True),
    )
    return (result.astype(jnp.bfloat16)[None], input_gradient[None]) + tuple(gradient_sums)


ALL = ("dp", "z", "core")
CHIPS = ("dp", "z")
CORE_BIT = 1
Z_BITS = (0, 2, 4, 6)
X_BIT = 8
Y_BIT = 16
TILE = 512
BLOCK_ROWS = 128


def swapped(value, mask):
    count = lax.axis_size(ALL)
    return lax.ppermute(value, ALL, [(source, source ^ mask) for source in range(count)])


def moved_kernel(table_ref, *refs, plan, source_count):
    sources, targets, sem = refs[:source_count], refs[source_count:-1], refs[-1]
    copies = []
    for source, source_at, target, target_at in plan:
        copy = pltpu.make_async_copy(
            sources[source].at[source_at(table_ref)],
            targets[target].at[target_at(table_ref)],
            sem.at[len(copies)],
        )
        copy.start()
        copies.append(copy)
    for copy in copies:
        copy.wait()


def moved(table, sources, plan, shapes):
    return pl.pallas_call(
        lambda *refs: moved_kernel(*refs, plan=plan, source_count=len(sources)),
        out_shape=[jax.ShapeDtypeStruct(shape, jnp.bfloat16) for shape in shapes],
        in_specs=[pl.BlockSpec(memory_space=pltpu.SMEM)]
        + [pl.BlockSpec(memory_space=pl.ANY)] * len(sources),
        out_specs=[pl.BlockSpec(memory_space=pltpu.VMEM)] * len(shapes),
        scratch_shapes=[pltpu.SemaphoreType.DMA((len(plan),))],
        cost_estimate=pl.CostEstimate(
            flops=0, bytes_accessed=6 * sum(math.prod(shape) for shape in shapes), transcendentals=0
        ),
        name="moved",
    )(table, *sources)


def slot(at):
    return lambda table: (table[at],)


def slot_rows(at, start, count):
    return lambda table: (table[at], pl.ds(start, count))


def slot_part(at, start, count, left, width):
    return lambda table: (table[at], pl.ds(start, count), pl.ds(left, width))


def looked(entry, count, column_at, width):
    return lambda table: (
        entry,
        pl.ds(0, count),
        pl.ds(pl.multiple_of(table[column_at] * width, 128), width),
    )


def fixed(*index):
    return lambda table: index


def after(value, *others):
    return lax.optimization_barrier((value, others))[0]


def line_of(piece):
    return [piece] + [swapped(piece, bits) for bits in Z_BITS[1:]]


def collected(line):
    stacked = jnp.stack(line)
    beside, above = swapped(stacked, X_BIT), swapped(stacked, Y_BIT)
    arrays = [stacked, beside, above, swapped(beside[:2], Y_BIT), swapped(above[2:], X_BIT)]
    held = [(at // 4, at % 4) for at in range(12)] + [(3, 0), (3, 1), (4, 0), (4, 1)]
    return arrays, held


def collected_small(line):
    stacked = jnp.stack(line)
    beside = swapped(stacked, X_BIT)
    arrays = [stacked, beside, swapped(stacked, Y_BIT), swapped(beside, Y_BIT)]
    return arrays, [(at // 4, at % 4) for at in range(16)]


GROUPS = ((0, 1, 4, 5), (8, 9, 12, 13), (2, 3, 10, 11), (6, 7, 14, 15))
GROUP_OF = {at: (group, place) for group, held in enumerate(GROUPS) for place, at in enumerate(held)}


def summed_first(grouped):
    low, full = jnp.bfloat16, jnp.float32
    keep_a, send_a, keep_b, send_b = grouped
    got_a = swapped(send_a, Y_BIT)
    got_b = swapped(send_b, X_BIT)
    onward_a = (keep_a[2:].astype(full) + got_a[2:].astype(full)).astype(low)
    onward_b = (keep_b[2:].astype(full) + got_b[2:].astype(full)).astype(low)
    here_a = keep_a[:2].astype(full) + got_a[:2].astype(full)
    here_b = keep_b[:2].astype(full) + got_b[:2].astype(full)
    return onward_a, onward_b, here_a, here_b


def summed_second(state):
    low, full = jnp.bfloat16, jnp.float32
    onward_a, onward_b, here_a, here_b = state
    here_a = here_a + swapped(onward_a, X_BIT).astype(full)
    here_b = here_b + swapped(onward_b, Y_BIT).astype(full)
    return here_a[0], here_a[1].astype(low), here_b[0].astype(low), here_b[1].astype(low)


def summed_third(state, *others):
    got = [swapped(state[along], Z_BITS[along]) for along in (1, 2, 3)]
    if others:
        got = after(got, *others)
    total = state[0]
    for piece in got:
        total = total + piece.astype(jnp.float32)
    return total


def lanes_low(rows):
    return lax.broadcasted_iota(jnp.int32, (rows, 2 * HD), 1) < HD


def head_forward_kernel(place_ref, *refs):
    pieces, sends, (joint_ref, mixed_ref, totals_ref), (acc_ref,) = (
        refs[:4],
        refs[4:8],
        refs[8:11],
        refs[11:],
    )
    wide = 2 * HD
    for at in range(16):
        to = pl.multiple_of(place_ref[at] * BLOCK_ROWS, BLOCK_ROWS)
        joint_ref[pl.ds(to, BLOCK_ROWS), :] = pieces[at // 4][
            (at % 4) * BLOCK_ROWS : (at % 4 + 1) * BLOCK_ROWS, :
        ]
    first = lanes_low(TILE)
    sides = (first, jnp.logical_not(first))
    row_ids = lax.broadcasted_iota(jnp.int32, (TILE, TILE), 0)
    col_ids = lax.broadcasted_iota(jnp.int32, (TILE, TILE), 1)
    causal = col_ids <= row_ids

    def tile_part(queries, key_at, masked):
        key_at = pl.multiple_of(key_at, TILE)
        key_rows = joint_ref[pl.ds(key_at, TILE), wide : 2 * wide]
        value_rows = joint_ref[pl.ds(key_at, TILE), 2 * wide :]
        for side in range(2):
            powers = jnp.exp(inner_cols(queries[side], key_rows))
            if masked:
                powers = jnp.where(causal, powers, 0.0)
            extended = jnp.where(sides[side], value_rows, jnp.ones_like(value_rows))
            acc_ref[side] += product(powers.astype(jnp.bfloat16), extended)

    def query_tile(index, carry):
        query_at = pl.multiple_of(index * TILE, TILE)
        scaled = joint_ref[pl.ds(query_at, TILE), :wide] * jnp.bfloat16(HD**-0.5)
        nothing = jnp.zeros_like(scaled)
        queries = [jnp.where(side, scaled, nothing) for side in sides]
        acc_ref[...] = jnp.zeros_like(acc_ref)

        def key_tile(key_index, inner):
            tile_part(queries, key_index * TILE, False)
            return inner

        lax.fori_loop(0, index, key_tile, 0)
        tile_part(queries, query_at, True)
        low_acc, high_acc = acc_ref[0], acc_ref[1]
        unnorm = jnp.where(first, low_acc, high_acc)
        totals = pltpu.roll(jnp.where(first, high_acc, low_acc), HD, 1)
        totals_ref[pl.ds(query_at, TILE), :] = totals
        mixed_ref[pl.ds(query_at, TILE), :] = unnorm / totals
        return carry

    lax.fori_loop(0, joint_ref.shape[0] // TILE, query_tile, 0)
    for at in range(16):
        to = pl.multiple_of(place_ref[at] * BLOCK_ROWS, BLOCK_ROWS)
        sends[at // 4][(at % 4) * BLOCK_ROWS : (at % 4 + 1) * BLOCK_ROWS, :] = mixed_ref[
            pl.ds(to, BLOCK_ROWS), :
        ].astype(jnp.bfloat16)


def head_forward(pieces, places):
    rows, wide = pieces[0].shape
    total_rows = 4 * rows
    vmem = pl.BlockSpec(memory_space=pltpu.VMEM)
    return pl.pallas_call(
        head_forward_kernel,
        out_shape=[jax.ShapeDtypeStruct((rows, 2 * HD), jnp.bfloat16)] * 4
        + [
            jax.ShapeDtypeStruct((total_rows, wide), jnp.bfloat16),
            jax.ShapeDtypeStruct((total_rows, 2 * HD), jnp.float32),
            jax.ShapeDtypeStruct((total_rows, 2 * HD), jnp.float32),
        ],
        in_specs=[pl.BlockSpec(memory_space=pltpu.SMEM)] + [vmem] * 4,
        out_specs=[vmem] * 7,
        scratch_shapes=[pltpu.VMEM((2, TILE, 2 * HD), jnp.float32)],
        cost_estimate=pl.CostEstimate(
            flops=12 * total_rows * total_rows * 2 * HD,
            bytes_accessed=8 * total_rows * wide,
            transcendentals=2 * total_rows * total_rows,
        ),
        name="head_forward",
    )(places, *pieces)


def head_backward_kernel(place_ref, joint_ref, mixed_ref, totals_ref, *refs):
    pieces, sends, (grad_ref, side_ref, query_ref, key_ref, value_ref, joint_grad) = (
        refs[:4],
        refs[4:8],
        refs[8:],
    )
    wide = 2 * HD
    total_rows = joint_ref.shape[0]
    for at in range(16):
        to = pl.multiple_of(place_ref[at] * BLOCK_ROWS, BLOCK_ROWS)
        grad_ref[pl.ds(to, BLOCK_ROWS), :] = pieces[at // 4][
            (at % 4) * BLOCK_ROWS : (at % 4 + 1) * BLOCK_ROWS, :
        ].astype(jnp.float32)
    first = lanes_low(TILE)
    sides = (first, jnp.logical_not(first))
    lane_ids = lax.broadcasted_iota(jnp.int32, (TILE, wide), 1)
    key_ids = lax.broadcasted_iota(jnp.int32, (TILE, TILE), 0)
    query_ids = lax.broadcasted_iota(jnp.int32, (TILE, TILE), 1)
    causal = key_ids <= query_ids

    def prepare(index, carry):
        at = pl.multiple_of(index * TILE, TILE)
        grad_mixed = grad_ref[pl.ds(at, TILE), :]
        totals = totals_ref[pl.ds(at, TILE), :]
        grad_unnorm = (grad_mixed / totals).astype(jnp.bfloat16).astype(jnp.float32)
        weighed = grad_mixed * mixed_ref[pl.ds(at, TILE), :] / totals
        for side in range(2):
            grad_totals = -jnp.sum(
                jnp.where(sides[side], weighed, 0.0), axis=1, keepdims=True
            )
            coarse = grad_totals.astype(jnp.bfloat16).astype(jnp.float32)
            fine = grad_totals - coarse
            base = (1 - side) * HD
            extra = jnp.where(
                lane_ids == base, coarse, jnp.where(lane_ids == base + 1, fine, 0.0)
            )
            side_ref[side, pl.ds(at, TILE), :] = jnp.where(
                sides[side], grad_unnorm, extra
            ).astype(jnp.bfloat16)
        return carry

    lax.fori_loop(0, total_rows // TILE, prepare, 0)
    query_ref[...] = jnp.zeros_like(query_ref)

    def tile_part(query_at, key_rows, values, masked):
        query_at = pl.multiple_of(query_at, TILE)
        scaled = joint_ref[pl.ds(query_at, TILE), :wide] * jnp.bfloat16(HD**-0.5)
        nothing = jnp.zeros_like(scaled)
        for side in range(2):
            powers = jnp.exp(inner_cols(key_rows, jnp.where(sides[side], scaled, nothing)))
            if masked:
                powers = jnp.where(causal, powers, 0.0)
            upstream = side_ref[side, pl.ds(query_at, TILE), :]
            grad_scores = (powers * inner_cols(values[side], upstream)).astype(jnp.bfloat16)
            value_ref[side] += product(powers.astype(jnp.bfloat16), upstream)
            key_ref[side] += product(grad_scores, scaled)
            query_ref[side, pl.ds(query_at, TILE), :] += inner_rows(grad_scores, key_rows)

    def key_tile(index, carry):
        key_at = pl.multiple_of(index * TILE, TILE)
        key_rows = joint_ref[pl.ds(key_at, TILE), wide : 2 * wide]
        value_rows = joint_ref[pl.ds(key_at, TILE), 2 * wide :]
        values = [jnp.where(side, value_rows, jnp.ones_like(value_rows)) for side in sides]
        key_ref[...] = jnp.zeros_like(key_ref)
        value_ref[...] = jnp.zeros_like(value_ref)
        tile_part(key_at, key_rows, values, True)

        def query_tile(query_index, inner):
            tile_part(query_index * TILE, key_rows, values, False)
            return inner

        lax.fori_loop(index + 1, total_rows // TILE, query_tile, 0)
        joint_grad[pl.ds(key_at, TILE), wide : 2 * wide] = jnp.where(
            first, key_ref[0], key_ref[1]
        ).astype(jnp.bfloat16)
        joint_grad[pl.ds(key_at, TILE), 2 * wide :] = jnp.where(
            first, value_ref[0], value_ref[1]
        ).astype(jnp.bfloat16)
        return carry

    lax.fori_loop(0, total_rows // TILE, key_tile, 0)

    def finish(index, carry):
        at = pl.multiple_of(index * TILE, TILE)
        joint_grad[pl.ds(at, TILE), :wide] = (
            jnp.where(first, query_ref[0, pl.ds(at, TILE), :], query_ref[1, pl.ds(at, TILE), :])
            * HD**-0.5
        ).astype(jnp.bfloat16)
        return carry

    lax.fori_loop(0, total_rows // TILE, finish, 0)
    for at in range(16):
        to = pl.multiple_of(place_ref[at] * BLOCK_ROWS, BLOCK_ROWS)
        sends[at // 4][(at % 4) * BLOCK_ROWS : (at % 4 + 1) * BLOCK_ROWS, :] = joint_grad[
            pl.ds(to, BLOCK_ROWS), :
        ]


def head_backward(joint_sorted, mixed_sorted, totals_sorted, pieces, places):
    rows = pieces[0].shape[0]
    total_rows, wide = joint_sorted.shape
    vmem = pl.BlockSpec(memory_space=pltpu.VMEM)
    return pl.pallas_call(
        head_backward_kernel,
        out_shape=[jax.ShapeDtypeStruct((rows, wide), jnp.bfloat16)] * 4,
        in_specs=[pl.BlockSpec(memory_space=pltpu.SMEM)] + [vmem] * 7,
        out_specs=[vmem] * 4,
        scratch_shapes=[
            pltpu.VMEM((total_rows, 2 * HD), jnp.float32),
            pltpu.VMEM((2, total_rows, 2 * HD), jnp.bfloat16),
            pltpu.VMEM((2, total_rows, 2 * HD), jnp.float32),
            pltpu.VMEM((2, TILE, 2 * HD), jnp.float32),
            pltpu.VMEM((2, TILE, 2 * HD), jnp.float32),
            pltpu.VMEM((total_rows, wide), jnp.bfloat16),
        ],
        cost_estimate=pl.CostEstimate(
            flops=30 * total_rows * total_rows * 2 * HD,
            bytes_accessed=8 * total_rows * wide,
            transcendentals=2 * total_rows * total_rows,
        ),
        name="head_backward",
    )(places, joint_sorted, mixed_sorted, totals_sorted, *pieces)


def norm_parts(values):
    average = jnp.mean(values, axis=-1, keepdims=True)
    centred = values - average
    spread_of = jnp.mean(centred * centred, axis=-1, keepdims=True)
    inverse = lax.rsqrt(spread_of + EPS)
    return centred * inverse, inverse


def norm_pull(grad, scaled, inverse, gain):
    lifted = grad * gain
    return (
        lifted
        - jnp.mean(lifted, axis=-1, keepdims=True)
        - scaled * jnp.mean(lifted * scaled, axis=-1, keepdims=True)
    ) * inverse


def chip_body(
    inputs,
    block_order,
    first_gain,
    first_shift,
    joint_weight,
    query_bias,
    value_bias,
    mixer_weight,
    mixer_bias,
    second_gain,
    second_shift,
    expand_weight,
    expand_bias,
    reduce_weight,
    reduce_bias,
    cotangent,
):
    low, full = jnp.bfloat16, jnp.float32
    group = lax.axis_index("dp")
    core = lax.axis_index("core")
    depth = lax.axis_index("z")
    even = core == 0
    own_rows = inputs.shape[1]
    share = joint_weight.shape[0]

    def chip_order(mine, theirs):
        return jnp.where(
            even,
            jnp.concatenate([mine, theirs], axis=0),
            jnp.concatenate([theirs, mine], axis=0),
        )

    def cores_exchanged(parts):
        mine = jnp.where(even, parts[0], parts[1])
        theirs = jnp.where(even, parts[1], parts[0])
        return chip_order(mine, swapped(theirs, CORE_BIT))

    def by_depth(value):
        value = jnp.where(depth % 2 == 0, value, value.reshape((2, 2) + value.shape[1:])[:, ::-1].reshape(value.shape))
        return jnp.where(depth < 2, value, jnp.concatenate([value[2:], value[:2]], axis=0))

    chip_ids = jnp.arange(16, dtype=jnp.int32)
    across, along = chip_ids // 4, chip_ids % 4
    slots = (across ^ group) * 4 + (along ^ depth)
    col_slots = jnp.arange(4, dtype=jnp.int32) ^ depth
    mixer_slots = ((slots // 8) ^ core) * 8 + (((slots // 2) % 4) ^ depth) * 2 + slots % 2
    table = jnp.concatenate([slots, col_slots, mixer_slots])
    places = block_order[
        ((chip_ids // 4) ^ depth) * 4 + (((chip_ids // 2) % 2) ^ core) * 2 + chip_ids % 2
    ]

    tokens = inputs[0]
    pair = jnp.concatenate([tokens, cotangent[0]], axis=0)
    pair_got = swapped(pair, CORE_BIT)

    units = expand_weight.shape[1] // 2
    small, left = jnp.zeros((384,), low), 0
    for item in (
        first_gain,
        first_shift,
        query_bias,
        value_bias,
        mixer_bias,
        second_gain,
        second_shift,
        reduce_bias,
        expand_bias,
    ):
        small = small + jnp.pad(item, (left, 384 - left - item.shape[0]))
        left += item.shape[0]
    small = small.reshape(1, 384)
    joint_parts = joint_weight.reshape(share, 3, 2, 4, 128).transpose(2, 0, 3, 1, 4).reshape(2, share, 1536)
    small_rows = jnp.pad(small, ((0, 7), (0, 1536 - 384)))
    joint_mine = jnp.where(even, joint_parts[0], joint_parts[1])
    joint_theirs = jnp.where(even, joint_parts[1], joint_parts[0])
    joint_got = swapped(jnp.concatenate([joint_theirs, small_rows]), CORE_BIT)
    small_got = joint_got[share:, :384]
    small_pair = jnp.concatenate(
        [
            jnp.where(even, small_rows[:, :384], small_got),
            jnp.where(even, small_got, small_rows[:, :384]),
            jnp.zeros((8, 768), low),
        ],
        axis=1,
    )
    joint_own = jnp.concatenate([chip_order(joint_mine, joint_got[:share]), small_pair])
    joint_line = line_of(joint_own)
    joint_arrays, joint_at = collected(joint_line)

    expand_parts = expand_weight.reshape(share, 16, 2, 128)
    expand_own = cores_exchanged(
        (expand_parts[:, :, 0].reshape(share, units), expand_parts[:, :, 1].reshape(share, units))
    )
    mixer_own = cores_exchanged((mixer_weight[:, : D // 2], mixer_weight[:, D // 2 :]))
    hidden_own = jnp.concatenate([expand_own[:, :D], expand_own[:, D:], reduce_weight])
    mixer_line = line_of(after(mixer_own, *joint_line[1:]))
    hidden_line = line_of(after(hidden_own, *mixer_line[1:]))
    mixer_arrays, mixer_at = collected_small(after(mixer_line, *joint_arrays[1:3]))
    token_rows = jnp.concatenate([tokens, pair_got[:own_rows]], axis=0).astype(full)
    upstream = jnp.concatenate([cotangent[0], pair_got[own_rows:]], axis=0)
    scaled_one, inverse_one = norm_parts(token_rows)
    joint_arrays = after(joint_arrays, scaled_one)
    joint_plan = []
    for at, (array, entry) in enumerate(joint_at):
        for col in range(4):
            source_at = looked(entry, 64, 16 + col, 384)
            joint_plan.append((array, source_at, 0, slot_part(at, 0, 64, col * 384, 384)))
        joint_plan.append((array, fixed(entry, pl.ds(64, 8), pl.ds(0, 768)), 1, slot(at)))
    joint_done = moved(
        table,
        joint_arrays,
        joint_plan,
        [(16, 64, 1536), (16, 8, 768)],
    )
    joint_full = joint_done[0].reshape(D, 1536)
    small_all = joint_done[1][:, 0].reshape(32, 384)
    count = share
    rows_of = small_all[:, : 8 * count].reshape(32, 8, count).transpose(1, 0, 2).reshape(8, 32 * count)
    (
        gain_one,
        shift_one,
        query_shift,
        value_shift,
        mixer_shift,
        gain_two,
        shift_two,
        reduce_shift,
    ) = [rows_of[at] for at in range(8)]
    expand_shift = small_all[:, 8 * count :].reshape(16, 2, 128)
    expand_shift = jnp.where(even, expand_shift[:, 0], expand_shift[:, 1]).reshape(-1)

    normed = (scaled_one * gain_one + shift_one).astype(low)
    halves_of = [
        jnp.where(even, item[: D // 2], item[D // 2 :]).reshape(4, 1, 128)
        for item in (query_shift, value_shift)
    ]
    joint_shift = by_depth(jnp.concatenate([halves_of[0], jnp.zeros_like(halves_of[0]), halves_of[1]], axis=1))
    normed = after(normed, mixer_arrays[1], mixer_arrays[2])
    joint_rows = (product(normed, joint_full) + joint_shift.reshape(1536)).astype(low)
    hidden_line = after(hidden_line, joint_rows, mixer_arrays)
    hidden_arrays, hidden_at = collected(hidden_line)
    head_pieces = [joint_rows[:, at * 384 : (at + 1) * 384] for at in range(4)]
    head_pieces = [head_pieces[0]] + [swapped(head_pieces[at], Z_BITS[at]) for at in (1, 2, 3)]
    hidden_plan = []
    for at, (array, entry) in enumerate(hidden_at):
        hidden_plan.append((array, fixed(entry, pl.ds(0, 64)), 0, slot_part(at, 0, 64, 0, D)))
        hidden_plan.append((array, fixed(entry, pl.ds(64, 64)), 0, slot_part(at, 0, 64, D, D)))
        hidden_plan.append((array, fixed(entry, pl.ds(128, 128)), 1, slot(at)))
    expand_full, reduce_full = moved(table, hidden_arrays, hidden_plan, [(16, 64, units), (16, 128, D)])
    expand_full, reduce_full = expand_full.reshape(D, units), reduce_full.reshape(units, D)
    mixer_cols = moved(
        table,
        mixer_arrays,
        [(array, fixed(entry), 0, slot(20 + at)) for at, (array, entry) in enumerate(mixer_at)],
        [(16, 64, D // 2)],
    )[0].reshape(2, D // 2, D // 2)
    mixer_mine, mixer_theirs = mixer_cols[0], swapped(mixer_cols[1], CORE_BIT)
    mixer_full = jnp.where(
        even,
        jnp.concatenate([mixer_mine, mixer_theirs], axis=1),
        jnp.concatenate([mixer_theirs, mixer_mine], axis=1),
    )
    forward = head_forward(head_pieces, places)
    mixed_out, (joint_sorted, mixed_sorted, totals_sorted) = forward[:4], forward[4:]
    mixed_out = after(mixed_out, hidden_arrays[1], hidden_arrays[2])
    mixed_rows = jnp.concatenate(
        [mixed_out[0]] + [swapped(mixed_out[at], Z_BITS[at]) for at in (1, 2, 3)], axis=1
    )

    def both_cores(part):
        turned = jnp.concatenate([part[own_rows:], part[:own_rows]], axis=0).astype(low)
        return part + swapped(turned, CORE_BIT).astype(full)

    def own_sum(part):
        return part[:own_rows] + swapped(part[own_rows:].astype(low), CORE_BIT).astype(full)

    middle = token_rows + (both_cores(product(mixed_rows, mixer_full)) + mixer_shift)
    scaled_two, inverse_two = norm_parts(middle)
    second = (scaled_two * gain_two + shift_two).astype(low)
    before = product(second, expand_full) + expand_shift
    active, gelu_pull = jax.vjp(gelu_tanh, before)
    active = active.astype(low)

    reduce_gradient = inner_rows(active, upstream).astype(low).reshape(16, 128, D)
    grad_before = gelu_pull(inner_cols(upstream, reduce_full))[0].astype(low)
    expand_gradient = inner_rows(second, grad_before).astype(low).reshape(16, 64, units)
    expand_shift_gradient = jnp.sum(grad_before.astype(full), axis=0)
    grad_second = both_cores(inner_cols(grad_before, expand_full))
    upstream_full = upstream.astype(full)
    grad_middle = upstream_full + norm_pull(grad_second, scaled_two, inverse_two, gain_two)
    grad_branch = grad_middle.astype(low)
    grad_mixed = inner_cols(grad_branch, mixer_full).astype(low)
    mixer_gradient = inner_rows(mixed_rows, after(grad_branch, grad_mixed)).astype(low)
    grad_pieces = [grad_mixed[:, at * 128 : (at + 1) * 128] for at in range(4)]
    grad_pieces = [grad_pieces[0]] + [swapped(grad_pieces[at], Z_BITS[at]) for at in (1, 2, 3)]
    mixer_keep = jnp.where(even, mixer_gradient[:, : D // 2], mixer_gradient[:, D // 2 :])
    mixer_send = jnp.where(even, mixer_gradient[:, D // 2 :], mixer_gradient[:, : D // 2])
    mixer_got = swapped(mixer_send, CORE_BIT)
    mixer_whole = jnp.concatenate([mixer_keep, mixer_got], axis=0).reshape(16, 64, D // 2)
    hidden_plan = []
    for at in range(16):
        to, place = GROUP_OF[at]
        hidden_plan.append((0, slot_part(at, 0, 64, 0, D), to, fixed(place, pl.ds(0, 64))))
        hidden_plan.append((0, slot_part(at, 0, 64, D, D), to, fixed(place, pl.ds(64, 64))))
        hidden_plan.append((1, slot(at), to, fixed(place, pl.ds(128, 128))))
        for half in range(2):
            left = fixed(place, pl.ds(256, 32), pl.ds(half * (D // 2), D // 2))
            hidden_plan.append((2, slot_rows(20 + at, half * 32, 32), to, left))
    expand_gradient = after(expand_gradient, grad_pieces[2])
    grouped = moved(
        table, (expand_gradient, reduce_gradient, mixer_whole), hidden_plan, [(4, 288, D)] * 4
    )
    hidden_state = summed_first(grouped)
    grad_pieces = after(grad_pieces, grouped)
    grad_out = head_backward(joint_sorted, mixed_sorted, totals_sorted, grad_pieces, places)
    grad_got = [swapped(grad_out[at], Z_BITS[at]) for at in (1, 2, 3)]
    hidden_state = summed_second(after(hidden_state, grad_got[0]))
    grad_got = after(grad_got, hidden_state)
    result = middle[:own_rows] + (own_sum(product(after(active, grad_out), reduce_full)) + reduce_shift)
    grad_joint = jnp.concatenate([grad_out[0]] + grad_got, axis=1)
    joint_gradient = inner_rows(normed, grad_joint).astype(low).reshape(16, 64, 1536)
    grad_normed_part = inner_cols(grad_joint, joint_full)
    joint_sums = by_depth(jnp.sum(grad_joint.astype(full), axis=0).reshape(4, 3, 128))

    def one_core(values):
        values = values.reshape(1, -1)
        nothing = jnp.zeros_like(values)
        return jnp.where(
            even, jnp.concatenate([values, nothing], axis=1), jnp.concatenate([nothing, values], axis=1)
        )[0]

    expand_rows = expand_shift_gradient.reshape(16, 1, 128)
    expand_rows = jnp.where(
        even,
        jnp.concatenate([expand_rows, jnp.zeros_like(expand_rows)], axis=1),
        jnp.concatenate([jnp.zeros_like(expand_rows), expand_rows], axis=1),
    ).reshape(32, 128)
    sums = jnp.stack(
        [
            jnp.sum(grad_normed_part * scaled_one, axis=0),
            jnp.sum(grad_normed_part, axis=0),
            one_core(joint_sums[:, 0]),
            one_core(joint_sums[:, 2]),
            jnp.sum(grad_branch[:own_rows].astype(full), axis=0),
            jnp.sum(grad_second[:own_rows] * scaled_two[:own_rows], axis=0),
            jnp.sum(grad_second[:own_rows], axis=0),
            jnp.sum(upstream_full[:own_rows], axis=0),
        ]
    )
    sums = sums.astype(low).reshape(8, 32, count).transpose(1, 0, 2).reshape(32, 8 * count)
    sums = jnp.concatenate([sums, expand_rows.astype(low)], axis=1).reshape(16, 1, 768)
    sums = jnp.pad(sums, ((0, 0), (0, 7), (0, 0)))
    joint_gradient = after(joint_gradient, hidden_state)
    joint_plan = []
    for at in range(16):
        to, place = GROUP_OF[at]
        for col in range(4):
            left = looked(place, 64, 16 + col, 384)
            joint_plan.append((0, slot_part(at, 0, 64, col * 384, 384), to, left))
        joint_plan.append((1, slot(at), to, fixed(place, pl.ds(64, 8), pl.ds(0, 768))))
    joint_state = summed_second(
        summed_first(moved(table, (joint_gradient, sums), joint_plan, [(4, 72, 1536)] * 4))
    )
    hidden_sum = summed_third(hidden_state, joint_state)
    joint_sum = summed_third(joint_state)
    grad_normed = own_sum(grad_normed_part)
    input_gradient = (
        grad_middle[:own_rows]
        + norm_pull(grad_normed, scaled_one[:own_rows], inverse_one[:own_rows], gain_one)
    ).astype(low)

    def paired(first_core, second_core):
        mine = jnp.where(even, first_core, second_core)
        got = swapped(jnp.where(even, second_core, first_core), CORE_BIT)
        return mine, got

    mixer_mine, mixer_got = paired(hidden_sum[256:, : D // 2], hidden_sum[256:, D // 2 :])
    mixer_out = jnp.where(
        even,
        jnp.concatenate([mixer_mine, mixer_got], axis=1),
        jnp.concatenate([mixer_got, mixer_mine], axis=1),
    )
    expand_pairs = hidden_sum[:128].reshape(2, 2, share, 8, 128)
    expand_mine, expand_got = paired(expand_pairs[:, 0], expand_pairs[:, 1])
    expand_out = jnp.where(
        even, jnp.stack([expand_mine, expand_got], axis=3), jnp.stack([expand_got, expand_mine], axis=3)
    )
    expand_out = expand_out.transpose(1, 0, 2, 3, 4).reshape(share, 2 * units)
    joint_mine = jnp.where(even, joint_sum[:share], joint_sum[share : 2 * share])
    joint_got = swapped(
        jnp.concatenate(
            [jnp.where(even, joint_sum[share : 2 * share], joint_sum[:share]), joint_sum[2 * share :]]
        ),
        CORE_BIT,
    )
    joint_mine_parts = joint_mine.reshape(share, 4, 3, 128)
    joint_got_parts = joint_got[:share].reshape(share, 4, 3, 128)
    joint_out = jnp.where(
        even,
        jnp.stack([joint_mine_parts, joint_got_parts], axis=1),
        jnp.stack([joint_got_parts, joint_mine_parts], axis=1),
    )
    joint_out = joint_out.transpose(0, 3, 1, 2, 4).reshape(share, 3 * D)
    own_sums = joint_sum[2 * share, :768] + joint_got[share, :768]
    own_sums = jnp.where(even, own_sums[:384], own_sums[384:])
    vectors = [own_sums[at * count : (at + 1) * count] for at in range(8)] + [own_sums[8 * count :]]
    return (
        result.astype(low)[None],
        input_gradient[None],
        vectors[0],
        vectors[1],
        joint_out,
        vectors[2],
        vectors[3],
        mixer_out,
        vectors[4],
        vectors[5],
        vectors[6],
        expand_out,
        vectors[8],
        hidden_sum[128:256],
        vectors[7],
    )


def solution(mesh):
    dp_size, sp_size = mesh.shape["dp"], mesh.shape["sp"]
    if dp_size == 4 and sp_size == 8:
        mesh = Mesh(mesh.devices.reshape(dp_size, sp_size // 2, 2), ALL)
        body, line = chip_body, ("z", "core")
    else:
        body, line = ring_body, ("sp",)
    rows = P("dp", line, None)
    vector = P(("dp",) + line)
    matrix = P(("dp",) + line, None)
    in_specs = (
        rows,
        P(),
        vector,
        vector,
        matrix,
        vector,
        vector,
        matrix,
        vector,
        vector,
        vector,
        matrix,
        vector,
        matrix,
        vector,
        rows,
    )
    out_specs = (
        rows,
        rows,
        vector,
        vector,
        matrix,
        vector,
        vector,
        matrix,
        vector,
        vector,
        vector,
        matrix,
        vector,
        matrix,
        vector,
    )
    return jax.shard_map(body, mesh=mesh, in_specs=in_specs, out_specs=out_specs, check_vma=False)
```
